32 devices in a mesh: dp: 4 (over y, core), seq: 8 (over z, x).
Axes of the slice: x: 2, y: 2, z: 4, core: 2. Of those that a mesh axis runs over, the one named last changes fastest.
Arguments:
- patches: bfloat16 [8192, 768], P(('dp', 'seq')), may hold values from -6 to 6
- cotangent: bfloat16 [8192, 768], P(('dp', 'seq')), may hold values from -6 to 6
- input_views: int32 [4], P('dp'), may hold values from 1 to 1, as said below
- token_live: int32 [8192], P(('dp', 'seq')), may hold values from 0 to 1, as said below
- master: float32 [768, 12, 768], P('dp', None, 'seq')
- moment_one: float32 [768, 12, 768], P('dp', None, 'seq')
- moment_two: float32 [768, 12, 768], P('dp', None, 'seq'), as said below
- norm_params: float32 [4, 768], replicated, as said below
- norm_moment_one: float32 [4, 768], replicated
- norm_moment_two: float32 [4, 768], replicated, as said below
Outputs:
- block_out: bfloat16 [8192, 768], P(('dp', 'seq'))
- patches_grad: float32 [8192, 768], P(('dp', 'seq'))
- new_master: float32 [768, 12, 768], P('dp', None, 'seq')
- new_copy: bfloat16 [768, 12, 768], P('dp', None, 'seq')
- new_moment_one: float32 [768, 12, 768], P('dp', None, 'seq')
- new_moment_two: float32 [768, 12, 768], P('dp', None, 'seq')
- new_norm_params: float32 [4, 768], replicated
- new_norm_moment_one: float32 [4, 768], replicated
- new_norm_moment_two: float32 [4, 768], replicated
- grad_norm: float32 [], replicated
The draws below stay inside these ranges and needn't reach their ends.
Inputs may be any that keep to these rules, and one draw needn't show every extreme that they name: Scene g's first input_views[g] views are input views, the rest target views. `token_live`: the first patch of every view is present. `moment_two`: positive. `norm_params`: rows 0 and 2 are positive. `norm_moment_two`: positive.
All inputs are finite; a program needn't handle non-finite values.
Results may differ from the reference program's by a relative error of at most 0.017.
Values may be sent and summed in bfloat16 or wider, within the bound.
No kernel may reach another device: no remote copies, remote signals or barrier semaphores. Data moves between devices by JAX's collectives and lax.ppermute only.
A program may use at most 192 MiB of HBM per device.

```python
import math
import jax
import jax.numpy as jnp
from jax import lax

D = 768
HEADS = 12
HEAD_DIM = 64
FF = 3072
VIEW = 1024
STEP = 10
TOK_DEV = 256
NVIEW = 2
TOKENS = 8192
BLOCKS = 12
N_DP = 4
N_SEQ = 8


def grad_scale():
    return 1.0 / jnp.sqrt(1.0 * (D * D * BLOCKS + 4 * D))


def draw_input_views(key, part):
    picked = jax.random.randint(jax.random.fold_in(key, 11), (N_DP,), 1, NVIEW)
    ranking = jax.random.permutation(jax.random.fold_in(key, 12), N_DP)
    picked = jnp.where(ranking == 0, 1, picked)
    picked = jnp.where(ranking == 1, NVIEW - 1, picked)
    return picked.astype(jnp.int32)


def draw_token_live(key, part):
    rolled = jax.random.randint(jax.random.fold_in(key, 21), (TOKENS,), 0, 8)
    living = (rolled > 0).astype(jnp.int32)
    firsts = jnp.arange(TOKENS, dtype=jnp.int32) % VIEW == 0
    return jnp.where(firsts, 1, living).astype(jnp.int32)


def draw_master(key, part):
    extent = (D, BLOCKS, D)
    normal_base = jax.random.normal(jax.random.fold_in(key, 31), extent, jnp.float32)
    block_index = jnp.arange(BLOCKS)
    scales = jnp.where(block_index < 2, 1.4, 1.0)
    scales = jnp.where(block_index == 3, 3.0, scales)
    scales = scales / jnp.sqrt(D * 1.0)
    scales = jnp.where(block_index >= 4 + FF // D, 1.0 / jnp.sqrt(FF * 1.0), scales)
    return (normal_base * scales[None, :, None]).astype(jnp.float32)


def draw_moment_one(key, part):
    noise = jax.random.normal(jax.random.fold_in(key, 41), (D, BLOCKS, D), jnp.float32)
    return (0.111 * grad_scale() * noise).astype(jnp.float32)


def draw_moment_two(key, part):
    factor = jax.random.uniform(jax.random.fold_in(key, 42), (D, BLOCKS, D), jnp.float32, 1.0, 4.0)
    return (0.0526 * grad_scale() * grad_scale() * factor).astype(jnp.float32)


def draw_norm_params(key, part):
    position = jnp.arange(D, dtype=jnp.float32) / (D - 1.0)
    rising = 0.5 + position
    jitter = jax.random.uniform(jax.random.fold_in(key, 51), (2, D), jnp.float32, 0.8, 1.25)
    shifts = 0.2 * jax.random.normal(jax.random.fold_in(key, 52), (2, D), jnp.float32)
    gains = rising[None, :] * jitter
    return jnp.stack([gains[0], shifts[0], gains[1], shifts[1]]).astype(jnp.float32)


def draw_norm_moment_one(key, part):
    noise = jax.random.normal(jax.random.fold_in(key, 61), (4, D), jnp.float32)
    return (0.222 * grad_scale() * noise).astype(jnp.float32)


def draw_norm_moment_two(key, part):
    factor = jax.random.uniform(jax.random.fold_in(key, 62), (4, D), jnp.float32, 1.0, 4.0)
    return (0.2104 * grad_scale() * grad_scale() * factor).astype(jnp.float32)


def block_levels(rng, dims, split, smallest, top_value):
    level, own = 1.0, jax.random.fold_in(rng, 6)
    for dim, parts in split:
        draws = jnp.exp(jax.random.uniform(jax.random.fold_in(own, dim), (parts,), jnp.float32, smallest / len(split), top_value / len(split)))
        level = level * jnp.repeat(draws, dims[dim] // parts).reshape([-1 if axis == dim else 1 for axis in range(len(dims))])
    return level


def gaussian(key, shape, width, limit, shards=(), kind=jnp.bfloat16):
    values = jax.random.normal(key, shape, jnp.float32) * width
    if len(shards) > 0:
        values = block_levels(key, shape, shards, -0.22, 0.18) * values
    return jnp.clip(values, min=-limit, max=limit).astype(kind)


def setup_inputs(seed: int = 0) -> dict:
    streams_of = jax.random.split(jax.random.key(seed), 11)
    return {
        "patches": gaussian(streams_of[0], (TOKENS, D), 1.0, 6.0, ((0, 32),)),
        "cotangent": gaussian(streams_of[1], (TOKENS, D), 1.0, 6.0, ((0, 32),)),
        "input_views": draw_input_views(jax.random.fold_in(streams_of[10], 71), 0),
        "token_live": draw_token_live(jax.random.fold_in(streams_of[10], 71), 0),
        "master": draw_master(jax.random.fold_in(streams_of[10], 71), 0),
        "moment_one": draw_moment_one(jax.random.fold_in(streams_of[10], 71), 0),
        "moment_two": draw_moment_two(jax.random.fold_in(streams_of[10], 71), 0),
        "norm_params": draw_norm_params(jax.random.fold_in(streams_of[10], 71), 0),
        "norm_moment_one": draw_norm_moment_one(jax.random.fold_in(streams_of[10], 71), 0),
        "norm_moment_two": draw_norm_moment_two(jax.random.fold_in(streams_of[10], 71), 0),
    }


@jax.custom_vjp
def low(v):
    return lax.optimization_barrier(v.astype(jnp.bfloat16)).astype(jnp.float32)

@jax.custom_vjp
def low_back(v):
    return v

def low_keep(v):
    return (low(v), None)

def low_pass(kept, grad):
    return (grad,)

def back_keep(v):
    return (v, None)

def back_low(kept, grad):
    return (low(grad),)
low.defvjp(low_keep, low_pass)
low_back.defvjp(back_keep, back_low)
highest = lax.Precision.HIGHEST
layer_eps = 1e-05
beta_first = 0.9
beta_second = 0.95
adam_eps = 1e-08
rate_matrix = 0.08
rate_vector = 0.8
weight_decay = 0.1
masked_score = -1e+30

def layer_norm(values, gain, shift):
    centre = lax.optimization_barrier(jnp.mean(values, axis=-1, keepdims=True))
    spread = lax.optimization_barrier(jnp.mean((values - centre) * (values - centre), axis=-1, keepdims=True))
    return (values - centre) * lax.rsqrt(spread + layer_eps) * gain + shift

def attend(query_rows, key_rows, value_rows, query_view, key_view, key_live, inputs_seen):
    scaling = 1.0 / math.sqrt(HEAD_DIM)
    scores = jnp.einsum('qhd,khd->hqk', query_rows, key_rows, precision=highest) * scaling
    scores = low_back(scores)
    visible = (key_live[None, :] > 0) & ((key_view[None, :] < inputs_seen) | (key_view[None, :] == query_view[:, None]))
    scores = jnp.where(visible[None], scores, masked_score)
    weights = jax.nn.softmax(scores, axis=-1)
    return jnp.einsum('hqk,khd->qhd', low(weights), value_rows, precision=highest)

def group_forward(patch_rows, weights, params, live_rows, inputs_seen):
    length = patch_rows.shape[0]
    wide_blocks = FF // D
    normed = low(layer_norm(patch_rows, params[0], params[1]))
    projected = jnp.einsum('td,dbc->tbc', normed, weights[:, 0:3, :], precision=highest)
    projected = low(low_back(projected))
    query_all = projected[:, 0, :].reshape(length, HEADS, HEAD_DIM)
    key_all = projected[:, 1, :].reshape(length, HEADS, HEAD_DIM)
    value_all = projected[:, 2, :].reshape(length, HEADS, HEAD_DIM)
    view_of = jnp.arange(length, dtype=jnp.int32) // VIEW
    block_size = math.gcd(length, 512)
    block_count = length // block_size

    def one_block(index):
        first = (index * block_size).astype(jnp.int32)
        rows_here = lax.dynamic_slice_in_dim(query_all, first, block_size, 0)
        views_here = lax.dynamic_slice_in_dim(view_of, first, block_size, 0)
        return attend(rows_here, key_all, value_all, views_here, view_of, live_rows, inputs_seen)
    mixed = lax.map(jax.checkpoint(one_block), jnp.arange(block_count, dtype=jnp.int32))
    mixed = low(low_back(mixed.reshape(length, D)))
    attended = low_back(jnp.dot(mixed, weights[:, 3, :], precision=highest))
    resid = patch_rows + attended
    normed_two = low(layer_norm(resid, params[2], params[3]))
    widened = low_back(jnp.einsum('td,dbc->tbc', normed_two, weights[:, 4:4 + wide_blocks, :], precision=highest))
    hidden = low(jax.nn.gelu(widened, approximate=False))
    narrowed = low_back(jnp.einsum('tbc,ibc->ti', hidden, weights[:, 4 + wide_blocks:, :], precision=highest))
    return resid + narrowed

def adam_step(params, grads, first, second, rate, decay):
    first_new = beta_first * first + (1.0 - beta_first) * grads
    second_new = beta_second * second + (1.0 - beta_second) * grads * grads
    first_hat = first_new / (1.0 - beta_first ** STEP)
    second_hat = second_new / (1.0 - beta_second ** STEP)
    params_new = params - rate * (first_hat / (jnp.sqrt(second_hat) + adam_eps) + decay * params)
    return (params_new, first_new, second_new)

def reference(patches, cotangent, input_views, token_live, master, moment_one, moment_two, norm_params, norm_moment_one, norm_moment_two):
    length = TOK_DEV * N_SEQ
    copy_weights = low(master)
    patch_groups = patches.astype(jnp.float32).reshape(N_DP, length, D)
    cot_groups = cotangent.astype(jnp.float32).reshape(N_DP, length, D)
    live_groups = token_live.reshape(N_DP, length)

    def per_group(running, item):
        patch_rows, cot_rows, live_rows, inputs_seen = item

        def forward(rows, weights, params):
            return group_forward(rows, weights, params, live_rows, inputs_seen)
        result, pullback = jax.vjp(forward, patch_rows, copy_weights, norm_params)
        row_grad, weight_grad, param_grad = pullback(cot_rows)
        return ((running[0] + weight_grad, running[1] + param_grad), (result, row_grad))
    zeros = (jnp.zeros_like(copy_weights), jnp.zeros_like(norm_params))
    sums, stacked = lax.scan(per_group, zeros, (patch_groups, cot_groups, live_groups, input_views))
    weight_sum, param_sum = sums
    outputs, row_grads = stacked
    grad_norm = jnp.sqrt(jnp.sum(weight_sum * weight_sum) + jnp.sum(param_sum * param_sum))
    clip = 1.0 / jnp.maximum(grad_norm, 1.0)
    new_master, new_moment_one, new_moment_two = adam_step(master, weight_sum * clip, moment_one, moment_two, rate_matrix, weight_decay)
    new_norm_params, new_norm_moment_one, new_norm_moment_two = adam_step(norm_params, param_sum * clip, norm_moment_one, norm_moment_two, rate_vector, 0.0)
    block_out = outputs.reshape(N_DP * length, D).astype(jnp.bfloat16)
    patches_grad = row_grads.reshape(N_DP * length, D)
    return (block_out, patches_grad, new_master, new_master.astype(jnp.bfloat16), new_moment_one, new_moment_two, new_norm_params, new_norm_moment_one, new_norm_moment_two, grad_norm)
```

```python
import math
from functools import partial

import jax
import jax.numpy as jnp
from jax import lax
from jax.sharding import PartitionSpec as P

D = 768
HEADS = 12
HEAD_DIM = 64
FF = 3072
VIEW = 1024
STEP = 10
GROUPS = 4
GROUP_HEADS = HEADS // GROUPS
GROUP_WIDTH = GROUP_HEADS * HEAD_DIM
WIDE = FF // D
RING = (0, 1, 3, 2)

layer_eps = 1e-05
beta_first = 0.9
beta_second = 0.95
adam_eps = 1e-08
rate_matrix = 0.08
rate_vector = 0.8
weight_decay = 0.1
masked_score = -1e30
bf16 = jnp.bfloat16
f32 = jnp.float32


def gray(v):
    return v ^ (v >> 1)


def hop_quarter(value, by):
    split = lax.axis_size("seq") // GROUPS
    pairs = [
        (RING[p] * split + x, RING[(p + by) % GROUPS] * split + x) for p in range(GROUPS) for x in range(split)
    ]
    return lax.ppermute(value, "seq", pairs)


def hop_within(value, by):
    split = lax.axis_size("seq") // GROUPS
    pairs = [(q * split + x, q * split + (x + by) % split) for q in range(GROUPS) for x in range(split)]
    return lax.ppermute(value, "seq", pairs)


def swap(value, axis, bit):
    return lax.ppermute(value, axis, [(i, i ^ bit) for i in range(lax.axis_size(axis))])


def bits_of(axis):
    return [1 << b for b in range(lax.axis_size(axis).bit_length() - 1)]


def total(value):
    for axis in ("dp", "seq"):
        for bit in bits_of(axis):
            value = value + swap(value, axis, bit)
    return value


def pick(stack, index):
    return lax.dynamic_index_in_dim(stack, index, 0, keepdims=False)


def layer_stats(values):
    centre = jnp.mean(values, axis=-1, keepdims=True)
    shifted = values - centre
    spread = jnp.mean(shifted * shifted, axis=-1, keepdims=True)
    inverse = lax.rsqrt(spread + layer_eps)
    return (shifted * inverse, inverse)


def layer_back(grad_normed, normalized, inverse, gain):
    scaled = grad_normed * gain
    centred = jnp.mean(scaled, axis=-1, keepdims=True)
    along = jnp.mean(scaled * normalized, axis=-1, keepdims=True)
    return inverse * (scaled - centred - normalized * along)


def mm(a, b):
    return jnp.dot(a, b, preferred_element_type=f32)


def mm_nt(a, b):
    return lax.dot_general(a, b, (((1,), (1,)), ((), ())), preferred_element_type=f32)


def mm_tn(a, b):
    return lax.dot_general(a, b, (((0,), (0,)), ((), ())), preferred_element_type=f32)


def gather_rows(piece):
    for bit in reversed(bits_of("dp")):
        piece = jnp.concatenate([piece, swap(piece, "dp", bit)], axis=1)
    return piece


def row_order():
    order = [0]
    for bit in reversed(bits_of("dp")):
        order = order + [o ^ bit for o in order]
    return order


def reduce_rows(piece):
    for bit in bits_of("dp"):
        half = piece.shape[1] // 2
        there = swap(piece[:, half:], "dp", bit)
        piece = (piece[:, :half].astype(f32) + there.astype(f32)).astype(bf16)
    return piece


def reduce_within(piece):
    own = piece[0].astype(f32)
    for j in range(1, piece.shape[0]):
        own = own + hop_within(piece[j], -j).astype(f32)
    return own.astype(bf16)


def reduce_ring(slots):
    moving = slots[1]
    for k in (2, 3):
        moving = (hop_quarter(moving, 1).astype(f32) + slots[k].astype(f32)).astype(bf16)
    return hop_quarter(moving, 1).astype(f32) + slots[0].astype(f32)


def adam_step(params, grads, first, second, rate, decay):
    first_new = beta_first * first + (1.0 - beta_first) * grads
    second_new = beta_second * second + (1.0 - beta_second) * grads * grads
    first_hat = first_new / (1.0 - beta_first**STEP)
    second_hat = second_new / (1.0 - beta_second**STEP)
    params_new = params - rate * (first_hat / (jnp.sqrt(second_hat) + adam_eps) + decay * params)
    return (params_new, first_new, second_new)


def local(
    patches,
    cotangent,
    input_views,
    token_live,
    master,
    moment_one,
    moment_two,
    norm_params,
    norm_moment_one,
    norm_moment_two,
):
    tokens = patches.shape[0]
    rows, blocks, cols = master.shape
    n_dp = lax.axis_size("dp")
    split = lax.axis_size("seq") // GROUPS
    dp = lax.axis_index("dp")
    seq = lax.axis_index("seq")
    quarter, within = seq // split, seq % split
    place = gray(quarter)
    inputs_seen = input_views[0]
    gain_one, shift_one, gain_two, shift_two = (norm_params[i] for i in range(4))
    order = row_order()
    dp_place = [order.index(a) for a in range(n_dp)]

    def quarter_behind(k):
        return gray((place - k) & 3)

    flags = jnp.pad(token_live.astype(bf16)[None, :], ((0, 7), (0, D - tokens)))
    ring = [jnp.concatenate([patches, flags], axis=0)]
    for _ in range(3):
        ring.append(hop_quarter(ring[-1], 1))
    pieces = [[ring[k]] + [hop_within(ring[k], j) for j in range(1, split)] for k in range(4)]
    scene = jnp.stack([jnp.stack([p[:tokens] for p in pieces[k]]) for k in range(4)])
    live = jnp.stack([jnp.concatenate([p[tokens, :tokens] for p in pieces[k]]) for k in range(4)])

    copy_low = master.astype(bf16)
    mine = copy_low[:, 0:3, :].reshape(rows, 3 * cols)
    near = jnp.stack([mine] + [hop_within(mine, j) for j in range(1, split)])
    near = gather_rows(near).reshape(split, n_dp, rows, 3, cols)
    near = jnp.stack([pick(near, (within - a) % split) for a in range(split)])
    near = jnp.moveaxis(near, 1, 0)
    near = jnp.stack([pick(near, order_at) for order_at in [relative(dp, a, order) for a in range(n_dp)]])
    w_qkv = jnp.transpose(near, (0, 2, 3, 1, 4)).reshape(D, 3, GROUP_WIDTH)

    up = copy_low[:, 4 : 4 + WIDE].reshape(rows, WIDE * cols)
    down = copy_low[:, 4 + WIDE :].reshape(rows, WIDE * cols)
    far = [jnp.concatenate([up, down, copy_low[:, 3]], axis=1)]
    for _ in range(3):
        far.append(hop_quarter(far[-1], 1))
    weights = [gather_rows(jnp.stack([f] + [hop_within(f, j) for j in range(1, split)])) for f in far]
    width = WIDE * cols
    w_up = [w[:, :, :width] for w in weights]
    w_down = [w[:, :, width : 2 * width] for w in weights]
    w_out = jnp.stack([w[:, :, 2 * width :] for w in weights]).reshape(4 * split, n_dp, rows, cols)

    def slot_of(quarter_abs, within_abs):
        return ((place - gray(quarter_abs)) & 3) * split + (within - within_abs) % split

    w_out = jnp.stack([pick(w_out, slot_of(a // split, a % split)) for a in range(4 * split)])
    w_out = jnp.moveaxis(w_out, 1, 0)
    w_out = jnp.stack([pick(w_out, relative(dp, a, order)) for a in range(n_dp)])
    w_out = jnp.transpose(w_out, (0, 2, 1, 3)).reshape(D, D)

    normal_one, inverse_one = layer_stats(scene.astype(f32))
    act_one = (normal_one * gain_one + shift_one).astype(bf16)
    act_all = act_one.reshape(4 * split * tokens, D)
    act_own = act_one[:, 0].reshape(4 * tokens, D)
    q = mm(act_own, w_qkv[:, 0]).astype(bf16)
    k = mm(act_all, w_qkv[:, 1]).astype(bf16)
    v = mm(act_all, w_qkv[:, 2]).astype(bf16)

    def heads(m):
        return jnp.transpose(m.reshape(m.shape[0], GROUP_HEADS, HEAD_DIM), (1, 0, 2))

    def unheads(m):
        return jnp.transpose(m, (1, 0, 2)).reshape(m.shape[1], GROUP_WIDTH)

    views = jnp.stack([(quarter_behind(i) * split * tokens) // VIEW for i in range(4)])
    open_block = (views[None, :] < inputs_seen) | (views[None, :] == views[:, None])
    visible = open_block[:, None, :, None] & (live > 0)[None, None]
    visible = jnp.broadcast_to(visible, (4, tokens, 4, split * tokens)).reshape(4 * tokens, -1)
    scaling = 1.0 / math.sqrt(HEAD_DIM)
    qh, kh, vh = heads(q), heads(k), heads(v)
    scores = jnp.einsum("hqd,hkd->hqk", qh, kh, preferred_element_type=f32) * scaling
    scores = jnp.where(visible[None], scores, masked_score)
    top = jnp.max(scores, axis=-1, keepdims=True)
    probs = jnp.where(visible[None], jnp.exp(scores - top), 0.0)
    probs = probs / jnp.sum(probs, axis=-1, keepdims=True)
    probs_low = probs.astype(bf16)
    attended = jnp.einsum("hqk,hkd->hqd", probs_low, vh, preferred_element_type=f32)
    flat = unheads(attended).astype(bf16).reshape(4, tokens, GROUP_WIDTH)
    back = jnp.stack([flat[0]] + [hop_quarter(flat[i], -i) for i in range(1, 4)])
    act_two = jnp.concatenate([pick(back, (gray(a) - place) & 3) for a in range(4)], axis=1)

    patch_float = patches.astype(f32)
    resid = patch_float + mm(act_two, w_out)
    normal_two, inverse_two = layer_stats(resid)
    act_three = (normal_two * gain_two + shift_two).astype(bf16)

    def to_relative(m):
        parts = m.reshape(tokens, n_dp, rows)
        return jnp.concatenate([lax.dynamic_index_in_dim(parts, dp ^ o, 1, keepdims=False) for o in order], axis=1)

    def from_relative(m):
        parts = m.reshape(tokens, n_dp, rows)
        return jnp.concatenate(
            [lax.dynamic_index_in_dim(parts, relative(dp, a, order), 1, keepdims=False) for a in range(n_dp)], axis=1
        )

    act_rel = to_relative(act_three)
    cot_rel = to_relative(cotangent)
    branch_rel = jnp.zeros((tokens, D), f32)
    three_rel = jnp.zeros((tokens, D), f32)
    far_grads = []
    for i in range(4):
        group = []
        for j in range(split):
            widened = mm(act_rel, w_up[i][j])
            activated, gelu_pull = jax.vjp(partial(jax.nn.gelu, approximate=False), widened)
            hidden = activated.astype(bf16)
            branch_rel = branch_rel + mm_nt(hidden, w_down[i][j])
            grad_wide = gelu_pull(mm(cot_rel, w_down[i][j]))[0].astype(bf16)
            three_rel = three_rel + mm_nt(grad_wide, w_up[i][j])
            grad_up = mm_tn(act_rel, grad_wide).astype(bf16)
            grad_down = mm_tn(cot_rel, hidden).astype(bf16)
            group.append((grad_up, grad_down))
        far_grads.append(group)
    block_out = (resid + from_relative(branch_rel)).astype(bf16)
    grad_three = from_relative(three_rel)
    gain_two_grad = jnp.sum(grad_three * normal_two, axis=0)
    shift_two_grad = jnp.sum(grad_three, axis=0)
    grad_resid = cotangent.astype(f32) + layer_back(grad_three, normal_two, inverse_two, gain_two)
    grad_branch = grad_resid.astype(bf16)
    grad_attended = mm_nt(grad_branch, w_out).astype(bf16)
    grad_w_out = mm_tn(act_two, grad_branch).astype(bf16)

    parts = jnp.transpose(grad_attended.reshape(tokens, 4, GROUP_WIDTH), (1, 0, 2))
    parts = [pick(parts, gray((place + i) & 3)) for i in range(4)]
    grad_here = jnp.concatenate([parts[0]] + [hop_quarter(parts[i], i) for i in range(1, 4)], axis=0)
    gh = heads(grad_here)
    dprobs = jnp.einsum("hqd,hkd->hqk", gh, vh, preferred_element_type=f32)
    delta = jnp.sum(gh.astype(f32) * attended, axis=-1, keepdims=True)
    grad_scores = (probs * (dprobs - delta)).astype(bf16)
    dq = unheads(jnp.einsum("hqk,hkd->hqd", grad_scores, kh, preferred_element_type=f32) * scaling).astype(bf16)
    dk = unheads(jnp.einsum("hqk,hqd->hkd", grad_scores, qh, preferred_element_type=f32) * scaling).astype(bf16)
    dv = unheads(jnp.einsum("hqk,hqd->hkd", probs_low, gh, preferred_element_type=f32)).astype(bf16)

    grad_near = jnp.stack([mm_tn(act_own, dq), mm_tn(act_all, dk), mm_tn(act_all, dv)], axis=1).astype(bf16)
    grad_near = grad_near.reshape(n_dp, rows, 3, split, cols)
    grad_near = jnp.stack([pick(grad_near, dp ^ o) for o in order])
    grad_near = jnp.transpose(grad_near, (3, 0, 1, 2, 4)).reshape(split, D, 3 * cols)
    grad_near = jnp.stack([pick(grad_near, (within - j) % split) for j in range(split)])
    grad_near = reduce_within(reduce_rows(grad_near)).astype(f32).reshape(rows, 3, cols)

    one_q = mm_nt(dq, w_qkv[:, 0]).reshape(4, 1, tokens, D)
    one_kv = (mm_nt(dk, w_qkv[:, 1]) + mm_nt(dv, w_qkv[:, 2])).reshape(4, split, tokens, D)
    one = jnp.concatenate([one_kv[:, :1] + one_q, one_kv[:, 1:]], axis=1)
    gain_one_grad = jnp.sum(one * normal_one, axis=(0, 1, 2))
    shift_one_grad = jnp.sum(one, axis=(0, 1, 2))
    one_low = one.astype(bf16)
    grad_one = reduce_ring([reduce_within(one_low[i]) for i in range(4)])
    patches_grad = grad_resid + layer_back(grad_one, normal_one[0, 0], inverse_one[0, 0], gain_one)

    out_parts = grad_w_out.reshape(n_dp, rows, 4 * split, cols)
    out_parts = jnp.stack([pick(out_parts, dp ^ o) for o in order])
    out_parts = jnp.transpose(out_parts, (2, 0, 1, 3)).reshape(4 * split, D, cols)
    slots = []
    for i in range(4):
        stack = []
        for j in range(split):
            own_out = pick(out_parts, quarter_behind(i) * split + (within - j) % split)
            stack.append(jnp.concatenate([*far_grads[i][j], own_out], axis=1))
        slots.append(reduce_within(reduce_rows(jnp.stack(stack))))
    far_sum = reduce_ring(slots)
    grad_up = far_sum[:, :width].reshape(rows, WIDE, cols)
    grad_down = far_sum[:, width : 2 * width].reshape(rows, WIDE, cols)
    grad_out = far_sum[:, 2 * width :].reshape(rows, 1, cols)

    weight_grad = jnp.concatenate([grad_near, grad_out, grad_up, grad_down], axis=1)
    param_grad = total(jnp.stack([gain_one_grad, shift_one_grad, gain_two_grad, shift_two_grad]))
    squares = total(jnp.full((8, 128), jnp.sum(weight_grad * weight_grad), f32))[0, 0] + jnp.sum(param_grad * param_grad)
    grad_norm = jnp.sqrt(squares)
    clip = 1.0 / jnp.maximum(grad_norm, 1.0)
    new_master, new_moment_one, new_moment_two = adam_step(
        master, weight_grad * clip, moment_one, moment_two, rate_matrix, weight_decay
    )
    new_norm_params, new_norm_moment_one, new_norm_moment_two = adam_step(
        norm_params, param_grad * clip, norm_moment_one, norm_moment_two, rate_vector, 0.0
    )
    return (
        block_out,
        patches_grad,
        new_master,
        new_master.astype(bf16),
        new_moment_one,
        new_moment_two,
        new_norm_params,
        new_norm_moment_one,
        new_norm_moment_two,
        grad_norm,
    )


def relative(dp, absolute, order):
    index = jnp.int32(0)
    for at, offset in enumerate(order):
        index = jnp.where((dp ^ absolute) == offset, at, index)
    return index


def solution(mesh):
    tokens = P(("dp", "seq"), None)
    weights = P("dp", None, "seq")
    return jax.shard_map(
        local,
        mesh=mesh,
        in_specs=(tokens, tokens, P("dp"), P(("dp", "seq")), weights, weights, weights, P(), P(), P()),
        out_specs=(tokens, tokens, weights, weights, weights, weights, P(), P(), P(), P()),
        check_vma=False,
    )
```

```python
import math
from functools import partial

import jax
import jax.numpy as jnp
from jax import lax
from jax.experimental import pallas as pl
from jax.experimental.pallas import tpu as pltpu
from jax.sharding import PartitionSpec as P

D = 768
HEADS = 12
HEAD_DIM = 64
FF = 3072
VIEW = 1024
STEP = 10
GROUPS = 4
GROUP_HEADS = HEADS // GROUPS
GROUP_WIDTH = GROUP_HEADS * HEAD_DIM
WIDE = FF // D
RING = (0, 1, 3, 2)

layer_eps = 1e-05
beta_first = 0.9
beta_second = 0.95
adam_eps = 1e-08
rate_matrix = 0.08
rate_vector = 0.8
weight_decay = 0.1
masked_score = -1e30
bf16 = jnp.bfloat16
f32 = jnp.float32


def gray(v):
    return v ^ (v >> 1)


def hop_quarter(value, by):
    split = lax.axis_size("seq") // GROUPS
    pairs = [
        (RING[p] * split + x, RING[(p + by) % GROUPS] * split + x) for p in range(GROUPS) for x in range(split)
    ]
    return lax.ppermute(value, "seq", pairs)


def hop_within(value, by):
    split = lax.axis_size("seq") // GROUPS
    pairs = [(q * split + x, q * split + (x + by) % split) for q in range(GROUPS) for x in range(split)]
    return lax.ppermute(value, "seq", pairs)


def swap(value, axis, bit):
    return lax.ppermute(value, axis, [(i, i ^ bit) for i in range(lax.axis_size(axis))])


def bits_of(axis):
    return [1 << b for b in range(lax.axis_size(axis).bit_length() - 1)]


def total(value):
    for axis in ("dp", "seq"):
        for bit in bits_of(axis):
            value = value + swap(value, axis, bit)
    return value


def pick(stack, index):
    return lax.dynamic_index_in_dim(stack, index, 0, keepdims=False)


def layer_stats(values):
    centre = jnp.mean(values, axis=-1, keepdims=True)
    shifted = values - centre
    spread = jnp.mean(shifted * shifted, axis=-1, keepdims=True)
    inverse = lax.rsqrt(spread + layer_eps)
    return (shifted * inverse, inverse)


def layer_back(grad_normed, normalized, inverse, gain):
    scaled = grad_normed * gain
    centred = jnp.mean(scaled, axis=-1, keepdims=True)
    along = jnp.mean(scaled * normalized, axis=-1, keepdims=True)
    return inverse * (scaled - centred - normalized * along)


def mm(a, b):
    return jnp.dot(a, b, preferred_element_type=f32)


def mm_nt(a, b):
    return lax.dot_general(a, b, (((1,), (1,)), ((), ())), preferred_element_type=f32)


def mm_tn(a, b):
    return lax.dot_general(a, b, (((0,), (0,)), ((), ())), preferred_element_type=f32)


def gather_rows(piece):
    for bit in reversed(bits_of("dp")):
        piece = jnp.concatenate([piece, swap(piece, "dp", bit)], axis=1)
    return piece


def row_order():
    order = [0]
    for bit in reversed(bits_of("dp")):
        order = order + [o ^ bit for o in order]
    return order


def reduce_rows(piece):
    for bit in bits_of("dp"):
        half = piece.shape[1] // 2
        there = swap(piece[:, half:], "dp", bit)
        piece = (piece[:, :half].astype(f32) + there.astype(f32)).astype(bf16)
    return piece


def reduce_within(piece):
    own = piece[0].astype(f32)
    for j in range(1, piece.shape[0]):
        own = own + hop_within(piece[j], -j).astype(f32)
    return own.astype(bf16)


def reduce_ring(slots):
    moving = slots[1]
    for k in (2, 3):
        moving = (hop_quarter(moving, 1).astype(f32) + slots[k].astype(f32)).astype(bf16)
    return hop_quarter(moving, 1).astype(f32) + slots[0].astype(f32)


def adam_step(params, grads, first, second, rate, decay):
    first_new = beta_first * first + (1.0 - beta_first) * grads
    second_new = beta_second * second + (1.0 - beta_second) * grads * grads
    first_hat = first_new / (1.0 - beta_first**STEP)
    second_hat = second_new / (1.0 - beta_second**STEP)
    params_new = params - rate * (first_hat / (jnp.sqrt(second_hat) + adam_eps) + decay * params)
    return (params_new, first_new, second_new)


def relative(dp, absolute, order):
    index = jnp.int32(0)
    for at, offset in enumerate(order):
        index = jnp.where((dp ^ absolute) == offset, at, index)
    return index


def step_general(
    patches,
    cotangent,
    input_views,
    token_live,
    master,
    moment_one,
    moment_two,
    norm_params,
    norm_moment_one,
    norm_moment_two,
):
    tokens = patches.shape[0]
    rows, blocks, cols = master.shape
    n_dp = lax.axis_size("dp")
    split = lax.axis_size("seq") // GROUPS
    dp = lax.axis_index("dp")
    seq = lax.axis_index("seq")
    quarter, within = seq // split, seq % split
    place = gray(quarter)
    inputs_seen = input_views[0]
    gain_one, shift_one, gain_two, shift_two = (norm_params[i] for i in range(4))
    order = row_order()
    dp_place = [order.index(a) for a in range(n_dp)]

    def quarter_behind(k):
        return gray((place - k) & 3)

    flags = jnp.pad(token_live.astype(bf16)[None, :], ((0, 7), (0, D - tokens)))
    ring = [jnp.concatenate([patches, flags], axis=0)]
    for _ in range(3):
        ring.append(hop_quarter(ring[-1], 1))
    pieces = [[ring[k]] + [hop_within(ring[k], j) for j in range(1, split)] for k in range(4)]
    scene = jnp.stack([jnp.stack([p[:tokens] for p in pieces[k]]) for k in range(4)])
    live = jnp.stack([jnp.concatenate([p[tokens, :tokens] for p in pieces[k]]) for k in range(4)])

    copy_low = master.astype(bf16)
    mine = copy_low[:, 0:3, :].reshape(rows, 3 * cols)
    near = jnp.stack([mine] + [hop_within(mine, j) for j in range(1, split)])
    near = gather_rows(near).reshape(split, n_dp, rows, 3, cols)
    near = jnp.stack([pick(near, (within - a) % split) for a in range(split)])
    near = jnp.moveaxis(near, 1, 0)
    near = jnp.stack([pick(near, order_at) for order_at in [relative(dp, a, order) for a in range(n_dp)]])
    w_qkv = jnp.transpose(near, (0, 2, 3, 1, 4)).reshape(D, 3, GROUP_WIDTH)

    up = copy_low[:, 4 : 4 + WIDE].reshape(rows, WIDE * cols)
    down = copy_low[:, 4 + WIDE :].reshape(rows, WIDE * cols)
    far = [jnp.concatenate([up, down, copy_low[:, 3]], axis=1)]
    for _ in range(3):
        far.append(hop_quarter(far[-1], 1))
    weights = [gather_rows(jnp.stack([f] + [hop_within(f, j) for j in range(1, split)])) for f in far]
    width = WIDE * cols
    w_up = [w[:, :, :width] for w in weights]
    w_down = [w[:, :, width : 2 * width] for w in weights]
    w_out = jnp.stack([w[:, :, 2 * width :] for w in weights]).reshape(4 * split, n_dp, rows, cols)

    def slot_of(quarter_abs, within_abs):
        return ((place - gray(quarter_abs)) & 3) * split + (within - within_abs) % split

    w_out = jnp.stack([pick(w_out, slot_of(a // split, a % split)) for a in range(4 * split)])
    w_out = jnp.moveaxis(w_out, 1, 0)
    w_out = jnp.stack([pick(w_out, relative(dp, a, order)) for a in range(n_dp)])
    w_out = jnp.transpose(w_out, (0, 2, 1, 3)).reshape(D, D)

    normal_one, inverse_one = layer_stats(scene.astype(f32))
    act_one = (normal_one * gain_one + shift_one).astype(bf16)
    act_all = act_one.reshape(4 * split * tokens, D)
    act_own = act_one[:, 0].reshape(4 * tokens, D)
    q = mm(act_own, w_qkv[:, 0]).astype(bf16)
    k = mm(act_all, w_qkv[:, 1]).astype(bf16)
    v = mm(act_all, w_qkv[:, 2]).astype(bf16)

    def heads(m):
        return jnp.transpose(m.reshape(m.shape[0], GROUP_HEADS, HEAD_DIM), (1, 0, 2))

    def unheads(m):
        return jnp.transpose(m, (1, 0, 2)).reshape(m.shape[1], GROUP_WIDTH)

    views = jnp.stack([(quarter_behind(i) * split * tokens) // VIEW for i in range(4)])
    open_block = (views[None, :] < inputs_seen) | (views[None, :] == views[:, None])
    visible = open_block[:, None, :, None] & (live > 0)[None, None]
    visible = jnp.broadcast_to(visible, (4, tokens, 4, split * tokens)).reshape(4 * tokens, -1)
    scaling = 1.0 / math.sqrt(HEAD_DIM)
    qh, kh, vh = heads(q), heads(k), heads(v)
    scores = jnp.einsum("hqd,hkd->hqk", qh, kh, preferred_element_type=f32) * scaling
    scores = jnp.where(visible[None], scores, masked_score)
    top = jnp.max(scores, axis=-1, keepdims=True)
    probs = jnp.where(visible[None], jnp.exp(scores - top), 0.0)
    probs = probs / jnp.sum(probs, axis=-1, keepdims=True)
    probs_low = probs.astype(bf16)
    attended = jnp.einsum("hqk,hkd->hqd", probs_low, vh, preferred_element_type=f32)
    flat = unheads(attended).astype(bf16).reshape(4, tokens, GROUP_WIDTH)
    back = jnp.stack([flat[0]] + [hop_quarter(flat[i], -i) for i in range(1, 4)])
    act_two = jnp.concatenate([pick(back, (gray(a) - place) & 3) for a in range(4)], axis=1)

    patch_float = patches.astype(f32)
    resid = patch_float + mm(act_two, w_out)
    normal_two, inverse_two = layer_stats(resid)
    act_three = (normal_two * gain_two + shift_two).astype(bf16)

    def to_relative(m):
        parts = m.reshape(tokens, n_dp, rows)
        return jnp.concatenate([lax.dynamic_index_in_dim(parts, dp ^ o, 1, keepdims=False) for o in order], axis=1)

    def from_relative(m):
        parts = m.reshape(tokens, n_dp, rows)
        return jnp.concatenate(
            [lax.dynamic_index_in_dim(parts, relative(dp, a, order), 1, keepdims=False) for a in range(n_dp)], axis=1
        )

    act_rel = to_relative(act_three)
    cot_rel = to_relative(cotangent)
    branch_rel = jnp.zeros((tokens, D), f32)
    three_rel = jnp.zeros((tokens, D), f32)
    far_grads = []
    for i in range(4):
        group = []
        for j in range(split):
            widened = mm(act_rel, w_up[i][j])
            activated, gelu_pull = jax.vjp(partial(jax.nn.gelu, approximate=False), widened)
            hidden = activated.astype(bf16)
            branch_rel = branch_rel + mm_nt(hidden, w_down[i][j])
            grad_wide = gelu_pull(mm(cot_rel, w_down[i][j]))[0].astype(bf16)
            three_rel = three_rel + mm_nt(grad_wide, w_up[i][j])
            grad_up = mm_tn(act_rel, grad_wide).astype(bf16)
            grad_down = mm_tn(cot_rel, hidden).astype(bf16)
            group.append((grad_up, grad_down))
        far_grads.append(group)
    block_out = (resid + from_relative(branch_rel)).astype(bf16)
    grad_three = from_relative(three_rel)
    gain_two_grad = jnp.sum(grad_three * normal_two, axis=0)
    shift_two_grad = jnp.sum(grad_three, axis=0)
    grad_resid = cotangent.astype(f32) + layer_back(grad_three, normal_two, inverse_two, gain_two)
    grad_branch = grad_resid.astype(bf16)
    grad_attended = mm_nt(grad_branch, w_out).astype(bf16)
    grad_w_out = mm_tn(act_two, grad_branch).astype(bf16)

    parts = jnp.transpose(grad_attended.reshape(tokens, 4, GROUP_WIDTH), (1, 0, 2))
    parts = [pick(parts, gray((place + i) & 3)) for i in range(4)]
    grad_here = jnp.concatenate([parts[0]] + [hop_quarter(parts[i], i) for i in range(1, 4)], axis=0)
    gh = heads(grad_here)
    dprobs = jnp.einsum("hqd,hkd->hqk", gh, vh, preferred_element_type=f32)
    delta = jnp.sum(gh.astype(f32) * attended, axis=-1, keepdims=True)
    grad_scores = (probs * (dprobs - delta)).astype(bf16)
    dq = unheads(jnp.einsum("hqk,hkd->hqd", grad_scores, kh, preferred_element_type=f32) * scaling).astype(bf16)
    dk = unheads(jnp.einsum("hqk,hqd->hkd", grad_scores, qh, preferred_element_type=f32) * scaling).astype(bf16)
    dv = unheads(jnp.einsum("hqk,hqd->hkd", probs_low, gh, preferred_element_type=f32)).astype(bf16)

    grad_near = jnp.stack([mm_tn(act_own, dq), mm_tn(act_all, dk), mm_tn(act_all, dv)], axis=1).astype(bf16)
    grad_near = grad_near.reshape(n_dp, rows, 3, split, cols)
    grad_near = jnp.stack([pick(grad_near, dp ^ o) for o in order])
    grad_near = jnp.transpose(grad_near, (3, 0, 1, 2, 4)).reshape(split, D, 3 * cols)
    grad_near = jnp.stack([pick(grad_near, (within - j) % split) for j in range(split)])
    grad_near = reduce_within(reduce_rows(grad_near)).astype(f32).reshape(rows, 3, cols)

    one_q = mm_nt(dq, w_qkv[:, 0]).reshape(4, 1, tokens, D)
    one_kv = (mm_nt(dk, w_qkv[:, 1]) + mm_nt(dv, w_qkv[:, 2])).reshape(4, split, tokens, D)
    one = jnp.concatenate([one_kv[:, :1] + one_q, one_kv[:, 1:]], axis=1)
    gain_one_grad = jnp.sum(one * normal_one, axis=(0, 1, 2))
    shift_one_grad = jnp.sum(one, axis=(0, 1, 2))
    one_low = one.astype(bf16)
    grad_one = reduce_ring([reduce_within(one_low[i]) for i in range(4)])
    patches_grad = grad_resid + layer_back(grad_one, normal_one[0, 0], inverse_one[0, 0], gain_one)

    out_parts = grad_w_out.reshape(n_dp, rows, 4 * split, cols)
    out_parts = jnp.stack([pick(out_parts, dp ^ o) for o in order])
    out_parts = jnp.transpose(out_parts, (2, 0, 1, 3)).reshape(4 * split, D, cols)
    slots = []
    for i in range(4):
        stack = []
        for j in range(split):
            own_out = pick(out_parts, quarter_behind(i) * split + (within - j) % split)
            stack.append(jnp.concatenate([*far_grads[i][j], own_out], axis=1))
        slots.append(reduce_within(reduce_rows(jnp.stack(stack))))
    far_sum = reduce_ring(slots)
    grad_up = far_sum[:, :width].reshape(rows, WIDE, cols)
    grad_down = far_sum[:, width : 2 * width].reshape(rows, WIDE, cols)
    grad_out = far_sum[:, 2 * width :].reshape(rows, 1, cols)

    weight_grad = jnp.concatenate([grad_near, grad_out, grad_up, grad_down], axis=1)
    param_grad = total(jnp.stack([gain_one_grad, shift_one_grad, gain_two_grad, shift_two_grad]))
    squares = total(jnp.full((8, 128), jnp.sum(weight_grad * weight_grad), f32))[0, 0] + jnp.sum(param_grad * param_grad)
    grad_norm = jnp.sqrt(squares)
    clip = 1.0 / jnp.maximum(grad_norm, 1.0)
    new_master, new_moment_one, new_moment_two = adam_step(
        master, weight_grad * clip, moment_one, moment_two, rate_matrix, weight_decay
    )
    new_norm_params, new_norm_moment_one, new_norm_moment_two = adam_step(
        norm_params, param_grad * clip, norm_moment_one, norm_moment_two, rate_vector, 0.0
    )
    return (
        block_out,
        patches_grad,
        new_master,
        new_master.astype(bf16),
        new_moment_one,
        new_moment_two,
        new_norm_params,
        new_norm_moment_one,
        new_norm_moment_two,
        grad_norm,
    )


HALF = 48
ANY = pl.BlockSpec(memory_space=pl.ANY)
SMEM = pl.BlockSpec(memory_space=pltpu.SMEM)
VMEM_LIMIT = 56 << 20


def call(body, name, ins, outs, operands, scratch=(), aliases=None):
    return pl.pallas_call(
        body,
        name=name,
        out_shape=outs,
        in_specs=ins,
        out_specs=jax.tree.map(lambda _: pl.BlockSpec(memory_space=pltpu.VMEM), outs),
        scratch_shapes=list(scratch),
        input_output_aliases=aliases or {},
        compiler_params=pltpu.CompilerParams(vmem_limit_bytes=VMEM_LIMIT),
    )(*operands)


VM = pl.BlockSpec(memory_space=pltpu.VMEM)


def shape(dims, dtype):
    return jax.ShapeDtypeStruct(dims, dtype)


def run_copies(copies):
    for c in copies:
        c.start()
    for c in copies:
        c.wait()


def place_qkv(own, x_place, y_place, core, pieces):
    def body(at, pieces_ref, out_ref, sems):
        x, y, c = at[0], at[1], at[2]
        copies = []
        for block in range(3):
            for xa in range(2):
                for half in range(2):
                    for ya in range(2):
                        source = ((x ^ xa) * 2 + (y ^ ya)) * 2 + (c ^ half)
                        row = block * GROUP_WIDTH + (xa * 2 + half) * HALF
                        copies.append(
                            pltpu.make_async_copy(
                                pieces_ref.at[source, pl.ds(block * HALF, HALF), :],
                                out_ref.at[pl.ds(row, HALF), pl.ds(ya * 384, 384)],
                                sems.at[len(copies)],
                            )
                        )
        run_copies(copies)

    at = jnp.stack([x_place, y_place, core]).astype(jnp.int32)
    return call(
        body, "place_qkv", [SMEM, ANY], shape((3 * GROUP_WIDTH, D), bf16), (at, pieces), [pltpu.SemaphoreType.DMA((24,))]
    )


def place_out(at, own_half, other_half):
    def body(at_ref, own_ref, other_ref, out_ref, sems):
        x, y, c, place = at_ref[0], at_ref[1], at_ref[2], at_ref[3]
        copies = []
        for k in range(4):
            quarter = gray((place - k) & 3)
            for j in range(2):
                for r in range(2):
                    for h, ref in ((0, own_ref), (1, other_ref)):
                        row = (quarter * 2 + (x ^ j)) * 96 + (c ^ h) * HALF
                        copies.append(
                            pltpu.make_async_copy(
                                ref.at[(k * 2 + j) * 2 + r],
                                out_ref.at[
                                    pl.ds(pl.multiple_of(row, 16), HALF),
                                    pl.ds(pl.multiple_of((y ^ r) * 384, 128), 384),
                                ],
                                sems.at[len(copies)],
                            )
                        )
        run_copies(copies)

    return call(
        body,
        "place_out",
        [SMEM, ANY, ANY],
        shape((D, D), bf16),
        (at, own_half, other_half),
        [pltpu.SemaphoreType.DMA((32,))],
    )


def normalize(values):
    centre = jnp.mean(values, axis=-1, keepdims=True)
    shifted = values - centre
    inverse = lax.rsqrt(jnp.mean(shifted * shifted, axis=-1, keepdims=True) + layer_eps)
    return shifted * inverse, inverse


def lane_index(dims):
    return lax.broadcasted_iota(jnp.int32, dims, len(dims) - 1)


def project(first, second, w_t, norms):
    def body(a_ref, b_ref, w_ref, norm_ref, act_ref, normal_ref, q_ref, k_ref, v_ref, wide_ref):
        wide_ref[...] = jnp.zeros_like(wide_ref)
        for h in range(9):
            wide_ref[h * 128 : h * 128 + 64, :] = w_ref[h * 64 : h * 64 + 64, :]
        gain, shift = norm_ref[0:1, :], norm_ref[1:2, :]
        for piece, ref in enumerate((a_ref, b_ref)):
            at = slice(piece * 256, piece * 256 + 256)
            normal, _ = normalize(ref[0:256, :].astype(f32))
            act = (normal * gain + shift).astype(bf16)
            normal_ref[at, :] = normal.astype(bf16)
            act_ref[at, :] = act
            flags = ref[256:257, 0:256].astype(f32)
            mask = jnp.where(flags > 0, 0.0, masked_score)
            mask = jnp.transpose(jnp.broadcast_to(mask, (128, 256)))
            lanes = lane_index((256, 128))
            for h in range(3):
                if piece == 0:
                    q = mm_nt(act, wide_ref[h * 128 : h * 128 + 128, :]).astype(bf16).astype(f32)
                    q = jnp.where(lanes == 64, 1.0, q * (1.0 / math.sqrt(HEAD_DIM)))
                    q_ref[h] = q.astype(bf16)
                k = mm_nt(act, wide_ref[(3 + h) * 128 : (4 + h) * 128, :])
                k = jnp.where(lanes == 64, mask, k)
                k_ref[h, at, :] = jnp.where((lanes > 64) & (lanes < 68), 1.0, k).astype(bf16)
                v = mm_nt(act, wide_ref[(6 + h) * 128 : (7 + h) * 128, :])
                v_ref[h, at, :] = jnp.where((lanes > 63) & (lanes < 67), 1.0, v).astype(bf16)

    outs = [
        shape((512, D), bf16),
        shape((512, D), bf16),
        shape((3, 256, 128), bf16),
        shape((3, 512, 128), bf16),
        shape((3, 512, 128), bf16),
    ]
    return call(body, "norm_project", [VM] * 4, outs, (first, second, w_t, norms), [pltpu.VMEM((1152, D), bf16)])


def in_three(value):
    high = value.astype(bf16).astype(f32)
    rest = value - high
    mid = rest.astype(bf16).astype(f32)
    return high, mid, rest - mid


def with_parts(base, lanes, first, value):
    for i, part in enumerate(in_three(value)):
        base = jnp.where(lanes == first + i, part, base)
    return base


def join_heads(parts):
    return jnp.concatenate([p[:, :HEAD_DIM] for p in parts], axis=1)


def attend(seen, qs, ks, vs):
    def body(seen_ref, *refs):
        q_refs, k_refs, v_refs = refs[0:4], refs[4:8], refs[8:12]
        low_refs, full_ref, back_refs = refs[12:16], refs[16], refs[17:21]
        top_ref, sum_ref = refs[21:23]
        lanes = lane_index((256, 128))

        def head(h, _):
            for i in range(4):
                q = q_refs[i][h]
                s = mm_nt(q, k_refs[i][h])
                top = jnp.max(s, axis=-1, keepdims=True)
                top_ref[...] = jnp.broadcast_to(top, (256, 128))
                sum_ref[...] = mm(jnp.exp(s - top).astype(bf16), v_refs[i][h])
                for c in range(4):
                    if c == i:
                        continue

                    @pl.when(seen_ref[i * 4 + c] > 0)
                    def _():
                        s = mm_nt(q, k_refs[c][h])
                        old = top_ref[:, 0:1]
                        top = jnp.maximum(old, jnp.max(s, axis=-1, keepdims=True))
                        top_ref[...] = jnp.broadcast_to(top, (256, 128))
                        p = jnp.exp(s - top).astype(bf16)
                        sum_ref[...] = sum_ref[...] * jnp.exp(old - top) + mm(p, v_refs[c][h])

                mixed = sum_ref[...]
                norm = mixed[:, HEAD_DIM : HEAD_DIM + 1]
                full_ref[h, i] = mixed / norm
                logsum = top_ref[:, 0:1] + jnp.log(norm)
                back_refs[i][h] = with_parts(q.astype(f32), lanes, 65, -logsum).astype(bf16)
            return 0

        lax.fori_loop(0, 3, head, 0)
        for i in range(4):
            low_refs[i][...] = join_heads([full_ref[h, i] for h in range(3)]).astype(bf16)

    outs = (
        [shape((256, GROUP_WIDTH), bf16)] * 4 + [shape((3, 4, 256, 128), f32)] + [shape((3, 256, 128), bf16)] * 4
    )
    got = call(
        body,
        "attend",
        [SMEM] + [VM] * 12,
        outs,
        (seen, *qs, *ks, *vs),
        [pltpu.VMEM((256, 128), f32), pltpu.VMEM((256, 128), f32)],
    )
    return got[0:4], got[4], got[5:9]


def attend_back(seen, qs, ks, vs, full, grads):
    def body(seen_ref, *refs):
        q_refs, k_refs, v_refs, full_ref, g_refs = refs[0:4], refs[4:8], refs[8:12], refs[12], refs[13:17]
        dq_refs, dk_refs, dv_refs = refs[17:21], refs[21:25], refs[25:29]
        g_ref, dq_ref, dk_ref, dv_ref = refs[29:33]
        lanes = lane_index((256, 128))
        for i in range(4):
            for h in range(3):
                g = g_refs[i][:, h * 64 : h * 64 + 64].astype(f32)
                delta = jnp.sum(g * full_ref[h, i][:, :64], axis=-1, keepdims=True)
                g = jnp.concatenate([g, jnp.zeros((256, 64), f32)], axis=1)
                g_ref[h, i] = with_parts(g, lanes, 64, -delta).astype(bf16)
        dq_ref[...] = jnp.zeros_like(dq_ref)
        dk_ref[...] = jnp.zeros_like(dk_ref)
        dv_ref[...] = jnp.zeros_like(dv_ref)

        def head(h, _):
            for c in range(4):
                k, v = k_refs[c][h], v_refs[c][h]
                for i in range(4):

                    @pl.when(seen_ref[i * 4 + c] > 0)
                    def _():
                        q, g = q_refs[i][h], g_ref[h, i]
                        p = jnp.exp(mm_nt(k, q))
                        ds = (p * mm_nt(v, g)).astype(bf16)
                        dv_ref[h, c] += mm(p.astype(bf16), g)
                        dk_ref[h, c] += mm(ds, q)
                        dq_ref[h, i] += mm_tn(ds, k)

            return 0

        lax.fori_loop(0, 3, head, 0)
        for i in range(4):
            dq_refs[i][...] = (join_heads([dq_ref[h, i] for h in range(3)]) * (1.0 / math.sqrt(HEAD_DIM))).astype(bf16)
            dk_refs[i][...] = join_heads([dk_ref[h, i] for h in range(3)]).astype(bf16)
            dv_refs[i][...] = join_heads([dv_ref[h, i] for h in range(3)]).astype(bf16)

    outs = [shape((256, GROUP_WIDTH), bf16)] * 4 + [shape((512, GROUP_WIDTH), bf16)] * 8
    got = call(
        body,
        "attend_back",
        [SMEM] + [VM] * 17,
        outs,
        (seen, *qs, *ks, *vs, full, *grads),
        [
            pltpu.VMEM((3, 4, 256, 128), bf16),
            pltpu.VMEM((3, 4, 256, 128), f32),
            pltpu.VMEM((3, 4, 512, 128), f32),
            pltpu.VMEM((3, 4, 512, 128), f32),
        ],
    )
    return got[0:4], got[4:8], got[8:12]


def project_back(at, acts, normals, dqs, dks, dvs, w_t):
    def body(at_ref, *refs):
        act_refs, normal_refs, dq_refs, dk_refs, dv_refs, w_ref = (
            refs[0:4],
            refs[4:8],
            refs[8:12],
            refs[12:16],
            refs[16:20],
            refs[20],
        )
        keep_refs, send_refs, w_keep_ref, w_send_ref, norm_ref, dw_ref = refs[21:25], refs[25:29], *refs[29:33]
        gains, shifts = jnp.zeros((1, D), f32), jnp.zeros((1, D), f32)
        for i in range(4):
            act = act_refs[i][...]
            for b, (ref, rows) in enumerate(((dq_refs[i], 256), (dk_refs[i], 512), (dv_refs[i], 512))):
                part = mm_tn(ref[...], act[:rows])
                at_rows = slice(b * GROUP_WIDTH, (b + 1) * GROUP_WIDTH)
                dw_ref[at_rows, :] = part if i == 0 else dw_ref[at_rows, :] + part
            for j, out_ref in enumerate((keep_refs[i], send_refs[i])):
                r = slice(j * 256, j * 256 + 256)
                one = mm(dk_refs[i][r, :], w_ref[192:384, :]) + mm(dv_refs[i][r, :], w_ref[384:576, :])
                if j == 0:
                    one = one + mm(dq_refs[i][...], w_ref[0:192, :])
                gains = gains + jnp.sum(one * normal_refs[i][r, :].astype(f32), axis=0, keepdims=True)
                shifts = shifts + jnp.sum(one, axis=0, keepdims=True)
                out_ref[...] = one.astype(bf16)
        norm_ref[...] = jnp.concatenate([gains, shifts, jnp.zeros((6, D), f32)], axis=0)
        x, c = at_ref[0], at_ref[2]
        for b in range(3):
            for xa in range(2):
                for half in range(2):
                    row = b * GROUP_WIDTH + (xa * 2 + half) * HALF
                    block = dw_ref[row : row + HALF, :].astype(bf16)

                    @pl.when(c == half)
                    def _():
                        w_keep_ref[(x ^ xa) * 3 + b] = block

                    @pl.when(c != half)
                    def _():
                        w_send_ref[(x ^ xa) * 3 + b] = block

    outs = (
        [shape((256, D), bf16)] * 8 + [shape((6, HALF, D), bf16)] * 2 + [shape((8, D), f32)]
    )
    got = call(
        body,
        "project_back",
        [SMEM] + [VM] * 21,
        outs,
        (at, *acts, *normals, *dqs, *dks, *dvs, w_t),
        [pltpu.VMEM((3 * GROUP_WIDTH, D), f32)],
    )
    return got[0:4], got[4:8], got[8], got[9], got[10]


def out_norm(at, patches, mixed, w_out, norms):
    def body(at_ref, x_ref, m0, m1, m2, m3, w_ref, norm_ref, two_ref, resid_ref, normal_ref, inverse_ref, three_ref):
        place = at_ref[3]
        parts = [m[...].astype(f32) for m in (m0, m1, m2, m3)]
        groups = []
        for a in range(4):
            steps = (gray(a) - place) & 3
            part = parts[0]
            for k in (1, 2, 3):
                part = jnp.where(steps == k, parts[k], part)
            groups.append(part)
        two = jnp.concatenate(groups, axis=1).astype(bf16)
        two_ref[...] = two
        resid = x_ref[...].astype(f32) + mm_nt(two, w_ref[...])
        resid_ref[...] = resid
        normal, inverse = normalize(resid)
        normal_ref[...] = normal
        inverse_ref[...] = jnp.broadcast_to(inverse, (256, 128))
        three_ref[...] = (normal * norm_ref[2:3, :] + norm_ref[3:4, :]).astype(bf16)

    outs = [
        shape((256, D), bf16),
        shape((256, D), f32),
        shape((256, D), f32),
        shape((256, 128), f32),
        shape((256, D), bf16),
    ]
    return call(body, "out_norm", [SMEM] + [VM] * 7, outs, (at, patches, *mixed, w_out, norms))


def mlp(at, acts, cots, weights, carried, last):
    count = len(weights)

    def body(at_ref, *refs):
        a_refs, c_refs = refs[0:2], refs[2:4]
        w_refs = refs[4 : 4 + 4 * count]
        at_in = 4 + 4 * count
        carried_refs = refs[at_in : at_in + len(carried)]
        outs = refs[at_in + len(carried) :]
        out_ref, three_ref = outs[0:2]
        keep_refs, send_refs = outs[2 : 2 + count], outs[2 + count : 2 + 2 * count]
        act_ref, cot_ref, w_ref, out_acc, three_acc, sems = outs[2 + 2 * count + (2 if last else 0) :]
        y = at_ref[1]
        own_lanes = pl.ds(pl.multiple_of(y * 384, 128), 384)
        other_lanes = pl.ds(pl.multiple_of((1 - y) * 384, 128), 384)
        copies = []
        for n in range(count):
            group = []
            for r, lanes in enumerate((own_lanes, other_lanes)):
                for j in range(2):
                    for u in range(2):
                        group.append(
                            pltpu.make_async_copy(
                                w_refs[4 * n + 2 * r + j].at[pl.ds(u * 192, 192), :],
                                w_ref.at[n, u, pl.ds(j * 192, 192), lanes],
                                sems.at[n, len(group)],
                            )
                        )
            copies.append(group)
            for c in group:
                c.start()
        for i in range(2):
            act_ref[i * 256 : i * 256 + 256, :] = a_refs[i][...]
            cot_ref[i * 256 : i * 256 + 256, :] = c_refs[i][...]
        for n in range(count):
            for c in copies[n]:
                c.wait()
            act, cot = act_ref[...], cot_ref[...]
            up, down = w_ref[n, 0], w_ref[n, 1]
            widened = mm_nt(act, up)
            inner = 0.5 * (1.0 + lax.erf(widened * (1.0 / math.sqrt(2.0))))
            slope = inner + widened * jnp.exp(-0.5 * widened * widened) * (1.0 / math.sqrt(2.0 * math.pi))
            hidden = (widened * inner).astype(bf16)
            grad_wide = (mm_nt(cot, down) * slope).astype(bf16)
            out = mm(hidden, down)
            three = mm(grad_wide, up)
            if n == 0 and not carried:
                out_acc[...] = out
                three_acc[...] = three
            elif n == 0:
                out_acc[...] = carried_refs[0][...] + out
                three_acc[...] = carried_refs[1][...] + three
            else:
                out_acc[...] += out
                three_acc[...] += three
            for lanes, ref in ((own_lanes, keep_refs[n]), (other_lanes, send_refs[n])):
                grad_up = mm_tn(grad_wide, act_ref[:, lanes]).astype(bf16)
                grad_down = mm_tn(hidden, cot_ref[:, lanes]).astype(bf16)
                for j in range(2):
                    ref[j, 0:192, :] = grad_up[j * 192 : j * 192 + 192]
                    ref[j, 192:384, :] = grad_down[j * 192 : j * 192 + 192]
        if last:
            out_ref[...] = out_acc[0:256, :]
            three_ref[...] = three_acc[0:256, :]
            outs[2 + 2 * count][...] = out_acc[256:512, :].astype(bf16)
            outs[3 + 2 * count][...] = three_acc[256:512, :].astype(bf16)
        else:
            out_ref[...] = out_acc[...]
            three_ref[...] = three_acc[...]

    rows = 256 if last else 512
    outs = [shape((rows, D), f32)] * 2 + [shape((2, 384, 384), bf16)] * (2 * count)
    if last:
        outs = outs + [shape((256, D), bf16)] * 2
    flat = [w for group in weights for w in group]
    return call(
        body,
        "mlp",
        [SMEM] + [VM] * 4 + [ANY] * len(flat) + [VM] * len(carried),
        outs,
        (at, *acts, *cots, *flat, *carried),
        [
            pltpu.VMEM((512, D), bf16),
            pltpu.VMEM((512, D), bf16),
            pltpu.VMEM((count, 2, 384, D), bf16),
            pltpu.VMEM((512, D), f32),
            pltpu.VMEM((512, D), f32),
            pltpu.SemaphoreType.DMA((count, 8)),
        ],
    )


def norm_out_back(at, three, three_there, cotangent, normal, inverse, two, w_out, norms):
    def body(at_ref, t_ref, s_ref, c_ref, n_ref, i_ref, two_ref, w_ref, norm_ref, *outs):
        resid_ref, sums_ref = outs[0:2]
        g_refs, keep_ref, send_ref, dw_ref = outs[2:6], outs[6], outs[7], outs[8]
        x, c, place = at_ref[0], at_ref[2], at_ref[3]
        grad = t_ref[...] + s_ref[...].astype(f32)
        normal = n_ref[...]
        sums_ref[...] = jnp.concatenate(
            [jnp.sum(grad * normal, axis=0, keepdims=True), jnp.sum(grad, axis=0, keepdims=True), jnp.zeros((6, D), f32)],
            axis=0,
        )
        resid = c_ref[...].astype(f32) + layer_back(grad, normal, i_ref[:, 0:1], norm_ref[2:3, :])
        resid_ref[...] = resid
        low = resid.astype(bf16)
        back = mm(low, w_ref[...])
        groups = [back[:, a * GROUP_WIDTH : (a + 1) * GROUP_WIDTH] for a in range(4)]
        for k in range(4):
            ahead = gray((place + k) & 3)
            part = groups[0]
            for a in (1, 2, 3):
                part = jnp.where(ahead == a, groups[a], part)
            g_refs[k][...] = part.astype(bf16)
        dw_ref[...] = mm_tn(low, two_ref[...])
        for q in range(4):
            for xa in range(2):
                slot = ((place - gray(q)) & 3) * 2 + (x ^ xa)
                for half in range(2):
                    row = (q * 2 + xa) * 96 + half * HALF
                    block = dw_ref[row : row + HALF, :].astype(bf16)

                    @pl.when(c == half)
                    def _():
                        keep_ref[slot] = block

                    @pl.when(c != half)
                    def _():
                        send_ref[slot] = block

    outs = (
        [shape((256, D), f32), shape((8, D), f32)]
        + [shape((256, GROUP_WIDTH), bf16)] * 4
        + [shape((8, HALF, D), bf16)] * 2
    )
    got = call(
        body,
        "norm_out_back",
        [SMEM] + [VM] * 8,
        outs,
        (at, three, three_there, cotangent, normal, inverse, two, w_out, norms),
        [pltpu.VMEM((D, D), f32)],
    )
    return got[0], got[1], got[2:6], got[6], got[7]


def add_low(a, b):
    return (a.astype(f32) + b.astype(f32)).astype(bf16)


def step_small(
    patches,
    cotangent,
    input_views,
    token_live,
    master,
    moment_one,
    moment_two,
    norm_params,
    norm_moment_one,
    norm_moment_two,
):
    tokens = patches.shape[0]
    rows, blocks, cols = master.shape
    dp = lax.axis_index("dp")
    seq = lax.axis_index("seq")
    quarter, x_place = seq // 2, seq % 2
    y_place, core = dp // 2, dp % 2
    place = gray(quarter)
    at = jnp.stack([x_place, y_place, core, place]).astype(jnp.int32)

    def to_core(value):
        return swap(value, "dp", 1)

    def to_y(value):
        return swap(value, "dp", 2)

    def to_x(value):
        return swap(value, "seq", 1)

    def by_core(first, second):
        return jnp.where(core == 0, first, second), jnp.where(core == 0, second, first)

    flags = jnp.pad(token_live.astype(bf16)[None, :], ((0, 7), (0, D - tokens)))
    ring = [jnp.concatenate([patches, flags], axis=0)]
    for _ in range(3):
        ring.append(hop_quarter(ring[-1], 1))
    beside = [to_x(piece) for piece in ring]
    cot_there = to_core(cotangent)

    low_t = jnp.transpose(master.astype(bf16), (1, 2, 0))
    halves = [
        jnp.concatenate(
            [
                low_t[4 + 2 * h : 6 + 2 * h].reshape(2 * cols, rows),
                low_t[8 + 2 * h : 10 + 2 * h].reshape(2 * cols, rows),
                low_t[3, h * HALF : (h + 1) * HALF],
                low_t[0:3, h * HALF : (h + 1) * HALF].reshape(3 * HALF, rows),
            ],
            axis=0,
        )
        for h in range(2)
    ]
    own, other = by_core(*halves)
    there = to_core(other)
    both = jnp.concatenate(by_core(own, there), axis=1)
    far = [both[:432]]
    near = both[432:]
    near = [near, to_x(near)]
    near = jnp.stack([near[0], to_y(near[0]), near[1], to_y(near[1])])
    near_there = to_core(near)
    near = jnp.stack([near, near_there], axis=1).reshape(8, 3 * HALF, 2 * rows)
    w_qkv = place_qkv(None, x_place, y_place, core, near)

    for _ in range(3):
        far.append(hop_quarter(far[-1], 1))
    far_x = [to_x(piece) for piece in far]
    far_y = [to_y(piece) for piece in far]
    far_xy = [to_y(piece) for piece in far_x]
    w_mlp = [(far[k], far_x[k], far_y[k], far_xy[k]) for k in range(4)]
    out_own = jnp.stack([p[384:] for k in range(4) for p in (far[k], far_y[k], far_x[k], far_xy[k])])
    w_out = place_out(at, out_own, to_core(out_own))

    got = [project(ring[k], beside[k], w_qkv, norm_params) for k in range(4)]
    acts, normals, qs, ks, vs = zip(*got)
    inputs_seen = input_views[0]
    views = jnp.stack([gray((place - k) & 3) * 2 * tokens // VIEW for k in range(4)])
    seen = (views[None, :] < inputs_seen) | (views[None, :] == views[:, None])
    seen = seen.astype(jnp.int32).reshape(16)
    mixed, full, qs_back = attend(seen, qs, ks, vs)
    mixed = [mixed[0]] + [hop_quarter(mixed[4 - k], k) for k in (3, 2, 1)]

    two, resid, normal_two, inverse_two, act_three = out_norm(at, patches, mixed, w_out, norm_params)

    acts3 = (act_three, to_core(act_three))
    cots = (cotangent, cot_there)
    first = mlp(at, acts3, cots, [w_mlp[1], w_mlp[2]], (), False)
    second = mlp(at, acts3, cots, [w_mlp[3], w_mlp[0]], first[0:2], True)
    out_mine, three_mine = second[0:2]
    out_send, three_send = second[6:8]
    keep = {1: first[2], 2: first[3], 3: second[2], 0: second[3]}
    send = {1: first[4], 2: first[5], 3: second[4], 0: second[5]}
    block_out = (resid + out_mine + to_core(out_send).astype(f32)).astype(bf16)

    grad_resid, sums_two, parts, w_out_keep, w_out_send = norm_out_back(
        at, three_mine, to_core(three_send), cotangent, normal_two, inverse_two, two, w_out, norm_params
    )
    grads = [parts[0]] + [hop_quarter(parts[k], k) for k in (1, 2, 3)]
    dqs, dks, dvs = attend_back(seen, qs_back, ks, vs, full, grads)
    one_keep, one_send, near_keep, near_send, sums_one = project_back(at, acts, normals, dqs, dks, dvs, w_qkv)

    one = [add_low(one_keep[k], to_x(one_send[k])) for k in range(4)]
    grad_one = reduce_ring(one)
    normal_one, inverse_one = layer_stats(patches.astype(f32))
    patches_grad = grad_resid + layer_back(grad_one, normal_one, inverse_one, norm_params[0])
    param_grad = total(jnp.concatenate([sums_one[0:2], sums_two[0:2]], axis=0))

    def own_y(value):
        return lax.dynamic_slice_in_dim(value, y_place * 384, 384, value.ndim - 1)

    def other_y(value):
        return lax.dynamic_slice_in_dim(value, (1 - y_place) * 384, 384, value.ndim - 1)

    out_sum = add_low(w_out_keep, to_core(w_out_send))
    out_sum = add_low(own_y(out_sum), to_y(other_y(out_sum)))
    slots = []
    for k in range(4):
        pair = add_low(keep[k], to_y(send[k]))
        stay = jnp.concatenate([pair[0], out_sum[2 * k]], axis=0)
        leave = jnp.concatenate([pair[1], out_sum[2 * k + 1]], axis=0)
        slots.append(add_low(stay, to_x(leave)))
    far_sum = reduce_ring(slots)

    near_sum = add_low(near_keep, to_core(near_send))
    near_sum = add_low(own_y(near_sum), to_y(other_y(near_sum)))
    near_sum = near_sum[0:3].astype(f32) + to_x(near_sum[3:6]).astype(f32)

    grads_t = jnp.concatenate([far_sum, near_sum.reshape(3 * HALF, 2 * rows)], axis=0)
    squares = jnp.sum(grads_t * grads_t)
    squares = total(jnp.full((8, 128), squares, f32))[0, 0] + jnp.sum(param_grad * param_grad)
    grad_norm = jnp.sqrt(squares)
    clip = 1.0 / jnp.maximum(grad_norm, 1.0)
    own, other = by_core(grads_t[:, :rows], grads_t[:, rows:])
    there = to_core(other.astype(bf16)).astype(f32)
    first, second = by_core(own, there)

    def blocks_of(half):
        up = half[0:192].reshape(2, cols, rows)
        down = half[192:384].reshape(2, cols, rows)
        return up, down, half[384:432], half[432:].reshape(3, HALF, rows)

    up0, down0, out0, near0 = blocks_of(first)
    up1, down1, out1, near1 = blocks_of(second)
    weight_grad = jnp.concatenate(
        [
            jnp.concatenate([near0, near1], axis=1),
            jnp.concatenate([out0, out1], axis=0)[None],
            up0,
            up1,
            down0,
            down1,
        ],
        axis=0,
    )
    weight_grad = jnp.transpose(weight_grad, (2, 0, 1))
    new_master, new_moment_one, new_moment_two = adam_step(
        master, weight_grad * clip, moment_one, moment_two, rate_matrix, weight_decay
    )
    new_norm_params, new_norm_moment_one, new_norm_moment_two = adam_step(
        norm_params, param_grad * clip, norm_moment_one, norm_moment_two, rate_vector, 0.0
    )
    return (
        block_out,
        patches_grad,
        new_master,
        new_master.astype(bf16),
        new_moment_one,
        new_moment_two,
        new_norm_params,
        new_norm_moment_one,
        new_norm_moment_two,
        grad_norm,
    )


def solution(mesh):
    tokens = P(("dp", "seq"), None)
    weights = P("dp", None, "seq")
    small = mesh.shape["dp"] == 4 and mesh.shape["seq"] == 8
    return jax.shard_map(
        step_small if small else step_general,
        mesh=mesh,
        in_specs=(tokens, tokens, P("dp"), P(("dp", "seq")), weights, weights, weights, P(), P(), P()),
        out_specs=(tokens, tokens, weights, weights, weights, weights, P(), P(), P(), P()),
        check_vma=False,
    )
```

```python
import math
from functools import partial

import jax
import jax.numpy as jnp
from jax import lax
from jax.experimental import pallas as pl
from jax.experimental.pallas import tpu as pltpu
from jax.sharding import PartitionSpec as P

D = 768
HEADS = 12
HEAD_DIM = 64
FF = 3072
VIEW = 1024
STEP = 10
GROUPS = 4
GROUP_HEADS = HEADS // GROUPS
GROUP_WIDTH = GROUP_HEADS * HEAD_DIM
WIDE = FF // D
RING = (0, 1, 3, 2)

layer_eps = 1e-05
beta_first = 0.9
beta_second = 0.95
adam_eps = 1e-08
rate_matrix = 0.08
rate_vector = 0.8
weight_decay = 0.1
masked_score = -1e30
bf16 = jnp.bfloat16
f32 = jnp.float32


def gray(v):
    return v ^ (v >> 1)


def hop_quarter(value, by):
    split = lax.axis_size("seq") // GROUPS
    pairs = [
        (RING[p] * split + x, RING[(p + by) % GROUPS] * split + x) for p in range(GROUPS) for x in range(split)
    ]
    return lax.ppermute(value, "seq", pairs)


def hop_within(value, by):
    split = lax.axis_size("seq") // GROUPS
    pairs = [(q * split + x, q * split + (x + by) % split) for q in range(GROUPS) for x in range(split)]
    return lax.ppermute(value, "seq", pairs)


def swap(value, axis, bit):
    return lax.ppermute(value, axis, [(i, i ^ bit) for i in range(lax.axis_size(axis))])


def bits_of(axis):
    return [1 << b for b in range(lax.axis_size(axis).bit_length() - 1)]


def total(value):
    for axis in ("dp", "seq"):
        for bit in bits_of(axis):
            value = value + swap(value, axis, bit)
    return value


def pick(stack, index):
    return lax.dynamic_index_in_dim(stack, index, 0, keepdims=False)


def layer_stats(values):
    centre = jnp.mean(values, axis=-1, keepdims=True)
    shifted = values - centre
    spread = jnp.mean(shifted * shifted, axis=-1, keepdims=True)
    inverse = lax.rsqrt(spread + layer_eps)
    return (shifted * inverse, inverse)


def layer_back(grad_normed, normalized, inverse, gain):
    scaled = grad_normed * gain
    centred = jnp.mean(scaled, axis=-1, keepdims=True)
    along = jnp.mean(scaled * normalized, axis=-1, keepdims=True)
    return inverse * (scaled - centred - normalized * along)


def mm(a, b):
    return jnp.dot(a, b, preferred_element_type=f32)


def mm_nt(a, b):
    return lax.dot_general(a, b, (((1,), (1,)), ((), ())), preferred_element_type=f32)


def mm_tn(a, b):
    return lax.dot_general(a, b, (((0,), (0,)), ((), ())), preferred_element_type=f32)


def gather_rows(piece):
    for bit in reversed(bits_of("dp")):
        piece = jnp.concatenate([piece, swap(piece, "dp", bit)], axis=1)
    return piece


def row_order():
    order = [0]
    for bit in reversed(bits_of("dp")):
        order = order + [o ^ bit for o in order]
    return order


def reduce_rows(piece):
    for bit in bits_of("dp"):
        half = piece.shape[1] // 2
        there = swap(piece[:, half:], "dp", bit)
        piece = (piece[:, :half].astype(f32) + there.astype(f32)).astype(bf16)
    return piece


def reduce_within(piece):
    own = piece[0].astype(f32)
    for j in range(1, piece.shape[0]):
        own = own + hop_within(piece[j], -j).astype(f32)
    return own.astype(bf16)


def reduce_ring(slots):
    moving = slots[1]
    for k in (2, 3):
        moving = (hop_quarter(moving, 1).astype(f32) + slots[k].astype(f32)).astype(bf16)
    return hop_quarter(moving, 1).astype(f32) + slots[0].astype(f32)


def adam_step(params, grads, first, second, rate, decay):
    first_new = beta_first * first + (1.0 - beta_first) * grads
    second_new = beta_second * second + (1.0 - beta_second) * grads * grads
    first_hat = first_new / (1.0 - beta_first**STEP)
    second_hat = second_new / (1.0 - beta_second**STEP)
    params_new = params - rate * (first_hat / (jnp.sqrt(second_hat) + adam_eps) + decay * params)
    return (params_new, first_new, second_new)


def relative(dp, absolute, order):
    index = jnp.int32(0)
    for at, offset in enumerate(order):
        index = jnp.where((dp ^ absolute) == offset, at, index)
    return index


def step_general(
    patches,
    cotangent,
    input_views,
    token_live,
    master,
    moment_one,
    moment_two,
    norm_params,
    norm_moment_one,
    norm_moment_two,
):
    tokens = patches.shape[0]
    rows, blocks, cols = master.shape
    n_dp = lax.axis_size("dp")
    split = lax.axis_size("seq") // GROUPS
    dp = lax.axis_index("dp")
    seq = lax.axis_index("seq")
    quarter, within = seq // split, seq % split
    place = gray(quarter)
    inputs_seen = input_views[0]
    gain_one, shift_one, gain_two, shift_two = (norm_params[i] for i in range(4))
    order = row_order()
    dp_place = [order.index(a) for a in range(n_dp)]

    def quarter_behind(k):
        return gray((place - k) & 3)

    flags = jnp.pad(token_live.astype(bf16)[None, :], ((0, 7), (0, D - tokens)))
    ring = [jnp.concatenate([patches, flags], axis=0)]
    for _ in range(3):
        ring.append(hop_quarter(ring[-1], 1))
    pieces = [[ring[k]] + [hop_within(ring[k], j) for j in range(1, split)] for k in range(4)]
    scene = jnp.stack([jnp.stack([p[:tokens] for p in pieces[k]]) for k in range(4)])
    live = jnp.stack([jnp.concatenate([p[tokens, :tokens] for p in pieces[k]]) for k in range(4)])

    copy_low = master.astype(bf16)
    mine = copy_low[:, 0:3, :].reshape(rows, 3 * cols)
    near = jnp.stack([mine] + [hop_within(mine, j) for j in range(1, split)])
    near = gather_rows(near).reshape(split, n_dp, rows, 3, cols)
    near = jnp.stack([pick(near, (within - a) % split) for a in range(split)])
    near = jnp.moveaxis(near, 1, 0)
    near = jnp.stack([pick(near, order_at) for order_at in [relative(dp, a, order) for a in range(n_dp)]])
    w_qkv = jnp.transpose(near, (0, 2, 3, 1, 4)).reshape(D, 3, GROUP_WIDTH)

    up = copy_low[:, 4 : 4 + WIDE].reshape(rows, WIDE * cols)
    down = copy_low[:, 4 + WIDE :].reshape(rows, WIDE * cols)
    far = [jnp.concatenate([up, down, copy_low[:, 3]], axis=1)]
    for _ in range(3):
        far.append(hop_quarter(far[-1], 1))
    weights = [gather_rows(jnp.stack([f] + [hop_within(f, j) for j in range(1, split)])) for f in far]
    width = WIDE * cols
    w_up = [w[:, :, :width] for w in weights]
    w_down = [w[:, :, width : 2 * width] for w in weights]
    w_out = jnp.stack([w[:, :, 2 * width :] for w in weights]).reshape(4 * split, n_dp, rows, cols)

    def slot_of(quarter_abs, within_abs):
        return ((place - gray(quarter_abs)) & 3) * split + (within - within_abs) % split

    w_out = jnp.stack([pick(w_out, slot_of(a // split, a % split)) for a in range(4 * split)])
    w_out = jnp.moveaxis(w_out, 1, 0)
    w_out = jnp.stack([pick(w_out, relative(dp, a, order)) for a in range(n_dp)])
    w_out = jnp.transpose(w_out, (0, 2, 1, 3)).reshape(D, D)

    normal_one, inverse_one = layer_stats(scene.astype(f32))
    act_one = (normal_one * gain_one + shift_one).astype(bf16)
    act_all = act_one.reshape(4 * split * tokens, D)
    act_own = act_one[:, 0].reshape(4 * tokens, D)
    q = mm(act_own, w_qkv[:, 0]).astype(bf16)
    k = mm(act_all, w_qkv[:, 1]).astype(bf16)
    v = mm(act_all, w_qkv[:, 2]).astype(bf16)

    def heads(m):
        return jnp.transpose(m.reshape(m.shape[0], GROUP_HEADS, HEAD_DIM), (1, 0, 2))

    def unheads(m):
        return jnp.transpose(m, (1, 0, 2)).reshape(m.shape[1], GROUP_WIDTH)

    views = jnp.stack([(quarter_behind(i) * split * tokens) // VIEW for i in range(4)])
    open_block = (views[None, :] < inputs_seen) | (views[None, :] == views[:, None])
    visible = open_block[:, None, :, None] & (live > 0)[None, None]
    visible = jnp.broadcast_to(visible, (4, tokens, 4, split * tokens)).reshape(4 * tokens, -1)
    scaling = 1.0 / math.sqrt(HEAD_DIM)
    qh, kh, vh = heads(q), heads(k), heads(v)
    scores = jnp.einsum("hqd,hkd->hqk", qh, kh, preferred_element_type=f32) * scaling
    scores = jnp.where(visible[None], scores, masked_score)
    top = jnp.max(scores, axis=-1, keepdims=True)
    probs = jnp.where(visible[None], jnp.exp(scores - top), 0.0)
    probs = probs / jnp.sum(probs, axis=-1, keepdims=True)
    probs_low = probs.astype(bf16)
    attended = jnp.einsum("hqk,hkd->hqd", probs_low, vh, preferred_element_type=f32)
    flat = unheads(attended).astype(bf16).reshape(4, tokens, GROUP_WIDTH)
    back = jnp.stack([flat[0]] + [hop_quarter(flat[i], -i) for i in range(1, 4)])
    act_two = jnp.concatenate([pick(back, (gray(a) - place) & 3) for a in range(4)], axis=1)

    patch_float = patches.astype(f32)
    resid = patch_float + mm(act_two, w_out)
    normal_two, inverse_two = layer_stats(resid)
    act_three = (normal_two * gain_two + shift_two).astype(bf16)

    def to_relative(m):
        parts = m.reshape(tokens, n_dp, rows)
        return jnp.concatenate([lax.dynamic_index_in_dim(parts, dp ^ o, 1, keepdims=False) for o in order], axis=1)

    def from_relative(m):
        parts = m.reshape(tokens, n_dp, rows)
        return jnp.concatenate(
            [lax.dynamic_index_in_dim(parts, relative(dp, a, order), 1, keepdims=False) for a in range(n_dp)], axis=1
        )

    act_rel = to_relative(act_three)
    cot_rel = to_relative(cotangent)
    branch_rel = jnp.zeros((tokens, D), f32)
    three_rel = jnp.zeros((tokens, D), f32)
    far_grads = []
    for i in range(4):
        group = []
        for j in range(split):
            widened = mm(act_rel, w_up[i][j])
            activated, gelu_pull = jax.vjp(partial(jax.nn.gelu, approximate=False), widened)
            hidden = activated.astype(bf16)
            branch_rel = branch_rel + mm_nt(hidden, w_down[i][j])
            grad_wide = gelu_pull(mm(cot_rel, w_down[i][j]))[0].astype(bf16)
            three_rel = three_rel + mm_nt(grad_wide, w_up[i][j])
            grad_up = mm_tn(act_rel, grad_wide).astype(bf16)
            grad_down = mm_tn(cot_rel, hidden).astype(bf16)
            group.append((grad_up, grad_down))
        far_grads.append(group)
    block_out = (resid + from_relative(branch_rel)).astype(bf16)
    grad_three = from_relative(three_rel)
    gain_two_grad = jnp.sum(grad_three * normal_two, axis=0)
    shift_two_grad = jnp.sum(grad_three, axis=0)
    grad_resid = cotangent.astype(f32) + layer_back(grad_three, normal_two, inverse_two, gain_two)
    grad_branch = grad_resid.astype(bf16)
    grad_attended = mm_nt(grad_branch, w_out).astype(bf16)
    grad_w_out = mm_tn(act_two, grad_branch).astype(bf16)

    parts = jnp.transpose(grad_attended.reshape(tokens, 4, GROUP_WIDTH), (1, 0, 2))
    parts = [pick(parts, gray((place + i) & 3)) for i in range(4)]
    grad_here = jnp.concatenate([parts[0]] + [hop_quarter(parts[i], i) for i in range(1, 4)], axis=0)
    gh = heads(grad_here)
    dprobs = jnp.einsum("hqd,hkd->hqk", gh, vh, preferred_element_type=f32)
    delta = jnp.sum(gh.astype(f32) * attended, axis=-1, keepdims=True)
    grad_scores = (probs * (dprobs - delta)).astype(bf16)
    dq = unheads(jnp.einsum("hqk,hkd->hqd", grad_scores, kh, preferred_element_type=f32) * scaling).astype(bf16)
    dk = unheads(jnp.einsum("hqk,hqd->hkd", grad_scores, qh, preferred_element_type=f32) * scaling).astype(bf16)
    dv = unheads(jnp.einsum("hqk,hqd->hkd", probs_low, gh, preferred_element_type=f32)).astype(bf16)

    grad_near = jnp.stack([mm_tn(act_own, dq), mm_tn(act_all, dk), mm_tn(act_all, dv)], axis=1).astype(bf16)
    grad_near = grad_near.reshape(n_dp, rows, 3, split, cols)
    grad_near = jnp.stack([pick(grad_near, dp ^ o) for o in order])
    grad_near = jnp.transpose(grad_near, (3, 0, 1, 2, 4)).reshape(split, D, 3 * cols)
    grad_near = jnp.stack([pick(grad_near, (within - j) % split) for j in range(split)])
    grad_near = reduce_within(reduce_rows(grad_near)).astype(f32).reshape(rows, 3, cols)

    one_q = mm_nt(dq, w_qkv[:, 0]).reshape(4, 1, tokens, D)
    one_kv = (mm_nt(dk, w_qkv[:, 1]) + mm_nt(dv, w_qkv[:, 2])).reshape(4, split, tokens, D)
    one = jnp.concatenate([one_kv[:, :1] + one_q, one_kv[:, 1:]], axis=1)
    gain_one_grad = jnp.sum(one * normal_one, axis=(0, 1, 2))
    shift_one_grad = jnp.sum(one, axis=(0, 1, 2))
    one_low = one.astype(bf16)
    grad_one = reduce_ring([reduce_within(one_low[i]) for i in range(4)])
    patches_grad = grad_resid + layer_back(grad_one, normal_one[0, 0], inverse_one[0, 0], gain_one)

    out_parts = grad_w_out.reshape(n_dp, rows, 4 * split, cols)
    out_parts = jnp.stack([pick(out_parts, dp ^ o) for o in order])
    out_parts = jnp.transpose(out_parts, (2, 0, 1, 3)).reshape(4 * split, D, cols)
    slots = []
    for i in range(4):
        stack = []
        for j in range(split):
            own_out = pick(out_parts, quarter_behind(i) * split + (within - j) % split)
            stack.append(jnp.concatenate([*far_grads[i][j], own_out], axis=1))
        slots.append(reduce_within(reduce_rows(jnp.stack(stack))))
    far_sum = reduce_ring(slots)
    grad_up = far_sum[:, :width].reshape(rows, WIDE, cols)
    grad_down = far_sum[:, width : 2 * width].reshape(rows, WIDE, cols)
    grad_out = far_sum[:, 2 * width :].reshape(rows, 1, cols)

    weight_grad = jnp.concatenate([grad_near, grad_out, grad_up, grad_down], axis=1)
    param_grad = total(jnp.stack([gain_one_grad, shift_one_grad, gain_two_grad, shift_two_grad]))
    squares = total(jnp.full((8, 128), jnp.sum(weight_grad * weight_grad), f32))[0, 0] + jnp.sum(param_grad * param_grad)
    grad_norm = jnp.sqrt(squares)
    clip = 1.0 / jnp.maximum(grad_norm, 1.0)
    new_master, new_moment_one, new_moment_two = adam_step(
        master, weight_grad * clip, moment_one, moment_two, rate_matrix, weight_decay
    )
    new_norm_params, new_norm_moment_one, new_norm_moment_two = adam_step(
        norm_params, param_grad * clip, norm_moment_one, norm_moment_two, rate_vector, 0.0
    )
    return (
        block_out,
        patches_grad,
        new_master,
        new_master.astype(bf16),
        new_moment_one,
        new_moment_two,
        new_norm_params,
        new_norm_moment_one,
        new_norm_moment_two,
        grad_norm,
    )


HALF = 48
ANY = pl.BlockSpec(memory_space=pl.ANY)
SMEM = pl.BlockSpec(memory_space=pltpu.SMEM)
VMEM_LIMIT = 56 << 20


def call(body, name, ins, outs, operands, scratch=(), us=4):
    return pl.pallas_call(
        body,
        name=name,
        out_shape=outs,
        in_specs=ins,
        out_specs=jax.tree.map(lambda _: pl.BlockSpec(memory_space=pltpu.VMEM), outs),
        scratch_shapes=list(scratch),
        cost_estimate=pl.CostEstimate(flops=us * 10**9, bytes_accessed=us * 3_600_000, transcendentals=0),
        compiler_params=pltpu.CompilerParams(vmem_limit_bytes=VMEM_LIMIT),
    )(*operands)


VM = pl.BlockSpec(memory_space=pltpu.VMEM)


def shape(dims, dtype):
    return jax.ShapeDtypeStruct(dims, dtype)


def run_copies(copies):
    for c in copies:
        c.start()
    for c in copies:
        c.wait()


def place_qkv(at, own_half, other_half):
    def body(at_ref, own_ref, other_ref, out_ref, sems):
        x, y, c = at_ref[0], at_ref[1], at_ref[2]
        copies = []
        for block in range(3):
            for j in range(2):
                for r in range(2):
                    for h, ref in ((0, own_ref), (1, other_ref)):
                        row = block * GROUP_WIDTH + (x ^ j) * 96 + (c ^ h) * HALF
                        copies.append(
                            pltpu.make_async_copy(
                                ref.at[r, j, pl.ds(block * HALF, HALF), :],
                                out_ref.at[
                                    pl.ds(pl.multiple_of(row, 16), HALF),
                                    pl.ds(pl.multiple_of((y ^ r) * 384, 128), 384),
                                ],
                                sems.at[len(copies)],
                            )
                        )
        run_copies(copies)

    return call(
        body,
        "place_qkv",
        [SMEM, ANY, ANY],
        shape((3 * GROUP_WIDTH, D), bf16),
        (at, own_half, other_half),
        [pltpu.SemaphoreType.DMA((24,))],
    )


def place_out(at, own_half, other_half):
    def body(at_ref, own_ref, other_ref, out_ref, sems):
        x, y, c, place = at_ref[0], at_ref[1], at_ref[2], at_ref[3]
        copies = []
        for k in range(4):
            quarter = gray((place - k) & 3)
            for j in range(2):
                for r in range(2):
                    for h, ref in ((0, own_ref), (1, other_ref)):
                        row = (quarter * 2 + (x ^ j)) * 96 + (c ^ h) * HALF
                        copies.append(
                            pltpu.make_async_copy(
                                ref.at[(k * 2 + j) * 2 + r],
                                out_ref.at[
                                    pl.ds(pl.multiple_of(row, 16), HALF),
                                    pl.ds(pl.multiple_of((y ^ r) * 384, 128), 384),
                                ],
                                sems.at[len(copies)],
                            )
                        )
        run_copies(copies)

    return call(
        body,
        "place_out",
        [SMEM, ANY, ANY],
        shape((D, D), bf16),
        (at, own_half, other_half),
        [pltpu.SemaphoreType.DMA((32,))],
    )


def normalize(values):
    centre = jnp.mean(values, axis=-1, keepdims=True)
    shifted = values - centre
    inverse = lax.rsqrt(jnp.mean(shifted * shifted, axis=-1, keepdims=True) + layer_eps)
    return shifted * inverse, inverse


def lane_index(dims):
    return lax.broadcasted_iota(jnp.int32, dims, len(dims) - 1)


def project(first, second, w_t, norms):
    def body(a_ref, b_ref, w_ref, norm_ref, act_ref, normal_ref, q_ref, k_ref, v_ref, wide_ref):
        wide_ref[...] = jnp.zeros_like(wide_ref)
        for h in range(9):
            wide_ref[h * 128 : h * 128 + 64, :] = w_ref[h * 64 : h * 64 + 64, :]
        gain, shift = norm_ref[0:1, :], norm_ref[1:2, :]
        for piece, ref in enumerate((a_ref, b_ref)):
            at = slice(piece * 256, piece * 256 + 256)
            normal, _ = normalize(ref[0:256, :].astype(f32))
            act = (normal * gain + shift).astype(bf16)
            normal_ref[at, :] = normal.astype(bf16)
            act_ref[at, :] = act
            flags = ref[256:257, 0:256].astype(f32)
            mask = jnp.where(flags > 0, 0.0, masked_score)
            mask = jnp.transpose(jnp.broadcast_to(mask, (128, 256)))
            lanes = lane_index((256, 128))
            for h in range(3):
                if piece == 0:
                    q = mm_nt(act, wide_ref[h * 128 : h * 128 + 128, :]).astype(bf16).astype(f32)
                    q = jnp.where(lanes == 64, 1.0, q * (1.0 / math.sqrt(HEAD_DIM)))
                    q_ref[h] = q.astype(bf16)
                k = mm_nt(act, wide_ref[(3 + h) * 128 : (4 + h) * 128, :])
                k = jnp.where(lanes == 64, mask, k)
                k_ref[h, at, :] = jnp.where((lanes > 64) & (lanes < 68), 1.0, k).astype(bf16)
                v = mm_nt(act, wide_ref[(6 + h) * 128 : (7 + h) * 128, :])
                v_ref[h, at, :] = jnp.where((lanes > 63) & (lanes < 67), 1.0, v).astype(bf16)

    outs = [
        shape((512, D), bf16),
        shape((512, D), bf16),
        shape((3, 256, 128), bf16),
        shape((3, 512, 128), bf16),
        shape((3, 512, 128), bf16),
    ]
    return call(body, "norm_project", [VM] * 4, outs, (first, second, w_t, norms), [pltpu.VMEM((1152, D), bf16)], us=4)


def in_three(value):
    high = value.astype(bf16).astype(f32)
    rest = value - high
    mid = rest.astype(bf16).astype(f32)
    return high, mid, rest - mid


def with_parts(base, lanes, first, value):
    for i, part in enumerate(in_three(value)):
        base = jnp.where(lanes == first + i, part, base)
    return base


def join_heads(parts):
    return jnp.concatenate([p[:, :HEAD_DIM] for p in parts], axis=1)


def stack_slots(place, slots, stacked, sems, base=0):
    return [
        pltpu.make_async_copy(ref, stacked.at[gray((place - k) & 3)], sems.at[base + k]) for k, ref in enumerate(slots)
    ]


def attend(at, qs, ks, vs):
    def body(at_ref, *refs):
        low_refs, full_ref, back_ref = refs[12:16], refs[16], refs[17]
        q_ref, k_ref, v_ref, sems = refs[18:22]
        place = at_ref[3]
        lanes = lane_index((256, 128))
        run_copies(
            stack_slots(place, refs[0:4], q_ref, sems)
            + stack_slots(place, refs[4:8], k_ref, sems, 4)
            + stack_slots(place, refs[8:12], v_ref, sems, 8)
        )

        def head(h, _):
            for i in range(4):
                chunks = (0, 1) if i < 2 else (0, 1, 2, 3)
                q = q_ref[i, h]
                scores = [mm_nt(q, k_ref[c, h]) for c in chunks]
                top = None
                for s in scores:
                    for b in range(0, s.shape[1], 128):
                        part = s[:, b : b + 128]
                        top = part if top is None else jnp.maximum(top, part)
                top = jnp.max(top, axis=1, keepdims=True)
                mixed = None
                for s, c in zip(scores, chunks):
                    part = mm(jnp.exp(s - top).astype(bf16), v_ref[c, h])
                    mixed = part if mixed is None else mixed + part
                norm = mixed[:, HEAD_DIM : HEAD_DIM + 1]
                full_ref[i, h] = mixed / norm
                logsum = top + jnp.log(norm)
                back_ref[i, h] = with_parts(q.astype(f32), lanes, 65, -logsum).astype(bf16)
            return 0

        lax.fori_loop(0, 3, head, 0)
        for k in range(4):
            i = gray((place - k) & 3)
            low_refs[k][...] = join_heads([full_ref[i, h] for h in range(3)]).astype(bf16)

    outs = (
        [shape((256, GROUP_WIDTH), bf16)] * 4 + [shape((4, 3, 256, 128), f32)] + [shape((4, 3, 256, 128), bf16)]
    )
    got = call(
        body,
        "attend",
        [SMEM] + [ANY] * 12,
        outs,
        (at, *qs, *ks, *vs),
        [
            pltpu.VMEM((4, 3, 256, 128), bf16),
            pltpu.VMEM((4, 3, 512, 128), bf16),
            pltpu.VMEM((4, 3, 512, 128), bf16),
            pltpu.SemaphoreType.DMA((12,)),
        ],
        us=12,
    )
    return got[0:4], got[4], got[5]


def attend_back(at, q_back, ks, vs, full, grads):
    def body(at_ref, q_ref, *refs):
        full_ref, g_refs = refs[8], refs[9:13]
        dq_refs, dk_refs, dv_refs = refs[13:17], refs[17:21], refs[21:25]
        k_ref, v_ref, g_ref, dq_ref, dk_ref, dv_ref, sems = refs[25:32]
        place = at_ref[3]
        copies = stack_slots(place, refs[0:4], k_ref, sems) + stack_slots(place, refs[4:8], v_ref, sems, 4)
        for c in copies:
            c.start()
        lanes = lane_index((256, 128))
        for k in range(4):
            i = gray((place - k) & 3)
            for h in range(3):
                g = g_refs[k][:, h * 64 : h * 64 + 64].astype(f32)
                delta = jnp.sum(g * full_ref[i, h][:, :64], axis=-1, keepdims=True)
                g = jnp.concatenate([g, jnp.zeros((256, 64), f32)], axis=1)
                g_ref[h, pl.ds(pl.multiple_of(i * 256, 256), 256), :] = with_parts(g, lanes, 64, -delta).astype(bf16)
        for c in copies:
            c.wait()

        def head(h, _):
            q_all = jnp.concatenate([q_ref[i, h] for i in range(4)], axis=0)
            for c in range(4):
                first = 0 if c < 2 else 512
                k, v = k_ref[c, h], v_ref[c, h]
                q, g = q_all[first:], g_ref[h, first:, :]
                p = jnp.exp(mm_nt(k, q))
                ds = (p * mm_nt(v, g)).astype(bf16)
                dv_ref[c, h] = mm(p.astype(bf16), g)
                dk_ref[c, h] = mm(ds, q)
                dq = mm(jnp.transpose(k), ds)
                if c == 0:
                    dq_ref[h] = dq
                else:
                    dq_ref[h, :, first:] += dq
            return 0

        lax.fori_loop(0, 3, head, 0)
        for k in range(4):
            i = gray((place - k) & 3)
            cols = pl.ds(pl.multiple_of(i * 256, 256), 256)
            parts = [jnp.transpose(dq_ref[h, :, cols]) for h in range(3)]
            dq_refs[k][...] = (join_heads(parts) * (1.0 / math.sqrt(HEAD_DIM))).astype(bf16)
            dk_refs[k][...] = join_heads([dk_ref[i, h] for h in range(3)]).astype(bf16)
            dv_refs[k][...] = join_heads([dv_ref[i, h] for h in range(3)]).astype(bf16)

    outs = [shape((256, GROUP_WIDTH), bf16)] * 4 + [shape((512, GROUP_WIDTH), bf16)] * 8
    got = call(
        body,
        "attend_back",
        [SMEM, VM] + [ANY] * 8 + [VM] * 5,
        outs,
        (at, q_back, *ks, *vs, full, *grads),
        [
            pltpu.VMEM((4, 3, 512, 128), bf16),
            pltpu.VMEM((4, 3, 512, 128), bf16),
            pltpu.VMEM((3, 1024, 128), bf16),
            pltpu.VMEM((3, 128, 1024), f32),
            pltpu.VMEM((4, 3, 512, 128), f32),
            pltpu.VMEM((4, 3, 512, 128), f32),
            pltpu.SemaphoreType.DMA((8,)),
        ],
        us=16,
    )
    return got[0:4], got[4:8], got[8:12]


def project_back(at, acts, normals, dqs, dks, dvs, w_t):
    def body(at_ref, *refs):
        act_refs, normal_refs, dq_refs, dk_refs, dv_refs, w_ref = (
            refs[0:4],
            refs[4:8],
            refs[8:12],
            refs[12:16],
            refs[16:20],
            refs[20],
        )
        keep_refs, send_refs, w_keep_ref, w_send_ref, norm_ref, dw_ref = refs[21:25], refs[25:29], *refs[29:33]
        gains, shifts = jnp.zeros((1, D), f32), jnp.zeros((1, D), f32)
        for i in range(4):
            act = act_refs[i][...]
            for b, (ref, rows) in enumerate(((dq_refs[i], 256), (dk_refs[i], 512), (dv_refs[i], 512))):
                part = mm_tn(ref[...], act[:rows])
                at_rows = slice(b * GROUP_WIDTH, (b + 1) * GROUP_WIDTH)
                dw_ref[at_rows, :] = part if i == 0 else dw_ref[at_rows, :] + part
            for j, out_ref in enumerate((keep_refs[i], send_refs[i])):
                r = slice(j * 256, j * 256 + 256)
                one = mm(dk_refs[i][r, :], w_ref[192:384, :]) + mm(dv_refs[i][r, :], w_ref[384:576, :])
                if j == 0:
                    one = one + mm(dq_refs[i][...], w_ref[0:192, :])
                gains = gains + jnp.sum(one * normal_refs[i][r, :].astype(f32), axis=0, keepdims=True)
                shifts = shifts + jnp.sum(one, axis=0, keepdims=True)
                out_ref[...] = one.astype(bf16)
        norm_ref[...] = jnp.concatenate([gains, shifts, jnp.zeros((6, D), f32)], axis=0)
        x, c = at_ref[0], at_ref[2]
        for b in range(3):
            for xa in range(2):
                for half in range(2):
                    row = b * GROUP_WIDTH + (xa * 2 + half) * HALF
                    block = dw_ref[row : row + HALF, :].astype(bf16)

                    @pl.when(c == half)
                    def _():
                        w_keep_ref[(x ^ xa) * 3 + b] = block

                    @pl.when(c != half)
                    def _():
                        w_send_ref[(x ^ xa) * 3 + b] = block

    outs = (
        [shape((256, D), bf16)] * 8 + [shape((6, HALF, D), bf16)] * 2 + [shape((8, D), f32)]
    )
    got = call(
        body,
        "project_back",
        [SMEM] + [VM] * 21,
        outs,
        (at, *acts, *normals, *dqs, *dks, *dvs, w_t),
        [pltpu.VMEM((3 * GROUP_WIDTH, D), f32)],
        us=10,
    )
    return got[0:4], got[4:8], got[8], got[9], got[10]


def out_norm(at, patches, mixed, w_out, norms):
    def body(at_ref, x_ref, m0, m1, m2, m3, w_ref, norm_ref, two_ref, resid_ref, normal_ref, inverse_ref, three_ref):
        place = at_ref[3]
        parts = [m[...].astype(f32) for m in (m0, m1, m2, m3)]
        groups = []
        for a in range(4):
            steps = (gray(a) - place) & 3
            part = parts[0]
            for k in (1, 2, 3):
                part = jnp.where(steps == k, parts[k], part)
            groups.append(part)
        two = jnp.concatenate(groups, axis=1).astype(bf16)
        two_ref[...] = two
        resid = x_ref[...].astype(f32) + mm_nt(two, w_ref[...])
        resid_ref[...] = resid
        normal, inverse = normalize(resid)
        normal_ref[...] = normal
        inverse_ref[...] = jnp.broadcast_to(inverse, (256, 128))
        three_ref[...] = (normal * norm_ref[2:3, :] + norm_ref[3:4, :]).astype(bf16)

    outs = [
        shape((256, D), bf16),
        shape((256, D), f32),
        shape((256, D), f32),
        shape((256, 128), f32),
        shape((256, D), bf16),
    ]
    return call(body, "out_norm", [SMEM] + [VM] * 7, outs, (at, patches, *mixed, w_out, norms))


def mlp(at, acts, cots, weights, carried, last):
    count = len(weights)

    def body(at_ref, *refs):
        a_refs, c_refs = refs[0:2], refs[2:4]
        w_refs = refs[4 : 4 + 2 * count]
        at_in = 4 + 2 * count
        carried_refs = refs[at_in : at_in + len(carried)]
        outs = refs[at_in + len(carried) :]
        out_ref, three_ref = outs[0:2]
        keep_refs, send_refs = outs[2 : 2 + count], outs[2 + count : 2 + 2 * count]
        act_ref, cot_ref, w_ref, out_acc, three_acc, sems = outs[2 + 2 * count + (2 if last else 0) :]
        y = at_ref[1]
        own_lanes = pl.ds(pl.multiple_of(y * 384, 128), 384)
        other_lanes = pl.ds(pl.multiple_of((1 - y) * 384, 128), 384)
        copies = []
        for n in range(count):
            group = []
            for r, lanes in enumerate((own_lanes, other_lanes)):
                for j in range(2):
                    for u in range(2):
                        group.append(
                            pltpu.make_async_copy(
                                w_refs[2 * n + r].at[j, pl.ds(u * 192, 192), :],
                                w_ref.at[n, u, pl.ds(j * 192, 192), lanes],
                                sems.at[n, len(group)],
                            )
                        )
            copies.append(group)
            for c in group:
                c.start()
        for i in range(2):
            act_ref[i * 256 : i * 256 + 256, :] = a_refs[i][...]
            cot_ref[i * 256 : i * 256 + 256, :] = c_refs[i][...]
        for n in range(count):
            for c in copies[n]:
                c.wait()
            act, cot = act_ref[...], cot_ref[...]
            up, down = w_ref[n, 0], w_ref[n, 1]
            widened = mm_nt(act, up)
            inner = 0.5 * (1.0 + lax.erf(widened * (1.0 / math.sqrt(2.0))))
            slope = inner + widened * jnp.exp(-0.5 * widened * widened) * (1.0 / math.sqrt(2.0 * math.pi))
            hidden = (widened * inner).astype(bf16)
            grad_wide = (mm_nt(cot, down) * slope).astype(bf16)
            out = mm(hidden, down)
            three = mm(grad_wide, up)
            if n == 0 and not carried:
                out_acc[...] = out
                three_acc[...] = three
            elif n == 0:
                out_acc[...] = carried_refs[0][...] + out
                three_acc[...] = carried_refs[1][...] + three
            else:
                out_acc[...] += out
                three_acc[...] += three
            for lanes, ref in ((own_lanes, keep_refs[n]), (other_lanes, send_refs[n])):
                grad_up = mm_tn(grad_wide, act_ref[:, lanes]).astype(bf16)
                grad_down = mm_tn(hidden, cot_ref[:, lanes]).astype(bf16)
                for j in range(2):
                    ref[j, 0:192, :] = grad_up[j * 192 : j * 192 + 192]
                    ref[j, 192:384, :] = grad_down[j * 192 : j * 192 + 192]
        if last:
            out_ref[...] = out_acc[0:256, :]
            three_ref[...] = three_acc[0:256, :]
            outs[2 + 2 * count][...] = out_acc[256:512, :].astype(bf16)
            outs[3 + 2 * count][...] = three_acc[256:512, :].astype(bf16)
        else:
            out_ref[...] = out_acc[...]
            three_ref[...] = three_acc[...]

    rows = 256 if last else 512
    outs = [shape((rows, D), f32)] * 2 + [shape((2, 384, 384), bf16)] * (2 * count)
    if last:
        outs = outs + [shape((256, D), bf16)] * 2
    flat = [w for group in weights for w in group]
    return call(
        body,
        "mlp",
        [SMEM] + [VM] * 4 + [ANY] * len(flat) + [VM] * len(carried),
        outs,
        (at, *acts, *cots, *flat, *carried),
        [
            pltpu.VMEM((512, D), bf16),
            pltpu.VMEM((512, D), bf16),
            pltpu.VMEM((count, 2, 384, D), bf16),
            pltpu.VMEM((512, D), f32),
            pltpu.VMEM((512, D), f32),
            pltpu.SemaphoreType.DMA((count, 8)),
        ],
        us=10,
    )


def norm_out_back(at, three, three_there, cotangent, normal, inverse, two, w_out, norms):
    def body(at_ref, t_ref, s_ref, c_ref, n_ref, i_ref, two_ref, w_ref, norm_ref, *outs):
        resid_ref, sums_ref = outs[0:2]
        g_refs, keep_ref, send_ref, dw_ref = outs[2:6], outs[6], outs[7], outs[8]
        x, c, place = at_ref[0], at_ref[2], at_ref[3]
        grad = t_ref[...] + s_ref[...].astype(f32)
        normal = n_ref[...]
        sums_ref[...] = jnp.concatenate(
            [jnp.sum(grad * normal, axis=0, keepdims=True), jnp.sum(grad, axis=0, keepdims=True), jnp.zeros((6, D), f32)],
            axis=0,
        )
        resid = c_ref[...].astype(f32) + layer_back(grad, normal, i_ref[:, 0:1], norm_ref[2:3, :])
        resid_ref[...] = resid
        low = resid.astype(bf16)
        back = mm(low, w_ref[...])
        groups = [back[:, a * GROUP_WIDTH : (a + 1) * GROUP_WIDTH] for a in range(4)]
        for k in range(4):
            ahead = gray((place + k) & 3)
            part = groups[0]
            for a in (1, 2, 3):
                part = jnp.where(ahead == a, groups[a], part)
            g_refs[k][...] = part.astype(bf16)
        dw_ref[...] = mm_tn(low, two_ref[...])
        for q in range(4):
            for xa in range(2):
                slot = ((place - gray(q)) & 3) * 2 + (x ^ xa)
                for half in range(2):
                    row = (q * 2 + xa) * 96 + half * HALF
                    block = dw_ref[row : row + HALF, :].astype(bf16)

                    @pl.when(c == half)
                    def _():
                        keep_ref[slot] = block

                    @pl.when(c != half)
                    def _():
                        send_ref[slot] = block

    outs = (
        [shape((256, D), f32), shape((8, D), f32)]
        + [shape((256, GROUP_WIDTH), bf16)] * 4
        + [shape((8, HALF, D), bf16)] * 2
    )
    got = call(
        body,
        "norm_out_back",
        [SMEM] + [VM] * 8,
        outs,
        (at, three, three_there, cotangent, normal, inverse, two, w_out, norms),
        [pltpu.VMEM((D, D), f32)],
    )
    return got[0], got[1], got[2:6], got[6], got[7]


def add_low(a, b):
    return (a.astype(f32) + b.astype(f32)).astype(bf16)


def step_small(
    patches,
    cotangent,
    input_views,
    token_live,
    master,
    moment_one,
    moment_two,
    norm_params,
    norm_moment_one,
    norm_moment_two,
):
    tokens = patches.shape[0]
    rows, blocks, cols = master.shape
    dp = lax.axis_index("dp")
    seq = lax.axis_index("seq")
    quarter, x_place = seq // 2, seq % 2
    y_place, core = dp // 2, dp % 2
    place = gray(quarter)
    at = jnp.stack([x_place, y_place, core, place]).astype(jnp.int32)

    def to_core(value):
        return swap(value, "dp", 1)

    def to_y(value):
        return swap(value, "dp", 2)

    def to_x(value):
        return swap(value, "seq", 1)

    def by_core(first, second):
        return jnp.where(core == 0, first, second), jnp.where(core == 0, second, first)

    flags = jnp.pad(token_live.astype(bf16)[None, :], ((0, 7), (0, D - tokens)))
    ring = [jnp.concatenate([patches, flags], axis=0)]
    for _ in range(3):
        ring.append(hop_quarter(ring[-1], 1))
    beside = [to_x(piece) for piece in ring]
    cot_there = to_core(cotangent)

    low_t = jnp.transpose(master.astype(bf16), (1, 2, 0))
    halves = [
        jnp.concatenate(
            [
                low_t[4 + 2 * h : 6 + 2 * h].reshape(2 * cols, rows),
                low_t[8 + 2 * h : 10 + 2 * h].reshape(2 * cols, rows),
                low_t[3, h * HALF : (h + 1) * HALF],
                low_t[0:3, h * HALF : (h + 1) * HALF].reshape(3 * HALF, rows),
            ],
            axis=0,
        )
        for h in range(2)
    ]
    own, other = by_core(*halves)
    there = to_core(other)
    both = jnp.concatenate(by_core(own, there), axis=1)
    far = [both[:432]]
    near = both[432:]
    near = jnp.stack([near, to_x(near)])
    near = jnp.stack([near, to_y(near)])
    w_qkv = place_qkv(at, near, to_core(near))

    for _ in range(3):
        far.append(hop_quarter(far[-1], 1))
    far_x = [to_x(piece) for piece in far]
    w_mlp = [jnp.stack([far[k], far_x[k]]) for k in range(4)]
    w_mlp = [(pair, to_y(pair)) for pair in w_mlp]
    out_own = jnp.stack([p[j, 384:] for k in range(4) for j in range(2) for p in w_mlp[k]])
    w_out = place_out(at, out_own, to_core(out_own))

    got = [project(ring[k], beside[k], w_qkv, norm_params) for k in range(4)]
    acts, normals, qs, ks, vs = zip(*got)
    mixed, full, q_back = attend(at, qs, ks, vs)
    mixed = [mixed[0]] + [hop_quarter(mixed[4 - k], k) for k in (3, 2, 1)]

    two, resid, normal_two, inverse_two, act_three = out_norm(at, patches, mixed, w_out, norm_params)

    acts3 = (act_three, to_core(act_three))
    cots = (cotangent, cot_there)
    first = mlp(at, acts3, cots, [w_mlp[1], w_mlp[2]], (), False)
    second = mlp(at, acts3, cots, [w_mlp[3], w_mlp[0]], first[0:2], True)
    out_mine, three_mine = second[0:2]
    out_send, three_send = second[6:8]
    keep = {1: first[2], 2: first[3], 3: second[2], 0: second[3]}
    send = {1: first[4], 2: first[5], 3: second[4], 0: second[5]}
    block_out = (resid + out_mine + to_core(out_send).astype(f32)).astype(bf16)

    grad_resid, sums_two, parts, w_out_keep, w_out_send = norm_out_back(
        at, three_mine, to_core(three_send), cotangent, normal_two, inverse_two, two, w_out, norm_params
    )
    grads = [parts[0]] + [hop_quarter(parts[k], k) for k in (1, 2, 3)]
    dqs, dks, dvs = attend_back(at, q_back, ks, vs, full, grads)
    one_keep, one_send, near_keep, near_send, sums_one = project_back(at, acts, normals, dqs, dks, dvs, w_qkv)

    one = [add_low(one_keep[k], to_x(one_send[k])) for k in range(4)]
    grad_one = reduce_ring(one)
    normal_one, inverse_one = layer_stats(patches.astype(f32))
    patches_grad = grad_resid + layer_back(grad_one, normal_one, inverse_one, norm_params[0])
    param_grad = jnp.concatenate([sums_one[0:2], sums_two[0:2]], axis=0)

    def own_y(value):
        return lax.dynamic_slice_in_dim(value, y_place * 384, 384, value.ndim - 1)

    def other_y(value):
        return lax.dynamic_slice_in_dim(value, (1 - y_place) * 384, 384, value.ndim - 1)

    out_sum = add_low(w_out_keep, to_core(w_out_send))
    out_sum = add_low(own_y(out_sum), to_y(other_y(out_sum)))
    slots = []
    for k in range(4):
        pair = add_low(keep[k], to_y(send[k]))
        stay = jnp.concatenate([pair[0], out_sum[2 * k]], axis=0)
        leave = jnp.concatenate([pair[1], out_sum[2 * k + 1]], axis=0)
        slots.append(add_low(stay, to_x(leave)))
    far_sum = reduce_ring(slots)

    near_sum = add_low(near_keep, to_core(near_send))
    near_sum = add_low(own_y(near_sum), to_y(other_y(near_sum)))
    near_sum = near_sum[0:3].astype(f32) + to_x(near_sum[3:6]).astype(f32)

    grads_t = jnp.concatenate([far_sum, near_sum.reshape(3 * HALF, 2 * rows)], axis=0)
    squares = jnp.full((4, D), jnp.sum(grads_t * grads_t), f32)
    sums = total(jnp.concatenate([param_grad, squares], axis=0))
    param_grad = sums[0:4]
    squares = sums[4, 0] + jnp.sum(param_grad * param_grad)
    grad_norm = jnp.sqrt(squares)
    clip = 1.0 / jnp.maximum(grad_norm, 1.0)
    own, other = by_core(grads_t[:, :rows], grads_t[:, rows:])
    there = to_core(other.astype(bf16)).astype(f32)
    first, second = by_core(own, there)

    def blocks_of(half):
        up = half[0:192].reshape(2, cols, rows)
        down = half[192:384].reshape(2, cols, rows)
        return up, down, half[384:432], half[432:].reshape(3, HALF, rows)

    up0, down0, out0, near0 = blocks_of(first)
    up1, down1, out1, near1 = blocks_of(second)
    weight_grad = jnp.concatenate(
        [
            jnp.concatenate([near0, near1], axis=1),
            jnp.concatenate([out0, out1], axis=0)[None],
            up0,
            up1,
            down0,
            down1,
        ],
        axis=0,
    )
    weight_grad = jnp.transpose(weight_grad, (2, 0, 1))
    new_master, new_moment_one, new_moment_two = adam_step(
        master, weight_grad * clip, moment_one, moment_two, rate_matrix, weight_decay
    )
    new_norm_params, new_norm_moment_one, new_norm_moment_two = adam_step(
        norm_params, param_grad * clip, norm_moment_one, norm_moment_two, rate_vector, 0.0
    )
    return (
        block_out,
        patches_grad,
        new_master,
        new_master.astype(bf16),
        new_moment_one,
        new_moment_two,
        new_norm_params,
        new_norm_moment_one,
        new_norm_moment_two,
        grad_norm,
    )


def solution(mesh):
    tokens = P(("dp", "seq"), None)
    weights = P("dp", None, "seq")
    small = mesh.shape["dp"] == 4 and mesh.shape["seq"] == 8
    return jax.shard_map(
        step_small if small else step_general,
        mesh=mesh,
        in_specs=(tokens, tokens, P("dp"), P(("dp", "seq")), weights, weights, weights, P(), P(), P()),
        out_specs=(tokens, tokens, weights, weights, weights, weights, P(), P(), P(), P()),
        check_vma=False,
    )
```

```python
import math
from functools import partial

import jax
import jax.numpy as jnp
from jax import lax
from jax.experimental import pallas as pl
from jax.experimental.pallas import tpu as pltpu
from jax.sharding import PartitionSpec as P

D = 768
HEADS = 12
HEAD_DIM = 64
FF = 3072
VIEW = 1024
STEP = 10
GROUPS = 4
GROUP_HEADS = HEADS // GROUPS
GROUP_WIDTH = GROUP_HEADS * HEAD_DIM
WIDE = FF // D
RING = (0, 1, 3, 2)

layer_eps = 1e-05
beta_first = 0.9
beta_second = 0.95
adam_eps = 1e-08
rate_matrix = 0.08
rate_vector = 0.8
weight_decay = 0.1
masked_score = -1e30
bf16 = jnp.bfloat16
f32 = jnp.float32


def gray(v):
    return v ^ (v >> 1)


def hop_quarter(value, by):
    split = lax.axis_size("seq") // GROUPS
    pairs = [
        (RING[p] * split + x, RING[(p + by) % GROUPS] * split + x) for p in range(GROUPS) for x in range(split)
    ]
    return lax.ppermute(value, "seq", pairs)


def hop_within(value, by):
    split = lax.axis_size("seq") // GROUPS
    pairs = [(q * split + x, q * split + (x + by) % split) for q in range(GROUPS) for x in range(split)]
    return lax.ppermute(value, "seq", pairs)


def swap(value, axis, bit):
    return lax.ppermute(value, axis, [(i, i ^ bit) for i in range(lax.axis_size(axis))])


def bits_of(axis):
    return [1 << b for b in range(lax.axis_size(axis).bit_length() - 1)]


def total(value):
    for axis in ("dp", "seq"):
        for bit in bits_of(axis):
            value = value + swap(value, axis, bit)
    return value


def pick(stack, index):
    return lax.dynamic_index_in_dim(stack, index, 0, keepdims=False)


def layer_stats(values):
    centre = jnp.mean(values, axis=-1, keepdims=True)
    shifted = values - centre
    spread = jnp.mean(shifted * shifted, axis=-1, keepdims=True)
    inverse = lax.rsqrt(spread + layer_eps)
    return (shifted * inverse, inverse)


def layer_back(grad_normed, normalized, inverse, gain):
    scaled = grad_normed * gain
    centred = jnp.mean(scaled, axis=-1, keepdims=True)
    along = jnp.mean(scaled * normalized, axis=-1, keepdims=True)
    return inverse * (scaled - centred - normalized * along)


def mm(a, b):
    return jnp.dot(a, b, preferred_element_type=f32)


def mm_nt(a, b):
    return lax.dot_general(a, b, (((1,), (1,)), ((), ())), preferred_element_type=f32)


def mm_tn(a, b):
    return lax.dot_general(a, b, (((0,), (0,)), ((), ())), preferred_element_type=f32)


def gather_rows(piece):
    for bit in reversed(bits_of("dp")):
        piece = jnp.concatenate([piece, swap(piece, "dp", bit)], axis=1)
    return piece


def row_order():
    order = [0]
    for bit in reversed(bits_of("dp")):
        order = order + [o ^ bit for o in order]
    return order


def reduce_rows(piece):
    for bit in bits_of("dp"):
        half = piece.shape[1] // 2
        there = swap(piece[:, half:], "dp", bit)
        piece = (piece[:, :half].astype(f32) + there.astype(f32)).astype(bf16)
    return piece


def reduce_within(piece):
    own = piece[0].astype(f32)
    for j in range(1, piece.shape[0]):
        own = own + hop_within(piece[j], -j).astype(f32)
    return own.astype(bf16)


def reduce_ring(slots):
    moving = slots[1]
    for k in (2, 3):
        moving = (hop_quarter(moving, 1).astype(f32) + slots[k].astype(f32)).astype(bf16)
    return hop_quarter(moving, 1).astype(f32) + slots[0].astype(f32)


def adam_step(params, grads, first, second, rate, decay):
    first_new = beta_first * first + (1.0 - beta_first) * grads
    second_new = beta_second * second + (1.0 - beta_second) * grads * grads
    first_hat = first_new / (1.0 - beta_first**STEP)
    second_hat = second_new / (1.0 - beta_second**STEP)
    params_new = params - rate * (first_hat / (jnp.sqrt(second_hat) + adam_eps) + decay * params)
    return (params_new, first_new, second_new)


def relative(dp, absolute, order):
    index = jnp.int32(0)
    for at, offset in enumerate(order):
        index = jnp.where((dp ^ absolute) == offset, at, index)
    return index


def step_general(
    patches,
    cotangent,
    input_views,
    token_live,
    master,
    moment_one,
    moment_two,
    norm_params,
    norm_moment_one,
    norm_moment_two,
):
    tokens = patches.shape[0]
    rows, blocks, cols = master.shape
    n_dp = lax.axis_size("dp")
    split = lax.axis_size("seq") // GROUPS
    dp = lax.axis_index("dp")
    seq = lax.axis_index("seq")
    quarter, within = seq // split, seq % split
    place = gray(quarter)
    inputs_seen = input_views[0]
    gain_one, shift_one, gain_two, shift_two = (norm_params[i] for i in range(4))
    order = row_order()
    dp_place = [order.index(a) for a in range(n_dp)]

    def quarter_behind(k):
        return gray((place - k) & 3)

    flags = jnp.pad(token_live.astype(bf16)[None, :], ((0, 7), (0, D - tokens)))
    ring = [jnp.concatenate([patches, flags], axis=0)]
    for _ in range(3):
        ring.append(hop_quarter(ring[-1], 1))
    pieces = [[ring[k]] + [hop_within(ring[k], j) for j in range(1, split)] for k in range(4)]
    scene = jnp.stack([jnp.stack([p[:tokens] for p in pieces[k]]) for k in range(4)])
    live = jnp.stack([jnp.concatenate([p[tokens, :tokens] for p in pieces[k]]) for k in range(4)])

    copy_low = master.astype(bf16)
    mine = copy_low[:, 0:3, :].reshape(rows, 3 * cols)
    near = jnp.stack([mine] + [hop_within(mine, j) for j in range(1, split)])
    near = gather_rows(near).reshape(split, n_dp, rows, 3, cols)
    near = jnp.stack([pick(near, (within - a) % split) for a in range(split)])
    near = jnp.moveaxis(near, 1, 0)
    near = jnp.stack([pick(near, order_at) for order_at in [relative(dp, a, order) for a in range(n_dp)]])
    w_qkv = jnp.transpose(near, (0, 2, 3, 1, 4)).reshape(D, 3, GROUP_WIDTH)

    up = copy_low[:, 4 : 4 + WIDE].reshape(rows, WIDE * cols)
    down = copy_low[:, 4 + WIDE :].reshape(rows, WIDE * cols)
    far = [jnp.concatenate([up, down, copy_low[:, 3]], axis=1)]
    for _ in range(3):
        far.append(hop_quarter(far[-1], 1))
    weights = [gather_rows(jnp.stack([f] + [hop_within(f, j) for j in range(1, split)])) for f in far]
    width = WIDE * cols
    w_up = [w[:, :, :width] for w in weights]
    w_down = [w[:, :, width : 2 * width] for w in weights]
    w_out = jnp.stack([w[:, :, 2 * width :] for w in weights]).reshape(4 * split, n_dp, rows, cols)

    def slot_of(quarter_abs, within_abs):
        return ((place - gray(quarter_abs)) & 3) * split + (within - within_abs) % split

    w_out = jnp.stack([pick(w_out, slot_of(a // split, a % split)) for a in range(4 * split)])
    w_out = jnp.moveaxis(w_out, 1, 0)
    w_out = jnp.stack([pick(w_out, relative(dp, a, order)) for a in range(n_dp)])
    w_out = jnp.transpose(w_out, (0, 2, 1, 3)).reshape(D, D)

    normal_one, inverse_one = layer_stats(scene.astype(f32))
    act_one = (normal_one * gain_one + shift_one).astype(bf16)
    act_all = act_one.reshape(4 * split * tokens, D)
    act_own = act_one[:, 0].reshape(4 * tokens, D)
    q = mm(act_own, w_qkv[:, 0]).astype(bf16)
    k = mm(act_all, w_qkv[:, 1]).astype(bf16)
    v = mm(act_all, w_qkv[:, 2]).astype(bf16)

    def heads(m):
        return jnp.transpose(m.reshape(m.shape[0], GROUP_HEADS, HEAD_DIM), (1, 0, 2))

    def unheads(m):
        return jnp.transpose(m, (1, 0, 2)).reshape(m.shape[1], GROUP_WIDTH)

    views = jnp.stack([(quarter_behind(i) * split * tokens) // VIEW for i in range(4)])
    open_block = (views[None, :] < inputs_seen) | (views[None, :] == views[:, None])
    visible = open_block[:, None, :, None] & (live > 0)[None, None]
    visible = jnp.broadcast_to(visible, (4, tokens, 4, split * tokens)).reshape(4 * tokens, -1)
    scaling = 1.0 / math.sqrt(HEAD_DIM)
    qh, kh, vh = heads(q), heads(k), heads(v)
    scores = jnp.einsum("hqd,hkd->hqk", qh, kh, preferred_element_type=f32) * scaling
    scores = jnp.where(visible[None], scores, masked_score)
    top = jnp.max(scores, axis=-1, keepdims=True)
    probs = jnp.where(visible[None], jnp.exp(scores - top), 0.0)
    probs = probs / jnp.sum(probs, axis=-1, keepdims=True)
    probs_low = probs.astype(bf16)
    attended = jnp.einsum("hqk,hkd->hqd", probs_low, vh, preferred_element_type=f32)
    flat = unheads(attended).astype(bf16).reshape(4, tokens, GROUP_WIDTH)
    back = jnp.stack([flat[0]] + [hop_quarter(flat[i], -i) for i in range(1, 4)])
    act_two = jnp.concatenate([pick(back, (gray(a) - place) & 3) for a in range(4)], axis=1)

    patch_float = patches.astype(f32)
    resid = patch_float + mm(act_two, w_out)
    normal_two, inverse_two = layer_stats(resid)
    act_three = (normal_two * gain_two + shift_two).astype(bf16)

    def to_relative(m):
        parts = m.reshape(tokens, n_dp, rows)
        return jnp.concatenate([lax.dynamic_index_in_dim(parts, dp ^ o, 1, keepdims=False) for o in order], axis=1)

    def from_relative(m):
        parts = m.reshape(tokens, n_dp, rows)
        return jnp.concatenate(
            [lax.dynamic_index_in_dim(parts, relative(dp, a, order), 1, keepdims=False) for a in range(n_dp)], axis=1
        )

    act_rel = to_relative(act_three)
    cot_rel = to_relative(cotangent)
    branch_rel = jnp.zeros((tokens, D), f32)
    three_rel = jnp.zeros((tokens, D), f32)
    far_grads = []
    for i in range(4):
        group = []
        for j in range(split):
            widened = mm(act_rel, w_up[i][j])
            activated, gelu_pull = jax.vjp(partial(jax.nn.gelu, approximate=False), widened)
            hidden = activated.astype(bf16)
            branch_rel = branch_rel + mm_nt(hidden, w_down[i][j])
            grad_wide = gelu_pull(mm(cot_rel, w_down[i][j]))[0].astype(bf16)
            three_rel = three_rel + mm_nt(grad_wide, w_up[i][j])
            grad_up = mm_tn(act_rel, grad_wide).astype(bf16)
            grad_down = mm_tn(cot_rel, hidden).astype(bf16)
            group.append((grad_up, grad_down))
        far_grads.append(group)
    block_out = (resid + from_relative(branch_rel)).astype(bf16)
    grad_three = from_relative(three_rel)
    gain_two_grad = jnp.sum(grad_three * normal_two, axis=0)
    shift_two_grad = jnp.sum(grad_three, axis=0)
    grad_resid = cotangent.astype(f32) + layer_back(grad_three, normal_two, inverse_two, gain_two)
    grad_branch = grad_resid.astype(bf16)
    grad_attended = mm_nt(grad_branch, w_out).astype(bf16)
    grad_w_out = mm_tn(act_two, grad_branch).astype(bf16)

    parts = jnp.transpose(grad_attended.reshape(tokens, 4, GROUP_WIDTH), (1, 0, 2))
    parts = [pick(parts, gray((place + i) & 3)) for i in range(4)]
    grad_here = jnp.concatenate([parts[0]] + [hop_quarter(parts[i], i) for i in range(1, 4)], axis=0)
    gh = heads(grad_here)
    dprobs = jnp.einsum("hqd,hkd->hqk", gh, vh, preferred_element_type=f32)
    delta = jnp.sum(gh.astype(f32) * attended, axis=-1, keepdims=True)
    grad_scores = (probs * (dprobs - delta)).astype(bf16)
    dq = unheads(jnp.einsum("hqk,hkd->hqd", grad_scores, kh, preferred_element_type=f32) * scaling).astype(bf16)
    dk = unheads(jnp.einsum("hqk,hqd->hkd", grad_scores, qh, preferred_element_type=f32) * scaling).astype(bf16)
    dv = unheads(jnp.einsum("hqk,hqd->hkd", probs_low, gh, preferred_element_type=f32)).astype(bf16)

    grad_near = jnp.stack([mm_tn(act_own, dq), mm_tn(act_all, dk), mm_tn(act_all, dv)], axis=1).astype(bf16)
    grad_near = grad_near.reshape(n_dp, rows, 3, split, cols)
    grad_near = jnp.stack([pick(grad_near, dp ^ o) for o in order])
    grad_near = jnp.transpose(grad_near, (3, 0, 1, 2, 4)).reshape(split, D, 3 * cols)
    grad_near = jnp.stack([pick(grad_near, (within - j) % split) for j in range(split)])
    grad_near = reduce_within(reduce_rows(grad_near)).astype(f32).reshape(rows, 3, cols)

    one_q = mm_nt(dq, w_qkv[:, 0]).reshape(4, 1, tokens, D)
    one_kv = (mm_nt(dk, w_qkv[:, 1]) + mm_nt(dv, w_qkv[:, 2])).reshape(4, split, tokens, D)
    one = jnp.concatenate([one_kv[:, :1] + one_q, one_kv[:, 1:]], axis=1)
    gain_one_grad = jnp.sum(one * normal_one, axis=(0, 1, 2))
    shift_one_grad = jnp.sum(one, axis=(0, 1, 2))
    one_low = one.astype(bf16)
    grad_one = reduce_ring([reduce_within(one_low[i]) for i in range(4)])
    patches_grad = grad_resid + layer_back(grad_one, normal_one[0, 0], inverse_one[0, 0], gain_one)

    out_parts = grad_w_out.reshape(n_dp, rows, 4 * split, cols)
    out_parts = jnp.stack([pick(out_parts, dp ^ o) for o in order])
    out_parts = jnp.transpose(out_parts, (2, 0, 1, 3)).reshape(4 * split, D, cols)
    slots = []
    for i in range(4):
        stack = []
        for j in range(split):
            own_out = pick(out_parts, quarter_behind(i) * split + (within - j) % split)
            stack.append(jnp.concatenate([*far_grads[i][j], own_out], axis=1))
        slots.append(reduce_within(reduce_rows(jnp.stack(stack))))
    far_sum = reduce_ring(slots)
    grad_up = far_sum[:, :width].reshape(rows, WIDE, cols)
    grad_down = far_sum[:, width : 2 * width].reshape(rows, WIDE, cols)
    grad_out = far_sum[:, 2 * width :].reshape(rows, 1, cols)

    weight_grad = jnp.concatenate([grad_near, grad_out, grad_up, grad_down], axis=1)
    param_grad = total(jnp.stack([gain_one_grad, shift_one_grad, gain_two_grad, shift_two_grad]))
    squares = total(jnp.full((8, 128), jnp.sum(weight_grad * weight_grad), f32))[0, 0] + jnp.sum(param_grad * param_grad)
    grad_norm = jnp.sqrt(squares)
    clip = 1.0 / jnp.maximum(grad_norm, 1.0)
    new_master, new_moment_one, new_moment_two = adam_step(
        master, weight_grad * clip, moment_one, moment_two, rate_matrix, weight_decay
    )
    new_norm_params, new_norm_moment_one, new_norm_moment_two = adam_step(
        norm_params, param_grad * clip, norm_moment_one, norm_moment_two, rate_vector, 0.0
    )
    return (
        block_out,
        patches_grad,
        new_master,
        new_master.astype(bf16),
        new_moment_one,
        new_moment_two,
        new_norm_params,
        new_norm_moment_one,
        new_norm_moment_two,
        grad_norm,
    )


HALF = 48
ANY = pl.BlockSpec(memory_space=pl.ANY)
SMEM = pl.BlockSpec(memory_space=pltpu.SMEM)
VMEM_LIMIT = 56 << 20
SCALE = 1.0


def call(body, name, ins, outs, operands, scratch=(), us=4, out_specs=None, aliases=None):
    return pl.pallas_call(
        body,
        name=name,
        out_shape=outs,
        in_specs=ins,
        out_specs=out_specs or jax.tree.map(lambda _: pl.BlockSpec(memory_space=pltpu.VMEM), outs),
        scratch_shapes=list(scratch),
        input_output_aliases=aliases or {},
        cost_estimate=pl.CostEstimate(flops=int(us * SCALE * 1e9), bytes_accessed=int(us * SCALE * 3.6e6), transcendentals=0),
        compiler_params=pltpu.CompilerParams(vmem_limit_bytes=VMEM_LIMIT),
    )(*operands)


VM = pl.BlockSpec(memory_space=pltpu.VMEM)


def shape(dims, dtype):
    return jax.ShapeDtypeStruct(dims, dtype)


def run_copies(copies):
    for c in copies:
        c.start()
    for c in copies:
        c.wait()


def place_qkv(at, own_half, other_half):
    def body(at_ref, own_ref, other_ref, out_ref, sems):
        x, y, c = at_ref[0], at_ref[1], at_ref[2]
        copies = []
        for block in range(3):
            for j in range(2):
                for r in range(2):
                    for h, ref in ((0, own_ref), (1, other_ref)):
                        row = block * GROUP_WIDTH + (x ^ j) * 96 + (c ^ h) * HALF
                        copies.append(
                            pltpu.make_async_copy(
                                ref.at[r, j, pl.ds(block * HALF, HALF), :],
                                out_ref.at[
                                    pl.ds(pl.multiple_of(row, 16), HALF),
                                    pl.ds(pl.multiple_of((y ^ r) * 384, 128), 384),
                                ],
                                sems.at[len(copies)],
                            )
                        )
        run_copies(copies)

    return call(
        body,
        "place_qkv",
        [SMEM, ANY, ANY],
        shape((3 * GROUP_WIDTH, D), bf16),
        (at, own_half, other_half),
        [pltpu.SemaphoreType.DMA((24,))],
    )


def place_out(at, own_half, other_half):
    def body(at_ref, own_ref, other_ref, out_ref, sems):
        x, y, c, place = at_ref[0], at_ref[1], at_ref[2], at_ref[3]
        copies = []
        for k in range(4):
            quarter = gray((place - k) & 3)
            for j in range(2):
                for r in range(2):
                    for h, ref in ((0, own_ref), (1, other_ref)):
                        row = (quarter * 2 + (x ^ j)) * 96
                        copies.append(
                            pltpu.make_async_copy(
                                ref.at[r, k * 2 + j],
                                out_ref.at[(y ^ r) * 2 + (c ^ h), pl.ds(pl.multiple_of(row, 16), 96), :],
                                sems.at[len(copies)],
                            )
                        )
        run_copies(copies)

    return call(
        body,
        "place_out",
        [SMEM, ANY, ANY],
        shape((4, D, 256), bf16),
        (at, own_half, other_half),
        [pltpu.SemaphoreType.DMA((32,))],
        us=3,
    )


def normalize(values):
    centre = jnp.mean(values, axis=-1, keepdims=True)
    shifted = values - centre
    inverse = lax.rsqrt(jnp.mean(shifted * shifted, axis=-1, keepdims=True) + layer_eps)
    return shifted * inverse, inverse


def lane_index(dims):
    return lax.broadcasted_iota(jnp.int32, dims, len(dims) - 1)


def project(first, second, w_t, norms):
    def body(a_ref, b_ref, w_ref, norm_ref, act_ref, normal_ref, q_ref, k_ref, v_ref, wide_ref):
        wide_ref[...] = jnp.zeros_like(wide_ref)
        for h in range(9):
            wide_ref[h * 128 : h * 128 + 64, :] = w_ref[h * 64 : h * 64 + 64, :]
        gain, shift = norm_ref[0:1, :], norm_ref[1:2, :]
        for piece, ref in enumerate((a_ref, b_ref)):
            at = slice(piece * 256, piece * 256 + 256)
            normal, _ = normalize(ref[0:256, :].astype(f32))
            act = (normal * gain + shift).astype(bf16)
            normal_ref[at, :] = normal.astype(bf16)
            act_ref[at, :] = act
            flags = ref[256:257, 0:256].astype(f32)
            mask = jnp.where(flags > 0, 0.0, masked_score)
            mask = jnp.transpose(jnp.broadcast_to(mask, (128, 256)))
            lanes = lane_index((256, 128))
            for h in range(3):
                if piece == 0:
                    q = mm_nt(act, wide_ref[h * 128 : h * 128 + 128, :]).astype(bf16).astype(f32)
                    q = jnp.where(lanes == 64, 1.0, q * (1.0 / math.sqrt(HEAD_DIM)))
                    q_ref[h] = q.astype(bf16)
                k = mm_nt(act, wide_ref[(3 + h) * 128 : (4 + h) * 128, :])
                k = jnp.where(lanes == 64, mask, k)
                k_ref[h, at, :] = jnp.where((lanes > 64) & (lanes < 68), 1.0, k).astype(bf16)
                v = mm_nt(act, wide_ref[(6 + h) * 128 : (7 + h) * 128, :])
                v_ref[h, at, :] = jnp.where((lanes > 63) & (lanes < 67), 1.0, v).astype(bf16)

    outs = [
        shape((512, D), bf16),
        shape((512, D), bf16),
        shape((3, 256, 128), bf16),
        shape((3, 512, 128), bf16),
        shape((3, 512, 128), bf16),
    ]
    return call(body, "norm_project", [VM] * 4, outs, (first, second, w_t, norms), [pltpu.VMEM((1152, D), bf16)], us=4)


def in_three(value):
    high = value.astype(bf16).astype(f32)
    rest = value - high
    mid = rest.astype(bf16).astype(f32)
    return high, mid, rest - mid


def with_parts(base, lanes, first, value):
    for i, part in enumerate(in_three(value)):
        base = jnp.where(lanes == first + i, part, base)
    return base


def join_heads(parts):
    return jnp.concatenate([p[:, :HEAD_DIM] for p in parts], axis=1)


def stack_slots(place, slots, stacked, sems, base=0):
    return [
        pltpu.make_async_copy(ref, stacked.at[gray((place - k) & 3)], sems.at[base + k]) for k, ref in enumerate(slots)
    ]


def attend(at, qs, ks, vs):
    def body(at_ref, *refs):
        low_refs, full_ref, back_ref = refs[12:16], refs[16], refs[17]
        q_ref, k_ref, v_ref, sems = refs[18:22]
        place = at_ref[3]
        lanes = lane_index((256, 128))
        run_copies(
            stack_slots(place, refs[0:4], q_ref, sems)
            + stack_slots(place, refs[4:8], k_ref, sems, 4)
            + stack_slots(place, refs[8:12], v_ref, sems, 8)
        )

        def head(h, _):
            for i in range(4):
                chunks = (0, 1) if i < 2 else (0, 1, 2, 3)
                q = q_ref[i, h]
                scores = [mm_nt(q, k_ref[c, h]) for c in chunks]
                top = None
                for s in scores:
                    for b in range(0, s.shape[1], 128):
                        part = s[:, b : b + 128]
                        top = part if top is None else jnp.maximum(top, part)
                top = jnp.max(top, axis=1, keepdims=True)
                mixed = None
                for s, c in zip(scores, chunks):
                    part = mm(jnp.exp(s - top).astype(bf16), v_ref[c, h])
                    mixed = part if mixed is None else mixed + part
                norm = mixed[:, HEAD_DIM : HEAD_DIM + 1]
                full_ref[i, h] = mixed / norm
                logsum = top + jnp.log(norm)
                back_ref[i, h] = with_parts(q.astype(f32), lanes, 65, -logsum).astype(bf16)
            return 0

        lax.fori_loop(0, 3, head, 0)
        for k in range(4):
            i = gray((place - k) & 3)
            low_refs[k][...] = join_heads([full_ref[i, h] for h in range(3)]).astype(bf16)

    outs = (
        [shape((256, GROUP_WIDTH), bf16)] * 4 + [shape((4, 3, 256, 128), f32)] + [shape((4, 3, 256, 128), bf16)]
    )
    got = call(
        body,
        "attend",
        [SMEM] + [ANY] * 12,
        outs,
        (at, *qs, *ks, *vs),
        [
            pltpu.VMEM((4, 3, 256, 128), bf16),
            pltpu.VMEM((4, 3, 512, 128), bf16),
            pltpu.VMEM((4, 3, 512, 128), bf16),
            pltpu.SemaphoreType.DMA((12,)),
        ],
        us=12,
    )
    return got[0:4], got[4], got[5]


def attend_back(at, q_back, ks, vs, full, grads):
    def body(at_ref, q_ref, *refs):
        full_ref, g_refs = refs[8], refs[9:13]
        dq_refs, dk_refs, dv_refs = refs[13:17], refs[17:21], refs[21:25]
        k_ref, v_ref, g_ref, dq_ref, dk_ref, dv_ref, sems = refs[25:32]
        place = at_ref[3]
        copies = stack_slots(place, refs[0:4], k_ref, sems) + stack_slots(place, refs[4:8], v_ref, sems, 4)
        for c in copies:
            c.start()
        lanes = lane_index((256, 128))
        for k in range(4):
            i = gray((place - k) & 3)
            for h in range(3):
                g = g_refs[k][:, h * 64 : h * 64 + 64].astype(f32)
                delta = jnp.sum(g * full_ref[i, h][:, :64], axis=-1, keepdims=True)
                g = jnp.concatenate([g, jnp.zeros((256, 64), f32)], axis=1)
                g_ref[h, pl.ds(pl.multiple_of(i * 256, 256), 256), :] = with_parts(g, lanes, 64, -delta).astype(bf16)
        for c in copies:
            c.wait()

        def head(h, _):
            q_all = jnp.concatenate([q_ref[i, h] for i in range(4)], axis=0)
            for c in range(4):
                first = 0 if c < 2 else 512
                k, v = k_ref[c, h], v_ref[c, h]
                q, g = q_all[first:], g_ref[h, first:, :]
                p = jnp.exp(mm_nt(k, q))
                ds = (p * mm_nt(v, g)).astype(bf16)
                dv_ref[c, h] = mm(p.astype(bf16), g)
                dk_ref[c, h] = mm(ds, q)
                dq = mm(jnp.transpose(k), ds)
                if c == 0:
                    dq_ref[h] = dq
                else:
                    dq_ref[h, :, first:] += dq
            return 0

        lax.fori_loop(0, 3, head, 0)
        for k in range(4):
            i = gray((place - k) & 3)
            cols = pl.ds(pl.multiple_of(i * 256, 256), 256)
            parts = [jnp.transpose(dq_ref[h, :, cols]) for h in range(3)]
            dq_refs[k][...] = (join_heads(parts) * (1.0 / math.sqrt(HEAD_DIM))).astype(bf16)
            dk_refs[k][...] = join_heads([dk_ref[i, h] for h in range(3)]).astype(bf16)
            dv_refs[k][...] = join_heads([dv_ref[i, h] for h in range(3)]).astype(bf16)

    outs = [shape((256, GROUP_WIDTH), bf16)] * 4 + [shape((512, GROUP_WIDTH), bf16)] * 8
    got = call(
        body,
        "attend_back",
        [SMEM, VM] + [ANY] * 8 + [VM] * 5,
        outs,
        (at, q_back, *ks, *vs, full, *grads),
        [
            pltpu.VMEM((4, 3, 512, 128), bf16),
            pltpu.VMEM((4, 3, 512, 128), bf16),
            pltpu.VMEM((3, 1024, 128), bf16),
            pltpu.VMEM((3, 128, 1024), f32),
            pltpu.VMEM((4, 3, 512, 128), f32),
            pltpu.VMEM((4, 3, 512, 128), f32),
            pltpu.SemaphoreType.DMA((8,)),
        ],
        us=16,
    )
    return got[0:4], got[4:8], got[8:12]


def input_back(normals, dqs, dks, dvs, w_t):
    count = len(normals)

    def body(*refs):
        normal_refs, dq_refs, dk_refs, dv_refs = (refs[n * count : (n + 1) * count] for n in range(4))
        w_ref, *outs = refs[4 * count :]
        keep_refs, send_refs, norm_ref = outs[0:count], outs[count : 2 * count], outs[2 * count]
        gains, shifts = jnp.zeros((1, D), f32), jnp.zeros((1, D), f32)
        for i in range(count):
            for j, out_ref in enumerate((keep_refs[i], send_refs[i])):
                r = slice(j * 256, j * 256 + 256)
                one = mm(dk_refs[i][r, :], w_ref[192:384, :]) + mm(dv_refs[i][r, :], w_ref[384:576, :])
                if j == 0:
                    one = one + mm(dq_refs[i][...], w_ref[0:192, :])
                gains = gains + jnp.sum(one * normal_refs[i][r, :].astype(f32), axis=0, keepdims=True)
                shifts = shifts + jnp.sum(one, axis=0, keepdims=True)
                out_ref[...] = one.astype(bf16)
        norm_ref[...] = jnp.concatenate([gains, shifts, jnp.zeros((6, D), f32)], axis=0)

    outs = [shape((256, D), bf16)] * (2 * count) + [shape((8, D), f32)]
    got = call(body, "input_back", [VM] * (4 * count + 1), outs, (*normals, *dqs, *dks, *dvs, w_t), us=count + 1)
    return got[0:count], got[count : 2 * count], got[2 * count]


def projections_back(at, acts, dqs, dks, dvs):
    def body(at_ref, *refs):
        act_refs, dq_refs, dk_refs, dv_refs = (refs[4 * n : 4 * n + 4] for n in range(4))
        w_keep_ref, w_send_ref, dw_ref = refs[16:19]
        for i in range(4):
            act = act_refs[i][...]
            for b, (ref, rows) in enumerate(((dq_refs[i], 256), (dk_refs[i], 512), (dv_refs[i], 512))):
                part = mm_tn(ref[...], act[:rows])
                at_rows = slice(b * GROUP_WIDTH, (b + 1) * GROUP_WIDTH)
                dw_ref[at_rows, :] = part if i == 0 else dw_ref[at_rows, :] + part
        x, c = at_ref[0], at_ref[2]
        for b in range(3):
            for xa in range(2):
                for half in range(2):
                    row = b * GROUP_WIDTH + (xa * 2 + half) * HALF
                    block = dw_ref[row : row + HALF, :].astype(bf16)

                    @pl.when(c == half)
                    def _():
                        w_keep_ref[(x ^ xa) * 3 + b] = block

                    @pl.when(c != half)
                    def _():
                        w_send_ref[(x ^ xa) * 3 + b] = block

    return call(
        body,
        "projections_back",
        [SMEM] + [VM] * 16,
        [shape((6, HALF, D), bf16)] * 2,
        (at, *acts, *dqs, *dks, *dvs),
        [pltpu.VMEM((3 * GROUP_WIDTH, D), f32)],
        us=6,
    )


def out_norm(at, patches, mixed, w_out, norms):
    def body(at_ref, x_ref, m0, m1, m2, m3, w_ref, norm_ref, two_ref, resid_ref, normal_ref, inverse_ref, three_ref):
        place = at_ref[3]
        parts = [m[...].astype(f32) for m in (m0, m1, m2, m3)]
        groups = []
        for a in range(4):
            steps = (gray(a) - place) & 3
            part = parts[0]
            for k in (1, 2, 3):
                part = jnp.where(steps == k, parts[k], part)
            groups.append(part)
        resid = x_ref[...].astype(f32)
        for a in range(4):
            resid = resid + mm_nt(groups[a].astype(bf16), w_ref[a][:, :GROUP_WIDTH])
        two_ref[...] = jnp.concatenate(groups, axis=1).astype(bf16)
        resid_ref[...] = resid
        normal, inverse = normalize(resid)
        normal_ref[...] = normal
        inverse_ref[...] = jnp.broadcast_to(inverse, (256, 128))
        three_ref[...] = (normal * norm_ref[2:3, :] + norm_ref[3:4, :]).astype(bf16)

    outs = [
        shape((256, D), bf16),
        shape((256, D), f32),
        shape((256, D), f32),
        shape((256, 128), f32),
        shape((256, D), bf16),
    ]
    return call(body, "out_norm", [SMEM] + [VM] * 7, outs, (at, patches, *mixed, w_out, norms))


def by_core_rows(values):
    return jnp.concatenate([values[:, n * 192 : n * 192 + 192] for n in (0, 2, 1, 3)], axis=1)


def mlp(at, act, cot, weights, out_dtype):
    def body(at_ref, a_ref, c_ref, *refs):
        w_refs = refs[0:4]
        hidden_ref, wide_ref, out_ref, three_ref, act_ref, cot_ref, w_ref, out_acc, three_acc, sems = refs[4:14]
        core = at_ref[2]
        own_lanes = pl.ds(pl.multiple_of(core * 384, 128), 384)
        other_lanes = pl.ds(pl.multiple_of((1 - core) * 384, 128), 384)
        copies = []
        for k in range(4):
            group = []
            for r, lanes in enumerate((own_lanes, other_lanes)):
                for j in range(2):
                    for u in range(2):
                        group.append(
                            pltpu.make_async_copy(
                                w_refs[2 * r + k // 2].at[2 * (k % 2) + j, pl.ds(u * 192, 192), :],
                                w_ref.at[k, u, pl.ds(j * 192, 192), lanes],
                                sems.at[k, len(group)],
                            )
                        )
            copies.append(group)
            for c in group:
                c.start()
        act_ref[...] = by_core_rows(a_ref[...])
        cot_ref[...] = by_core_rows(c_ref[...])
        for k in range(4):
            for c in copies[k]:
                c.wait()
            up, down = w_ref[k, 0], w_ref[k, 1]
            widened = mm_nt(act_ref[...], up)
            inner = 0.5 * (1.0 + lax.erf(widened * (1.0 / math.sqrt(2.0))))
            slope = inner + widened * jnp.exp(-0.5 * widened * widened) * (1.0 / math.sqrt(2.0 * math.pi))
            hidden = (widened * inner).astype(bf16)
            wide = (mm_nt(cot_ref[...], down) * slope).astype(bf16)
            hidden_ref[:, k * 384 : k * 384 + 384] = hidden
            wide_ref[:, k * 384 : k * 384 + 384] = wide
            out, three = mm(hidden, down), mm(wide, up)
            out_acc[...] = out if k == 0 else out_acc[...] + out
            three_acc[...] = three if k == 0 else three_acc[...] + three
        out_ref[...] = by_core_rows(out_acc[...]).astype(out_dtype)
        three_ref[...] = by_core_rows(three_acc[...]).astype(out_dtype)

    return call(
        body,
        "mlp",
        [SMEM] + [VM] * 2 + [ANY] * 4,
        [shape((256, 1536), bf16)] * 2 + [shape((256, D), out_dtype)] * 2,
        (at, act, cot, *weights),
        [
            pltpu.VMEM((256, D), bf16),
            pltpu.VMEM((256, D), bf16),
            pltpu.VMEM((4, 2, 384, D), bf16),
            pltpu.VMEM((256, D), f32),
            pltpu.VMEM((256, D), f32),
            pltpu.SemaphoreType.DMA((4, 8)),
        ],
        us=8,
    )


def mlp_weights(at, acts, cots, hiddens, wides, slots):
    count = len(slots)

    def body(at_ref, *refs):
        a_refs, c_refs, h_refs, w_refs = (refs[2 * n : 2 * n + 2] for n in range(4))
        keep_ref, send_ref, act_ref, cot_ref, in_ref, stage_ref, in_sems, out_sems = refs[8:16]
        arriving = []
        for n, k in enumerate(slots):
            group = []
            for which, sources in enumerate((w_refs, h_refs)):
                for i in range(2):
                    group.append(
                        pltpu.make_async_copy(
                            sources[i].at[:, pl.ds(k * 384, 384)],
                            in_ref.at[n, which, pl.ds(i * 256, 256), :],
                            in_sems.at[n, len(group)],
                        )
                    )
                    group[-1].start()
            arriving.append(group)
        for i in range(2):
            act_ref[i * 256 : i * 256 + 256, :] = by_core_rows(a_refs[i][...])
            cot_ref[i * 256 : i * 256 + 256, :] = by_core_rows(c_refs[i][...])
        core = at_ref[2]
        own_lanes = pl.ds(pl.multiple_of(core * 384, 128), 384)
        other_lanes = pl.ds(pl.multiple_of((1 - core) * 384, 128), 384)
        leaving = []
        for n in range(count):
            for c in arriving[n]:
                c.wait()
            up = mm_tn(in_ref[n, 0], act_ref[...]).astype(bf16)
            down = mm_tn(in_ref[n, 1], cot_ref[...]).astype(bf16)
            for j in range(2):
                stage_ref[n, j, 0:192, :] = up[j * 192 : j * 192 + 192]
                stage_ref[n, j, 192:384, :] = down[j * 192 : j * 192 + 192]
            for i, (lanes, ref) in enumerate(((own_lanes, keep_ref), (other_lanes, send_ref))):
                leaving.append(pltpu.make_async_copy(stage_ref.at[n, :, :, lanes], ref.at[:, n], out_sems.at[n, i]))
                leaving[-1].start()
        for c in leaving:
            c.wait()

    return call(
        body,
        "mlp_weights",
        [SMEM] + [VM] * 4 + [ANY] * 4,
        [shape((2, count, 384, 384), bf16)] * 2,
        (at, *acts, *cots, *hiddens, *wides),
        [
            pltpu.VMEM((512, D), bf16),
            pltpu.VMEM((512, D), bf16),
            pltpu.VMEM((count, 2, 512, 384), bf16),
            pltpu.VMEM((count, 2, 384, D), bf16),
            pltpu.SemaphoreType.DMA((count, 4)),
            pltpu.SemaphoreType.DMA((count, 2)),
        ],
        us=4,
        out_specs=[ANY] * 2,
    )


def norm_out_back(at, three, three_there, cotangent, normal, inverse, two, w_out, norms):
    def body(at_ref, t_ref, s_ref, c_ref, n_ref, i_ref, two_ref, w_ref, norm_ref, *outs):
        resid_ref, sums_ref = outs[0:2]
        g_refs, keep_ref, send_ref, dw_ref = outs[2:6], outs[6], outs[7], outs[8]
        x, c, place = at_ref[0], at_ref[2], at_ref[3]
        grad = t_ref[...] + s_ref[...].astype(f32)
        normal = n_ref[...]
        sums_ref[...] = jnp.concatenate(
            [jnp.sum(grad * normal, axis=0, keepdims=True), jnp.sum(grad, axis=0, keepdims=True), jnp.zeros((6, D), f32)],
            axis=0,
        )
        resid = c_ref[...].astype(f32) + layer_back(grad, normal, i_ref[:, 0:1], norm_ref[2:3, :])
        resid_ref[...] = resid
        low = resid.astype(bf16)
        groups = [mm(low, w_ref[a][:, :GROUP_WIDTH]) for a in range(4)]
        for k in range(4):
            ahead = gray((place + k) & 3)
            part = groups[0]
            for a in (1, 2, 3):
                part = jnp.where(ahead == a, groups[a], part)
            g_refs[k][...] = part.astype(bf16)
        dw_ref[...] = mm_tn(low, two_ref[...])
        for q in range(4):
            for xa in range(2):
                slot = ((place - gray(q)) & 3) * 2 + (x ^ xa)
                for half in range(2):
                    row = (q * 2 + xa) * 96 + half * HALF
                    block = dw_ref[row : row + HALF, :].astype(bf16)

                    @pl.when(c == half)
                    def _():
                        keep_ref[slot] = block

                    @pl.when(c != half)
                    def _():
                        send_ref[slot] = block

    outs = (
        [shape((256, D), f32), shape((8, D), f32)]
        + [shape((256, GROUP_WIDTH), bf16)] * 4
        + [shape((8, HALF, D), bf16)] * 2
    )
    got = call(
        body,
        "norm_out_back",
        [SMEM] + [VM] * 8,
        outs,
        (at, three, three_there, cotangent, normal, inverse, two, w_out, norms),
        [pltpu.VMEM((D, D), f32)],
    )
    return got[0], got[1], got[2:6], got[6], got[7]


FAR_AFTER = 3


def after(value, *others):
    return lax.optimization_barrier((value, *others))[0]


def turn(at, far_own, far_there, near_own, near_there):
    def body(at_ref, far_own_ref, far_there_ref, near_own_ref, near_there_ref, out_ref):
        def write_far(refs):
            for half, ref in enumerate(refs):
                for u in range(2):
                    for j in range(2):
                        row = u * 192 + j * 96
                        out_ref[4 + 4 * u + 2 * half + j] = jnp.transpose(ref[row : row + 96, :].astype(f32))

        def write_near(refs):
            for b in range(4):
                rows = slice(b * HALF, (b + 1) * HALF)
                block = jnp.concatenate([ref[rows, :].astype(f32) for ref in refs], axis=0)
                out_ref[b] = jnp.transpose(block)

        for value in range(2):

            @pl.when(at_ref[1] == value)
            def _():
                write_far((far_own_ref, far_there_ref)[:: 1 if value == 0 else -1])

            @pl.when(at_ref[2] == value)
            def _():
                write_near((near_own_ref, near_there_ref)[:: 1 if value == 0 else -1])

    return call(
        body,
        "turn",
        [SMEM] + [VM] * 4,
        shape((12, 192, 96), f32),
        (at, far_own, far_there, near_own, near_there),
        us=4,
    )


def sync(*values):
    return lax.optimization_barrier(values)


def add_low(a, b):
    return (a.astype(f32) + b.astype(f32)).astype(bf16)


def step_small(
    patches,
    cotangent,
    input_views,
    token_live,
    master,
    moment_one,
    moment_two,
    norm_params,
    norm_moment_one,
    norm_moment_two,
):
    tokens = patches.shape[0]
    rows, blocks, cols = master.shape
    dp = lax.axis_index("dp")
    seq = lax.axis_index("seq")
    quarter, x_place = seq // 2, seq % 2
    y_place, core = dp // 2, dp % 2
    place = gray(quarter)
    at = jnp.stack([x_place, y_place, core, place]).astype(jnp.int32)

    def to_core(value):
        return swap(value, "dp", 1)

    def to_y(value):
        return swap(value, "dp", 2)

    def to_x(value):
        return swap(value, "seq", 1)

    def by_core(first, second):
        return jnp.where(core == 0, first, second), jnp.where(core == 0, second, first)

    def by_y(first, second):
        return jnp.where(y_place == 0, first, second), jnp.where(y_place == 0, second, first)

    def own_y(value):
        return lax.dynamic_slice_in_dim(value, y_place * 384, 384, value.ndim - 1)

    def other_y(value):
        return lax.dynamic_slice_in_dim(value, (1 - y_place) * 384, 384, value.ndim - 1)

    master_t = jnp.transpose(master, (1, 0, 2))
    low_t = jnp.transpose(master_t.astype(bf16), (0, 2, 1))
    flags = jnp.pad(token_live.astype(bf16)[None, :], ((0, 7), (0, D - tokens)))
    out_block = jnp.pad(low_t[3], ((0, 0), (0, 256 - rows))).reshape(3, 32, 256)
    out_block = jnp.transpose(out_block, (1, 0, 2)).reshape(32, D)
    ring0 = jnp.concatenate([patches, flags, out_block], axis=0)
    near_halves = [low_t[0:3, h * HALF : (h + 1) * HALF].reshape(3 * HALF, rows) for h in range(2)]
    far_halves = [
        jnp.concatenate(
            [low_t[4 + 2 * h : 6 + 2 * h].reshape(2 * cols, rows), low_t[8 + 2 * h : 10 + 2 * h].reshape(2 * cols, rows)],
            axis=0,
        )
        for h in range(2)
    ]

    ring1, beside0 = hop_quarter(ring0, 1), to_x(ring0)
    own, other = by_core(*near_halves)
    near = jnp.concatenate(by_core(own, to_core(other)), axis=1)
    near = jnp.stack([near, to_x(near)])
    own, other = by_y(*far_halves)
    far0 = jnp.concatenate(by_y(own, to_y(other)), axis=1)
    ring1, beside0, near, far0 = sync(ring1, beside0, near, far0)

    ring2, beside1 = hop_quarter(ring1, 1), to_x(ring1)
    near = jnp.stack([near, to_y(near)])
    near_there = to_core(near)
    ring2, beside1, near, near_there = sync(ring2, beside1, near, near_there)

    ring3, beside2, cot_there = hop_quarter(ring2, 1), to_x(ring2), to_y(cotangent)
    w_qkv = place_qkv(at, near, near_there)
    got0 = list(project(ring0, beside0, w_qkv, norm_params))
    ring3, beside2, cot_there, first = sync(ring3, beside2, cot_there, got0[0])
    got0[0] = first

    beside3, far1 = to_x(ring3), hop_quarter(far0, 1)
    got1 = list(project(ring1, after(beside1, first), w_qkv, norm_params))
    got2 = list(project(ring2, beside2, w_qkv, norm_params))
    beside3, far1, got1[0], got2[0] = sync(beside3, far1, got1[0], got2[0])

    far2, far3 = hop_quarter(after(far1, beside3), 1), hop_quarter(after(far0, beside3), 3)
    far01 = jnp.stack([far0, far1])
    far01 = jnp.stack([far01, to_x(after(far01, beside3))], axis=1).reshape(4, 384, 384)
    out_own = jnp.stack([p[264:] for p in (ring0, beside0, ring1, beside1, ring2, beside2, ring3, beside3)])
    out_own = jnp.transpose(out_own.reshape(8, 32, 3, 256), (0, 2, 1, 3)).reshape(8, 96, 256)
    out_own = jnp.stack([out_own, to_y(out_own)])
    got3 = project(ring3, beside3, w_qkv, norm_params)
    acts, normals, qs, ks, vs = zip(got0, got1, got2, got3)
    mixed, full, q_back = attend(at, qs, ks, vs)
    mixed = list(mixed)
    *mixed, full, far2, far3, far01, out_own = sync(*mixed, full, far2, far3, far01, out_own)

    mixed = [mixed[0]] + [hop_quarter(mixed[4 - k], k) for k in (3, 2, 1)]
    far23 = jnp.stack([far2, far3])
    far23 = jnp.stack([far23, to_x(far23)], axis=1).reshape(4, 384, 384)
    w_out = place_out(at, out_own, to_core(out_own))
    *mixed, far23, w_out = sync(*mixed, far23, w_out)

    far01_there, far23_there = to_core(far01), to_core(far23)
    two, resid, normal_two, inverse_two, act_three = out_norm(at, patches, mixed, w_out, norm_params)
    w_mlp = (far01, far23, far01_there, far23_there)
    act_three, *w_mlp = sync(act_three, *w_mlp)

    act_there = to_y(act_three)
    hidden, wide, out_mine, three_mine = mlp(at, act_three, cotangent, w_mlp, f32)
    act_there, out_mine = sync(act_there, out_mine)
    hidden_there, wide_there, out_send, three_send = mlp(at, act_there, cot_there, w_mlp, bf16)
    three_send, hidden_there = sync(three_send, hidden_there)
    three_there = to_y(three_send)
    operands = (at, (act_three, act_there), (cotangent, cot_there), (hidden, hidden_there), (wide, wide_there))
    low_keep, low_send = mlp_weights(*operands, (1, 2))
    low_there = to_core(low_send)
    high_keep, high_send = mlp_weights(*operands, (3, 0))
    three_there, low_there, high_send = sync(three_there, low_there, high_send)

    low_sum = add_low(low_keep, low_there)
    low_x = to_x(low_sum[1])
    high_there = to_core(high_send)
    grad_resid, sums_two, parts, w_out_keep, w_out_send = norm_out_back(
        at, three_mine, three_there, cotangent, normal_two, inverse_two, two, w_out, norm_params
    )
    *parts, w_out_send, high_there = sync(*parts, w_out_send, high_there)

    grads = [parts[0]] + [hop_quarter(parts[k], k) for k in (1, 2, 3)]
    high_sum = add_low(high_keep, high_there)
    out_sum = add_low(w_out_keep, to_core(w_out_send))
    out_sum = add_low(own_y(out_sum), to_y(other_y(out_sum))).reshape(4, 2, HALF, 384)
    *grads, low_x, high_sum, out_sum = sync(*grads, low_x, high_sum, out_sum)

    low_half = add_low(low_sum[0], low_x)
    far_got = [hop_quarter(low_half[0], -1), hop_quarter(low_half[1], -2)]
    high_half = add_low(high_sum[0], to_x(high_sum[1]))
    out_sum = add_low(out_sum[:, 0], to_x(out_sum[:, 1]))
    dqs, dks, dvs = attend_back(at, q_back, ks, vs, full, grads)
    dqs = list(dqs)
    dqs[1], high_half, out_sum = sync(dqs[1], high_half, out_sum)

    last = hop_quarter(jnp.concatenate([high_half[0], out_sum[3]], axis=0), -3)
    out_got = [hop_quarter(out_sum[1], -1), hop_quarter(out_sum[2], -2), last[384:]]
    far_got = [*far_got, last[:384]]
    one, sums_one = {}, []
    for ks_here in ((1, 2), (3, 0)):
        keep, send, sums = input_back(*([m[k] for k in ks_here] for m in (normals, dqs, dks, dvs)), w_qkv)
        dqs[0], dqs[3] = after(dqs[0], keep[0]), after(dqs[3], keep[0])
        sums_one.append(sums)
        for k, a, b in zip(ks_here, keep, send):
            one[k] = (a, b)
    near_keep, near_send = projections_back(at, acts, dqs, dks, dvs)
    one1 = to_x(one[1][1])
    one2 = to_x(after(one[2][1], one[0][0]))
    out_there = to_y(after(out_send, near_keep))
    block_out = (resid + out_mine + out_there.astype(f32)).astype(bf16)
    one1, near_send, *far_got = sync(one1, near_send, *far_got)
    far_sum = high_half[1].astype(f32)
    for part in far_got:
        far_sum = far_sum + part.astype(f32)
    out_sum = out_sum[0].astype(f32)
    for part in out_got:
        out_sum = out_sum + part.astype(f32)

    one_ring = hop_quarter(add_low(one[1][0], one1), 1)
    one_ring = hop_quarter(add_low(one_ring, add_low(one[2][0], one2)), 1)
    near_sum = add_low(near_keep, to_core(near_send))
    near_sum = add_low(own_y(near_sum), to_y(other_y(near_sum)))
    near_x = to_x(near_sum[3:6])
    one3 = add_low(one[3][0], to_x(after(one[3][1], near_x)))
    one0 = add_low(one[0][0], to_x(after(one[0][1], near_x)))
    one_ring = hop_quarter(add_low(one_ring, one3), 1)
    grad_one = one_ring.astype(f32) + one0.astype(f32)
    normal_one, inverse_one = layer_stats(patches.astype(f32))
    patches_grad = grad_resid + layer_back(grad_one, normal_one, inverse_one, norm_params[0])
    param_grad = jnp.concatenate([sums_one[0][0:2] + sums_one[1][0:2], sums_two[0:2]], axis=0)

    near_sum = near_sum[0:3].astype(f32) + near_x.astype(f32)
    near_sum = jnp.concatenate([near_sum.reshape(3 * HALF, 2 * rows), out_sum], axis=0)
    far_own, far_other = by_y(far_sum[:, :rows], far_sum[:, rows:])
    near_own, near_other = by_core(near_sum[:, :rows], near_sum[:, rows:])
    weight_grad = turn(at, far_own, to_y(far_other.astype(bf16)), near_own, to_core(near_other.astype(bf16)))
    squares = jnp.full((4, D), jnp.sum(far_sum * far_sum) + jnp.sum(near_sum * near_sum), f32)
    sums = jnp.concatenate([param_grad, squares], axis=0)
    for by in (1, 2):
        sums = sums + hop_quarter(sums, by)
    sums = sums + swap(sums, "seq", 1)
    sums = after(sums, weight_grad)
    sums = sums + swap(sums, "dp", 2)
    sums = sums + swap(sums, "dp", 1)
    param_grad = sums[0:4]
    squares = sums[4, 0] + jnp.sum(param_grad * param_grad)
    grad_norm = jnp.sqrt(squares)
    clip = 1.0 / jnp.maximum(grad_norm, 1.0)
    moments = jnp.transpose(moment_one, (1, 0, 2)), jnp.transpose(moment_two, (1, 0, 2))
    new_master, *moments = adam_step(master_t, weight_grad * clip, *moments, rate_matrix, weight_decay)
    new_master, new_copy, new_moment_one, new_moment_two = (
        jnp.transpose(m, (1, 0, 2)) for m in (new_master, new_master.astype(bf16), *moments)
    )
    new_norm_params, new_norm_moment_one, new_norm_moment_two = adam_step(
        norm_params, param_grad * clip, norm_moment_one, norm_moment_two, rate_vector, 0.0
    )
    return (
        block_out,
        patches_grad,
        new_master,
        new_copy,
        new_moment_one,
        new_moment_two,
        new_norm_params,
        new_norm_moment_one,
        new_norm_moment_two,
        grad_norm,
    )


def solution(mesh):
    tokens = P(("dp", "seq"), None)
    weights = P("dp", None, "seq")
    small = mesh.shape["dp"] == 4 and mesh.shape["seq"] == 8
    return jax.shard_map(
        step_small if small else step_general,
        mesh=mesh,
        in_specs=(tokens, tokens, P("dp"), P(("dp", "seq")), weights, weights, weights, P(), P(), P()),
        out_specs=(tokens, tokens, weights, weights, weights, weights, P(), P(), P(), P()),
        check_vma=False,
    )
```

```python
import math
from functools import partial

import jax
import jax.numpy as jnp
from jax import lax
from jax.experimental import pallas as pl
from jax.experimental.pallas import tpu as pltpu
from jax.sharding import PartitionSpec as P

D = 768
HEADS = 12
HEAD_DIM = 64
FF = 3072
VIEW = 1024
STEP = 10
GROUPS = 4
GROUP_HEADS = HEADS // GROUPS
GROUP_WIDTH = GROUP_HEADS * HEAD_DIM
WIDE = FF // D
RING = (0, 1, 3, 2)

layer_eps = 1e-05
beta_first = 0.9
beta_second = 0.95
adam_eps = 1e-08
rate_matrix = 0.08
rate_vector = 0.8
weight_decay = 0.1
masked_score = -1e30
bf16 = jnp.bfloat16
f32 = jnp.float32


def gray(v):
    return v ^ (v >> 1)


def hop_quarter(value, by):
    split = lax.axis_size("seq") // GROUPS
    pairs = [
        (RING[p] * split + x, RING[(p + by) % GROUPS] * split + x) for p in range(GROUPS) for x in range(split)
    ]
    return lax.ppermute(value, "seq", pairs)


def hop_within(value, by):
    split = lax.axis_size("seq") // GROUPS
    pairs = [(q * split + x, q * split + (x + by) % split) for q in range(GROUPS) for x in range(split)]
    return lax.ppermute(value, "seq", pairs)


def swap(value, axis, bit):
    return lax.ppermute(value, axis, [(i, i ^ bit) for i in range(lax.axis_size(axis))])


def bits_of(axis):
    return [1 << b for b in range(lax.axis_size(axis).bit_length() - 1)]


def total(value):
    for axis in ("dp", "seq"):
        for bit in bits_of(axis):
            value = value + swap(value, axis, bit)
    return value


def pick(stack, index):
    return lax.dynamic_index_in_dim(stack, index, 0, keepdims=False)


def layer_stats(values):
    centre = jnp.mean(values, axis=-1, keepdims=True)
    shifted = values - centre
    spread = jnp.mean(shifted * shifted, axis=-1, keepdims=True)
    inverse = lax.rsqrt(spread + layer_eps)
    return (shifted * inverse, inverse)


def layer_back(grad_normed, normalized, inverse, gain):
    scaled = grad_normed * gain
    centred = jnp.mean(scaled, axis=-1, keepdims=True)
    along = jnp.mean(scaled * normalized, axis=-1, keepdims=True)
    return inverse * (scaled - centred - normalized * along)


def mm(a, b):
    return jnp.dot(a, b, preferred_element_type=f32)


def mm_nt(a, b):
    return lax.dot_general(a, b, (((1,), (1,)), ((), ())), preferred_element_type=f32)


def mm_tn(a, b):
    return lax.dot_general(a, b, (((0,), (0,)), ((), ())), preferred_element_type=f32)


def gather_rows(piece):
    for bit in reversed(bits_of("dp")):
        piece = jnp.concatenate([piece, swap(piece, "dp", bit)], axis=1)
    return piece


def row_order():
    order = [0]
    for bit in reversed(bits_of("dp")):
        order = order + [o ^ bit for o in order]
    return order


def reduce_rows(piece):
    for bit in bits_of("dp"):
        half = piece.shape[1] // 2
        there = swap(piece[:, half:], "dp", bit)
        piece = (piece[:, :half].astype(f32) + there.astype(f32)).astype(bf16)
    return piece


def reduce_within(piece):
    own = piece[0].astype(f32)
    for j in range(1, piece.shape[0]):
        own = own + hop_within(piece[j], -j).astype(f32)
    return own.astype(bf16)


def reduce_ring(slots):
    moving = slots[1]
    for k in (2, 3):
        moving = (hop_quarter(moving, 1).astype(f32) + slots[k].astype(f32)).astype(bf16)
    return hop_quarter(moving, 1).astype(f32) + slots[0].astype(f32)


def adam_step(params, grads, first, second, rate, decay):
    first_new = beta_first * first + (1.0 - beta_first) * grads
    second_new = beta_second * second + (1.0 - beta_second) * grads * grads
    first_hat = first_new / (1.0 - beta_first**STEP)
    second_hat = second_new / (1.0 - beta_second**STEP)
    params_new = params - rate * (first_hat / (jnp.sqrt(second_hat) + adam_eps) + decay * params)
    return (params_new, first_new, second_new)


def relative(dp, absolute, order):
    index = jnp.int32(0)
    for at, offset in enumerate(order):
        index = jnp.where((dp ^ absolute) == offset, at, index)
    return index


def step_general(
    patches,
    cotangent,
    input_views,
    token_live,
    master,
    moment_one,
    moment_two,
    norm_params,
    norm_moment_one,
    norm_moment_two,
):
    tokens = patches.shape[0]
    rows, blocks, cols = master.shape
    n_dp = lax.axis_size("dp")
    split = lax.axis_size("seq") // GROUPS
    dp = lax.axis_index("dp")
    seq = lax.axis_index("seq")
    quarter, within = seq // split, seq % split
    place = gray(quarter)
    inputs_seen = input_views[0]
    gain_one, shift_one, gain_two, shift_two = (norm_params[i] for i in range(4))
    order = row_order()
    dp_place = [order.index(a) for a in range(n_dp)]

    def quarter_behind(k):
        return gray((place - k) & 3)

    flags = jnp.pad(token_live.astype(bf16)[None, :], ((0, 7), (0, D - tokens)))
    ring = [jnp.concatenate([patches, flags], axis=0)]
    for _ in range(3):
        ring.append(hop_quarter(ring[-1], 1))
    pieces = [[ring[k]] + [hop_within(ring[k], j) for j in range(1, split)] for k in range(4)]
    scene = jnp.stack([jnp.stack([p[:tokens] for p in pieces[k]]) for k in range(4)])
    live = jnp.stack([jnp.concatenate([p[tokens, :tokens] for p in pieces[k]]) for k in range(4)])

    copy_low = master.astype(bf16)
    mine = copy_low[:, 0:3, :].reshape(rows, 3 * cols)
    near = jnp.stack([mine] + [hop_within(mine, j) for j in range(1, split)])
    near = gather_rows(near).reshape(split, n_dp, rows, 3, cols)
    near = jnp.stack([pick(near, (within - a) % split) for a in range(split)])
    near = jnp.moveaxis(near, 1, 0)
    near = jnp.stack([pick(near, order_at) for order_at in [relative(dp, a, order) for a in range(n_dp)]])
    w_qkv = jnp.transpose(near, (0, 2, 3, 1, 4)).reshape(D, 3, GROUP_WIDTH)

    up = copy_low[:, 4 : 4 + WIDE].reshape(rows, WIDE * cols)
    down = copy_low[:, 4 + WIDE :].reshape(rows, WIDE * cols)
    far = [jnp.concatenate([up, down, copy_low[:, 3]], axis=1)]
    for _ in range(3):
        far.append(hop_quarter(far[-1], 1))
    weights = [gather_rows(jnp.stack([f] + [hop_within(f, j) for j in range(1, split)])) for f in far]
    width = WIDE * cols
    w_up = [w[:, :, :width] for w in weights]
    w_down = [w[:, :, width : 2 * width] for w in weights]
    w_out = jnp.stack([w[:, :, 2 * width :] for w in weights]).reshape(4 * split, n_dp, rows, cols)

    def slot_of(quarter_abs, within_abs):
        return ((place - gray(quarter_abs)) & 3) * split + (within - within_abs) % split

    w_out = jnp.stack([pick(w_out, slot_of(a // split, a % split)) for a in range(4 * split)])
    w_out = jnp.moveaxis(w_out, 1, 0)
    w_out = jnp.stack([pick(w_out, relative(dp, a, order)) for a in range(n_dp)])
    w_out = jnp.transpose(w_out, (0, 2, 1, 3)).reshape(D, D)

    normal_one, inverse_one = layer_stats(scene.astype(f32))
    act_one = (normal_one * gain_one + shift_one).astype(bf16)
    act_all = act_one.reshape(4 * split * tokens, D)
    act_own = act_one[:, 0].reshape(4 * tokens, D)
    q = mm(act_own, w_qkv[:, 0]).astype(bf16)
    k = mm(act_all, w_qkv[:, 1]).astype(bf16)
    v = mm(act_all, w_qkv[:, 2]).astype(bf16)

    def heads(m):
        return jnp.transpose(m.reshape(m.shape[0], GROUP_HEADS, HEAD_DIM), (1, 0, 2))

    def unheads(m):
        return jnp.transpose(m, (1, 0, 2)).reshape(m.shape[1], GROUP_WIDTH)

    views = jnp.stack([(quarter_behind(i) * split * tokens) // VIEW for i in range(4)])
    open_block = (views[None, :] < inputs_seen) | (views[None, :] == views[:, None])
    visible = open_block[:, None, :, None] & (live > 0)[None, None]
    visible = jnp.broadcast_to(visible, (4, tokens, 4, split * tokens)).reshape(4 * tokens, -1)
    scaling = 1.0 / math.sqrt(HEAD_DIM)
    qh, kh, vh = heads(q), heads(k), heads(v)
    scores = jnp.einsum("hqd,hkd->hqk", qh, kh, preferred_element_type=f32) * scaling
    scores = jnp.where(visible[None], scores, masked_score)
    top = jnp.max(scores, axis=-1, keepdims=True)
    probs = jnp.where(visible[None], jnp.exp(scores - top), 0.0)
    probs = probs / jnp.sum(probs, axis=-1, keepdims=True)
    probs_low = probs.astype(bf16)
    attended = jnp.einsum("hqk,hkd->hqd", probs_low, vh, preferred_element_type=f32)
    flat = unheads(attended).astype(bf16).reshape(4, tokens, GROUP_WIDTH)
    back = jnp.stack([flat[0]] + [hop_quarter(flat[i], -i) for i in range(1, 4)])
    act_two = jnp.concatenate([pick(back, (gray(a) - place) & 3) for a in range(4)], axis=1)

    patch_float = patches.astype(f32)
    resid = patch_float + mm(act_two, w_out)
    normal_two, inverse_two = layer_stats(resid)
    act_three = (normal_two * gain_two + shift_two).astype(bf16)

    def to_relative(m):
        parts = m.reshape(tokens, n_dp, rows)
        return jnp.concatenate([lax.dynamic_index_in_dim(parts, dp ^ o, 1, keepdims=False) for o in order], axis=1)

    def from_relative(m):
        parts = m.reshape(tokens, n_dp, rows)
        return jnp.concatenate(
            [lax.dynamic_index_in_dim(parts, relative(dp, a, order), 1, keepdims=False) for a in range(n_dp)], axis=1
        )

    act_rel = to_relative(act_three)
    cot_rel = to_relative(cotangent)
    branch_rel = jnp.zeros((tokens, D), f32)
    three_rel = jnp.zeros((tokens, D), f32)
    far_grads = []
    for i in range(4):
        group = []
        for j in range(split):
            widened = mm(act_rel, w_up[i][j])
            activated, gelu_pull = jax.vjp(partial(jax.nn.gelu, approximate=False), widened)
            hidden = activated.astype(bf16)
            branch_rel = branch_rel + mm_nt(hidden, w_down[i][j])
            grad_wide = gelu_pull(mm(cot_rel, w_down[i][j]))[0].astype(bf16)
            three_rel = three_rel + mm_nt(grad_wide, w_up[i][j])
            grad_up = mm_tn(act_rel, grad_wide).astype(bf16)
            grad_down = mm_tn(cot_rel, hidden).astype(bf16)
            group.append((grad_up, grad_down))
        far_grads.append(group)
    block_out = (resid + from_relative(branch_rel)).astype(bf16)
    grad_three = from_relative(three_rel)
    gain_two_grad = jnp.sum(grad_three * normal_two, axis=0)
    shift_two_grad = jnp.sum(grad_three, axis=0)
    grad_resid = cotangent.astype(f32) + layer_back(grad_three, normal_two, inverse_two, gain_two)
    grad_branch = grad_resid.astype(bf16)
    grad_attended = mm_nt(grad_branch, w_out).astype(bf16)
    grad_w_out = mm_tn(act_two, grad_branch).astype(bf16)

    parts = jnp.transpose(grad_attended.reshape(tokens, 4, GROUP_WIDTH), (1, 0, 2))
    parts = [pick(parts, gray((place + i) & 3)) for i in range(4)]
    grad_here = jnp.concatenate([parts[0]] + [hop_quarter(parts[i], i) for i in range(1, 4)], axis=0)
    gh = heads(grad_here)
    dprobs = jnp.einsum("hqd,hkd->hqk", gh, vh, preferred_element_type=f32)
    delta = jnp.sum(gh.astype(f32) * attended, axis=-1, keepdims=True)
    grad_scores = (probs * (dprobs - delta)).astype(bf16)
    dq = unheads(jnp.einsum("hqk,hkd->hqd", grad_scores, kh, preferred_element_type=f32) * scaling).astype(bf16)
    dk = unheads(jnp.einsum("hqk,hqd->hkd", grad_scores, qh, preferred_element_type=f32) * scaling).astype(bf16)
    dv = unheads(jnp.einsum("hqk,hqd->hkd", probs_low, gh, preferred_element_type=f32)).astype(bf16)

    grad_near = jnp.stack([mm_tn(act_own, dq), mm_tn(act_all, dk), mm_tn(act_all, dv)], axis=1).astype(bf16)
    grad_near = grad_near.reshape(n_dp, rows, 3, split, cols)
    grad_near = jnp.stack([pick(grad_near, dp ^ o) for o in order])
    grad_near = jnp.transpose(grad_near, (3, 0, 1, 2, 4)).reshape(split, D, 3 * cols)
    grad_near = jnp.stack([pick(grad_near, (within - j) % split) for j in range(split)])
    grad_near = reduce_within(reduce_rows(grad_near)).astype(f32).reshape(rows, 3, cols)

    one_q = mm_nt(dq, w_qkv[:, 0]).reshape(4, 1, tokens, D)
    one_kv = (mm_nt(dk, w_qkv[:, 1]) + mm_nt(dv, w_qkv[:, 2])).reshape(4, split, tokens, D)
    one = jnp.concatenate([one_kv[:, :1] + one_q, one_kv[:, 1:]], axis=1)
    gain_one_grad = jnp.sum(one * normal_one, axis=(0, 1, 2))
    shift_one_grad = jnp.sum(one, axis=(0, 1, 2))
    one_low = one.astype(bf16)
    grad_one = reduce_ring([reduce_within(one_low[i]) for i in range(4)])
    patches_grad = grad_resid + layer_back(grad_one, normal_one[0, 0], inverse_one[0, 0], gain_one)

    out_parts = grad_w_out.reshape(n_dp, rows, 4 * split, cols)
    out_parts = jnp.stack([pick(out_parts, dp ^ o) for o in order])
    out_parts = jnp.transpose(out_parts, (2, 0, 1, 3)).reshape(4 * split, D, cols)
    slots = []
    for i in range(4):
        stack = []
        for j in range(split):
            own_out = pick(out_parts, quarter_behind(i) * split + (within - j) % split)
            stack.append(jnp.concatenate([*far_grads[i][j], own_out], axis=1))
        slots.append(reduce_within(reduce_rows(jnp.stack(stack))))
    far_sum = reduce_ring(slots)
    grad_up = far_sum[:, :width].reshape(rows, WIDE, cols)
    grad_down = far_sum[:, width : 2 * width].reshape(rows, WIDE, cols)
    grad_out = far_sum[:, 2 * width :].reshape(rows, 1, cols)

    weight_grad = jnp.concatenate([grad_near, grad_out, grad_up, grad_down], axis=1)
    param_grad = total(jnp.stack([gain_one_grad, shift_one_grad, gain_two_grad, shift_two_grad]))
    squares = total(jnp.full((8, 128), jnp.sum(weight_grad * weight_grad), f32))[0, 0] + jnp.sum(param_grad * param_grad)
    grad_norm = jnp.sqrt(squares)
    clip = 1.0 / jnp.maximum(grad_norm, 1.0)
    new_master, new_moment_one, new_moment_two = adam_step(
        master, weight_grad * clip, moment_one, moment_two, rate_matrix, weight_decay
    )
    new_norm_params, new_norm_moment_one, new_norm_moment_two = adam_step(
        norm_params, param_grad * clip, norm_moment_one, norm_moment_two, rate_vector, 0.0
    )
    return (
        block_out,
        patches_grad,
        new_master,
        new_master.astype(bf16),
        new_moment_one,
        new_moment_two,
        new_norm_params,
        new_norm_moment_one,
        new_norm_moment_two,
        grad_norm,
    )


HALF = 48
ANY = pl.BlockSpec(memory_space=pl.ANY)
SMEM = pl.BlockSpec(memory_space=pltpu.SMEM)
VMEM_LIMIT = 20
SCALE = 0.1


def call(body, name, ins, outs, operands, scratch=(), us=4, out_specs=None, aliases=None, mem=None):
    return pl.pallas_call(
        body,
        name=name,
        out_shape=outs,
        in_specs=ins,
        out_specs=out_specs or jax.tree.map(lambda _: pl.BlockSpec(memory_space=pltpu.VMEM), outs),
        scratch_shapes=list(scratch),
        input_output_aliases=aliases or {},
        cost_estimate=pl.CostEstimate(flops=int(us * SCALE * 1e9), bytes_accessed=int(us * SCALE * 3.6e6), transcendentals=0),
        compiler_params=pltpu.CompilerParams(vmem_limit_bytes=(mem or VMEM_LIMIT) << 20),
    )(*operands)


VM = pl.BlockSpec(memory_space=pltpu.VMEM)


def shape(dims, dtype):
    return jax.ShapeDtypeStruct(dims, dtype)


def run_copies(copies):
    for c in copies:
        c.start()
    for c in copies:
        c.wait()


def place_qkv(at, own_half, other_half):
    def body(at_ref, own_ref, other_ref, out_ref, sems):
        x, y, c = at_ref[0], at_ref[1], at_ref[2]
        copies = []
        for block in range(3):
            for j in range(2):
                for r in range(2):
                    for h, ref in ((0, own_ref), (1, other_ref)):
                        row = block * GROUP_WIDTH + (x ^ j) * 96 + (c ^ h) * HALF
                        copies.append(
                            pltpu.make_async_copy(
                                ref.at[r, j, pl.ds(block * HALF, HALF), :],
                                out_ref.at[
                                    pl.ds(pl.multiple_of(row, 16), HALF),
                                    pl.ds(pl.multiple_of((y ^ r) * 384, 128), 384),
                                ],
                                sems.at[len(copies)],
                            )
                        )
        run_copies(copies)

    return call(
        body,
        "place_qkv",
        [SMEM, ANY, ANY],
        shape((3 * GROUP_WIDTH, D), bf16),
        (at, own_half, other_half),
        [pltpu.SemaphoreType.DMA((24,))],
    )


def place_out(at, own_half, other_half):
    def body(at_ref, own_ref, other_ref, out_ref, sems):
        x, y, c, place = at_ref[0], at_ref[1], at_ref[2], at_ref[3]
        copies = []
        for k in range(4):
            quarter = gray((place - k) & 3)
            for j in range(2):
                for r in range(2):
                    for h, ref in ((0, own_ref), (1, other_ref)):
                        row = (quarter * 2 + (x ^ j)) * 96
                        copies.append(
                            pltpu.make_async_copy(
                                ref.at[r, k * 2 + j],
                                out_ref.at[(y ^ r) * 2 + (c ^ h), pl.ds(pl.multiple_of(row, 16), 96), :],
                                sems.at[len(copies)],
                            )
                        )
        run_copies(copies)

    return call(
        body,
        "place_out",
        [SMEM, ANY, ANY],
        shape((4, D, 256), bf16),
        (at, own_half, other_half),
        [pltpu.SemaphoreType.DMA((32,))],
        us=3,
    )


def normalize(values):
    centre = jnp.mean(values, axis=-1, keepdims=True)
    shifted = values - centre
    inverse = lax.rsqrt(jnp.mean(shifted * shifted, axis=-1, keepdims=True) + layer_eps)
    return shifted * inverse, inverse


def lane_index(dims):
    return lax.broadcasted_iota(jnp.int32, dims, len(dims) - 1)


def project(first, second, w_t, norms):
    def body(a_ref, b_ref, w_ref, norm_ref, act_ref, normal_ref, q_ref, k_ref, v_ref, out_ref, wide_ref):
        wide_ref[...] = jnp.zeros_like(wide_ref)
        for h in range(9):
            wide_ref[h * 128 : h * 128 + 64, :] = w_ref[h * 64 : h * 64 + 64, :]
        gain, shift = norm_ref[0:1, :], norm_ref[1:2, :]
        for piece, ref in enumerate((a_ref, b_ref)):
            at = slice(piece * 256, piece * 256 + 256)
            normal, _ = normalize(ref[0:256, :].astype(f32))
            act = (normal * gain + shift).astype(bf16)
            normal_ref[at, :] = normal.astype(bf16)
            act_ref[at, :] = act
            for n in range(3):
                out_ref[piece, n * 32 : n * 32 + 32, :] = ref[264:296, n * 256 : n * 256 + 256]
            flags = ref[256:257, 0:256].astype(f32)
            mask = jnp.where(flags > 0, 0.0, masked_score)
            mask = jnp.transpose(jnp.broadcast_to(mask, (128, 256)))
            lanes = lane_index((256, 128))
            for h in range(3):
                if piece == 0:
                    q = mm_nt(act, wide_ref[h * 128 : h * 128 + 128, :]).astype(bf16).astype(f32)
                    q = jnp.where(lanes == 64, 1.0, q * (1.0 / math.sqrt(HEAD_DIM)))
                    q_ref[h] = q.astype(bf16)
                k = mm_nt(act, wide_ref[(3 + h) * 128 : (4 + h) * 128, :])
                k = jnp.where(lanes == 64, mask, k)
                k_ref[h, at, :] = jnp.where((lanes > 64) & (lanes < 68), 1.0, k).astype(bf16)
                v = mm_nt(act, wide_ref[(6 + h) * 128 : (7 + h) * 128, :])
                v_ref[h, at, :] = jnp.where((lanes > 63) & (lanes < 67), 1.0, v).astype(bf16)

    outs = [
        shape((512, D), bf16),
        shape((512, D), bf16),
        shape((3, 256, 128), bf16),
        shape((3, 512, 128), bf16),
        shape((3, 512, 128), bf16),
        shape((2, 96, 256), bf16),
    ]
    return call(body, "norm_project", [VM] * 4, outs, (first, second, w_t, norms), [pltpu.VMEM((1152, D), bf16)], us=4)


def in_three(value):
    high = value.astype(bf16).astype(f32)
    rest = value - high
    mid = rest.astype(bf16).astype(f32)
    return high, mid, rest - mid


def with_parts(base, lanes, first, value):
    for i, part in enumerate(in_three(value)):
        base = jnp.where(lanes == first + i, part, base)
    return base


def join_heads(parts):
    return jnp.concatenate([p[:, :HEAD_DIM] for p in parts], axis=1)


def stack_slots(place, slots, stacked, sems, base=0):
    return [
        pltpu.make_async_copy(ref, stacked.at[gray((place - k) & 3)], sems.at[base + k]) for k, ref in enumerate(slots)
    ]


def attend(at, qs, ks, vs):
    def body(at_ref, *refs):
        low_refs, full_ref, back_ref = refs[12:16], refs[16], refs[17]
        q_ref, k_ref, v_ref, sems = refs[18:22]
        place = at_ref[3]
        lanes = lane_index((256, 128))
        run_copies(
            stack_slots(place, refs[0:4], q_ref, sems)
            + stack_slots(place, refs[4:8], k_ref, sems, 4)
            + stack_slots(place, refs[8:12], v_ref, sems, 8)
        )

        def head(h, _):
            for i in range(4):
                chunks = (0, 1) if i < 2 else (0, 1, 2, 3)
                q = q_ref[i, h]
                scores = [mm_nt(q, k_ref[c, h]) for c in chunks]
                top = None
                for s in scores:
                    for b in range(0, s.shape[1], 128):
                        part = s[:, b : b + 128]
                        top = part if top is None else jnp.maximum(top, part)
                top = jnp.max(top, axis=1, keepdims=True)
                mixed = None
                for s, c in zip(scores, chunks):
                    part = mm(jnp.exp(s - top).astype(bf16), v_ref[c, h])
                    mixed = part if mixed is None else mixed + part
                norm = mixed[:, HEAD_DIM : HEAD_DIM + 1]
                full_ref[i, h] = mixed / norm
                logsum = top + jnp.log(norm)
                back_ref[i, h] = with_parts(q.astype(f32), lanes, 65, -logsum).astype(bf16)
            return 0

        lax.fori_loop(0, 3, head, 0)
        for k in range(4):
            i = gray((place - k) & 3)
            low_refs[k][...] = join_heads([full_ref[i, h] for h in range(3)]).astype(bf16)

    outs = (
        [shape((256, GROUP_WIDTH), bf16)] * 4 + [shape((4, 3, 256, 128), f32)] + [shape((4, 3, 256, 128), bf16)]
    )
    got = call(
        body,
        "attend",
        [SMEM] + [ANY] * 12,
        outs,
        (at, *qs, *ks, *vs),
        [
            pltpu.VMEM((4, 3, 256, 128), bf16),
            pltpu.VMEM((4, 3, 512, 128), bf16),
            pltpu.VMEM((4, 3, 512, 128), bf16),
            pltpu.SemaphoreType.DMA((12,)),
        ],
        us=12,
    )
    return got[0:4], got[4], got[5]


def attend_back(at, q_back, ks, vs, full, grads):
    def body(at_ref, q_ref, *refs):
        full_ref, g_refs = refs[8], refs[9:13]
        dq_refs, dk_refs, dv_refs = refs[13:17], refs[17:21], refs[21:25]
        k_ref, v_ref, g_ref, dq_ref, dk_ref, dv_ref, sems = refs[25:32]
        place = at_ref[3]
        copies = stack_slots(place, refs[0:4], k_ref, sems) + stack_slots(place, refs[4:8], v_ref, sems, 4)
        for c in copies:
            c.start()
        lanes = lane_index((256, 128))
        for k in range(4):
            i = gray((place - k) & 3)
            for h in range(3):
                g = g_refs[k][:, h * 64 : h * 64 + 64].astype(f32)
                delta = jnp.sum(g * full_ref[i, h][:, :64], axis=-1, keepdims=True)
                g = jnp.concatenate([g, jnp.zeros((256, 64), f32)], axis=1)
                g_ref[h, pl.ds(pl.multiple_of(i * 256, 256), 256), :] = with_parts(g, lanes, 64, -delta).astype(bf16)
        for c in copies:
            c.wait()

        def head(h, _):
            q_all = jnp.concatenate([q_ref[i, h] for i in range(4)], axis=0)
            for c in range(4):
                first = 0 if c < 2 else 512
                k, v = k_ref[c, h], v_ref[c, h]
                q, g = q_all[first:], g_ref[h, first:, :]
                p = jnp.exp(mm_nt(k, q))
                ds = (p * mm_nt(v, g)).astype(bf16)
                dv_ref[c, h] = mm(p.astype(bf16), g)
                dk_ref[c, h] = mm(ds, q)
                dq = mm(jnp.transpose(k), ds)
                if c == 0:
                    dq_ref[h] = dq
                else:
                    dq_ref[h, :, first:] += dq
            return 0

        lax.fori_loop(0, 3, head, 0)
        for k in range(4):
            i = gray((place - k) & 3)
            cols = pl.ds(pl.multiple_of(i * 256, 256), 256)
            parts = [jnp.transpose(dq_ref[h, :, cols]) for h in range(3)]
            dq_refs[k][...] = (join_heads(parts) * (1.0 / math.sqrt(HEAD_DIM))).astype(bf16)
            dk_refs[k][...] = join_heads([dk_ref[i, h] for h in range(3)]).astype(bf16)
            dv_refs[k][...] = join_heads([dv_ref[i, h] for h in range(3)]).astype(bf16)

    outs = [shape((256, GROUP_WIDTH), bf16)] * 4 + [shape((512, GROUP_WIDTH), bf16)] * 8
    got = call(
        body,
        "attend_back",
        [SMEM, VM] + [ANY] * 8 + [VM] * 5,
        outs,
        (at, q_back, *ks, *vs, full, *grads),
        [
            pltpu.VMEM((4, 3, 512, 128), bf16),
            pltpu.VMEM((4, 3, 512, 128), bf16),
            pltpu.VMEM((3, 1024, 128), bf16),
            pltpu.VMEM((3, 128, 1024), f32),
            pltpu.VMEM((4, 3, 512, 128), f32),
            pltpu.VMEM((4, 3, 512, 128), f32),
            pltpu.SemaphoreType.DMA((8,)),
        ],
        us=16,
        mem=32,
    )
    return got[0:4], got[4:8], got[8:12]


def input_back(normals, dqs, dks, dvs, w_t):
    count = len(normals)

    def body(*refs):
        normal_refs, dq_refs, dk_refs, dv_refs = (refs[n * count : (n + 1) * count] for n in range(4))
        w_ref, *outs = refs[4 * count :]
        keep_refs, send_refs, norm_ref = outs[0:count], outs[count : 2 * count], outs[2 * count]
        gains, shifts = jnp.zeros((1, D), f32), jnp.zeros((1, D), f32)
        for i in range(count):
            for j, out_ref in enumerate((keep_refs[i], send_refs[i])):
                r = slice(j * 256, j * 256 + 256)
                one = mm(dk_refs[i][r, :], w_ref[192:384, :]) + mm(dv_refs[i][r, :], w_ref[384:576, :])
                if j == 0:
                    one = one + mm(dq_refs[i][...], w_ref[0:192, :])
                gains = gains + jnp.sum(one * normal_refs[i][r, :].astype(f32), axis=0, keepdims=True)
                shifts = shifts + jnp.sum(one, axis=0, keepdims=True)
                out_ref[...] = one.astype(bf16)
        norm_ref[...] = jnp.concatenate([gains, shifts, jnp.zeros((6, D), f32)], axis=0)

    outs = [shape((256, D), bf16)] * (2 * count) + [shape((8, D), f32)]
    got = call(body, "input_back", [VM] * (4 * count + 1), outs, (*normals, *dqs, *dks, *dvs, w_t), us=count + 1)
    return got[0:count], got[count : 2 * count], got[2 * count]


def projections_back(at, acts, dqs, dks, dvs):
    def body(at_ref, *refs):
        act_refs, dq_refs, dk_refs, dv_refs = (refs[4 * n : 4 * n + 4] for n in range(4))
        w_keep_ref, w_send_ref, dw_ref = refs[16:19]
        for i in range(4):
            act = act_refs[i][...]
            for b, (ref, rows) in enumerate(((dq_refs[i], 256), (dk_refs[i], 512), (dv_refs[i], 512))):
                part = mm_tn(ref[...], act[:rows])
                at_rows = slice(b * GROUP_WIDTH, (b + 1) * GROUP_WIDTH)
                dw_ref[at_rows, :] = part if i == 0 else dw_ref[at_rows, :] + part
        x, c = at_ref[0], at_ref[2]
        for b in range(3):
            for xa in range(2):
                for half in range(2):
                    row = b * GROUP_WIDTH + (xa * 2 + half) * HALF
                    block = dw_ref[row : row + HALF, :].astype(bf16)

                    @pl.when(c == half)
                    def _():
                        w_keep_ref[(x ^ xa) * 3 + b] = block

                    @pl.when(c != half)
                    def _():
                        w_send_ref[(x ^ xa) * 3 + b] = block

    return call(
        body,
        "projections_back",
        [SMEM] + [VM] * 16,
        [shape((6, HALF, D), bf16)] * 2,
        (at, *acts, *dqs, *dks, *dvs),
        [pltpu.VMEM((3 * GROUP_WIDTH, D), f32)],
        us=6,
    )


def out_norm(at, patches, mixed, w_out, norms):
    def body(at_ref, x_ref, m0, m1, m2, m3, w_ref, norm_ref, two_ref, resid_ref, normal_ref, inverse_ref, three_ref):
        place = at_ref[3]
        parts = [m[...].astype(f32) for m in (m0, m1, m2, m3)]
        groups = []
        for a in range(4):
            steps = (gray(a) - place) & 3
            part = parts[0]
            for k in (1, 2, 3):
                part = jnp.where(steps == k, parts[k], part)
            groups.append(part)
        resid = x_ref[...].astype(f32)
        for a in range(4):
            resid = resid + mm_nt(groups[a].astype(bf16), w_ref[a][:, :GROUP_WIDTH])
        two_ref[...] = jnp.concatenate(groups, axis=1).astype(bf16)
        resid_ref[...] = resid
        normal, inverse = normalize(resid)
        normal_ref[...] = normal
        inverse_ref[...] = jnp.broadcast_to(inverse, (256, 128))
        three_ref[...] = (normal * norm_ref[2:3, :] + norm_ref[3:4, :]).astype(bf16)

    outs = [
        shape((256, D), bf16),
        shape((256, D), f32),
        shape((256, D), f32),
        shape((256, 128), f32),
        shape((256, D), bf16),
    ]
    return call(body, "out_norm", [SMEM] + [VM] * 7, outs, (at, patches, *mixed, w_out, norms))


def by_core_rows(values):
    return jnp.concatenate([values[:, n * 192 : n * 192 + 192] for n in (0, 2, 1, 3)], axis=1)


def mlp(at, act, cot, weights, out_dtype):
    def body(at_ref, a_ref, c_ref, *refs):
        w_refs = refs[0:4]
        hidden_ref, wide_ref, out_ref, three_ref, act_ref, cot_ref, w_ref, out_acc, three_acc, sems = refs[4:14]
        core = at_ref[2]
        own_lanes = pl.ds(pl.multiple_of(core * 384, 128), 384)
        other_lanes = pl.ds(pl.multiple_of((1 - core) * 384, 128), 384)
        copies = []
        for k in range(4):
            group = []
            for r, lanes in enumerate((own_lanes, other_lanes)):
                for j in range(2):
                    for u in range(2):
                        group.append(
                            pltpu.make_async_copy(
                                w_refs[2 * r + (k == 2)].at[2 * (0, 1, 0, 2)[k] + j, pl.ds(u * 192, 192), :],
                                w_ref.at[k, u, pl.ds(j * 192, 192), lanes],
                                sems.at[k, len(group)],
                            )
                        )
            copies.append(group)
            for c in group:
                c.start()
        act_ref[...] = by_core_rows(a_ref[...])
        cot_ref[...] = by_core_rows(c_ref[...])
        for k in range(4):
            for c in copies[k]:
                c.wait()
            up, down = w_ref[k, 0], w_ref[k, 1]
            widened = mm_nt(act_ref[...], up)
            inner = 0.5 * (1.0 + lax.erf(widened * (1.0 / math.sqrt(2.0))))
            slope = inner + widened * jnp.exp(-0.5 * widened * widened) * (1.0 / math.sqrt(2.0 * math.pi))
            hidden = (widened * inner).astype(bf16)
            wide = (mm_nt(cot_ref[...], down) * slope).astype(bf16)
            hidden_ref[:, k * 384 : k * 384 + 384] = hidden
            wide_ref[:, k * 384 : k * 384 + 384] = wide
            out, three = mm(hidden, down), mm(wide, up)
            out_acc[...] = out if k == 0 else out_acc[...] + out
            three_acc[...] = three if k == 0 else three_acc[...] + three
        out_ref[...] = by_core_rows(out_acc[...]).astype(out_dtype)
        three_ref[...] = by_core_rows(three_acc[...]).astype(out_dtype)

    return call(
        body,
        "mlp",
        [SMEM] + [VM] * 2 + [ANY] * 4,
        [shape((256, 1536), bf16)] * 2 + [shape((256, D), out_dtype)] * 2,
        (at, act, cot, *weights),
        [
            pltpu.VMEM((256, D), bf16),
            pltpu.VMEM((256, D), bf16),
            pltpu.VMEM((4, 2, 384, D), bf16),
            pltpu.VMEM((256, D), f32),
            pltpu.VMEM((256, D), f32),
            pltpu.SemaphoreType.DMA((4, 8)),
        ],
        us=8,
    )


def mlp_weights(at, acts, cots, hiddens, wides, slots):
    count = len(slots)

    def body(at_ref, *refs):
        a_refs, c_refs, h_refs, w_refs = (refs[2 * n : 2 * n + 2] for n in range(4))
        keep_ref, send_ref, act_ref, cot_ref, in_ref, stage_ref, in_sems, out_sems = refs[8:16]
        arriving = []
        for n, k in enumerate(slots):
            group = []
            for which, sources in enumerate((w_refs, h_refs)):
                for i in range(2):
                    group.append(
                        pltpu.make_async_copy(
                            sources[i].at[:, pl.ds(k * 384, 384)],
                            in_ref.at[n, which, pl.ds(i * 256, 256), :],
                            in_sems.at[n, len(group)],
                        )
                    )
                    group[-1].start()
            arriving.append(group)
        for i in range(2):
            act_ref[i * 256 : i * 256 + 256, :] = by_core_rows(a_refs[i][...])
            cot_ref[i * 256 : i * 256 + 256, :] = by_core_rows(c_refs[i][...])
        core = at_ref[2]
        own_lanes = pl.ds(pl.multiple_of(core * 384, 128), 384)
        other_lanes = pl.ds(pl.multiple_of((1 - core) * 384, 128), 384)
        leaving = []
        for n in range(count):
            for c in arriving[n]:
                c.wait()
            up = mm_tn(in_ref[n, 0], act_ref[...]).astype(bf16)
            down = mm_tn(in_ref[n, 1], cot_ref[...]).astype(bf16)
            for j in range(2):
                stage_ref[n, j, 0:192, :] = up[j * 192 : j * 192 + 192]
                stage_ref[n, j, 192:384, :] = down[j * 192 : j * 192 + 192]
            for i, (lanes, ref) in enumerate(((own_lanes, keep_ref), (other_lanes, send_ref))):
                leaving.append(pltpu.make_async_copy(stage_ref.at[n, :, :, lanes], ref.at[:, n], out_sems.at[n, i]))
                leaving[-1].start()
        for c in leaving:
            c.wait()

    return call(
        body,
        "mlp_weights",
        [SMEM] + [VM] * 4 + [ANY] * 4,
        [shape((2, count, 384, 384), bf16)] * 2,
        (at, *acts, *cots, *hiddens, *wides),
        [
            pltpu.VMEM((512, D), bf16),
            pltpu.VMEM((512, D), bf16),
            pltpu.VMEM((count, 2, 512, 384), bf16),
            pltpu.VMEM((count, 2, 384, D), bf16),
            pltpu.SemaphoreType.DMA((count, 4)),
            pltpu.SemaphoreType.DMA((count, 2)),
        ],
        us=4,
        out_specs=[ANY] * 2,
    )


def norm_out_back(at, three, three_there, cotangent, normal, inverse, w_out, norms):
    def body(at_ref, t_ref, s_ref, c_ref, n_ref, i_ref, w_ref, norm_ref, *outs):
        resid_ref, sums_ref = outs[0:2]
        g_refs, low_ref = outs[2:6], outs[6]
        place = at_ref[3]
        grad = t_ref[...] + s_ref[...].astype(f32)
        normal = n_ref[...]
        sums_ref[...] = jnp.concatenate(
            [jnp.sum(grad * normal, axis=0, keepdims=True), jnp.sum(grad, axis=0, keepdims=True), jnp.zeros((6, D), f32)],
            axis=0,
        )
        resid = c_ref[...].astype(f32) + layer_back(grad, normal, i_ref[:, 0:1], norm_ref[2:3, :])
        resid_ref[...] = resid
        low = resid.astype(bf16)
        groups = [mm(low, w_ref[a][:, :GROUP_WIDTH]) for a in range(4)]
        for k in range(4):
            ahead = gray((place + k) & 3)
            part = groups[0]
            for a in (1, 2, 3):
                part = jnp.where(ahead == a, groups[a], part)
            g_refs[k][...] = part.astype(bf16)
        low_ref[...] = low

    outs = (
        [shape((256, D), f32), shape((8, D), f32)] + [shape((256, GROUP_WIDTH), bf16)] * 4 + [shape((256, D), bf16)]
    )
    got = call(
        body,
        "norm_out_back",
        [SMEM] + [VM] * 7,
        outs,
        (at, three, three_there, cotangent, normal, inverse, w_out, norms),
        us=4,
    )
    return got[0], got[1], got[2:6], got[6]


def out_weights(at, low, two):
    def body(at_ref, low_ref, two_ref, keep_ref, send_ref, dw_ref):
        x, c, place = at_ref[0], at_ref[2], at_ref[3]
        dw_ref[...] = mm_tn(low_ref[...], two_ref[...])
        for q in range(4):
            for xa in range(2):
                slot = ((place - gray(q)) & 3) * 2 + (x ^ xa)
                for half in range(2):
                    row = (q * 2 + xa) * 96 + half * HALF
                    block = dw_ref[row : row + HALF, :].astype(bf16)

                    @pl.when(c == half)
                    def _():
                        keep_ref[slot] = block

                    @pl.when(c != half)
                    def _():
                        send_ref[slot] = block

    return call(
        body,
        "out_weights",
        [SMEM, VM, VM],
        [shape((8, HALF, D), bf16)] * 2,
        (at, low, two),
        [pltpu.VMEM((D, D), f32)],
        us=3,
    )


def after(value, *others):
    return lax.optimization_barrier((value, *others))[0]


def turn(at, far_own, far_there, near_own, near_there):
    def body(at_ref, far_own_ref, far_there_ref, near_own_ref, near_there_ref, out_ref):
        def write_far(refs):
            for half, ref in enumerate(refs):
                for u in range(2):
                    for j in range(2):
                        row = u * 192 + j * 96
                        out_ref[4 + 4 * u + 2 * half + j] = jnp.transpose(ref[row : row + 96, :].astype(f32))

        def write_near(refs):
            for b in range(4):
                rows = slice(b * HALF, (b + 1) * HALF)
                block = jnp.concatenate([ref[rows, :].astype(f32) for ref in refs], axis=0)
                out_ref[b] = jnp.transpose(block)

        for value in range(2):

            @pl.when(at_ref[1] == value)
            def _():
                write_far((far_own_ref, far_there_ref)[:: 1 if value == 0 else -1])

            @pl.when(at_ref[2] == value)
            def _():
                write_near((near_own_ref, near_there_ref)[:: 1 if value == 0 else -1])

    return call(
        body,
        "turn",
        [SMEM] + [VM] * 4,
        shape((12, 192, 96), f32),
        (at, far_own, far_there, near_own, near_there),
        us=4,
    )


def update(sums, weights, norms):
    def body(sums_ref, w_ref, g_ref, first_ref, second_ref, p_ref, p_first_ref, p_second_ref, *outs):
        grads = sums_ref[0:4, :]
        total_squares = sums_ref[4:5, 0:1] + jnp.sum(jnp.sum(grads * grads, axis=1, keepdims=True), axis=0, keepdims=True)
        norm = jnp.sqrt(total_squares)
        outs[7][...] = jnp.broadcast_to(norm, (8, 128))
        clip = 1.0 / jnp.maximum(norm, 1.0)
        new = adam_step(p_ref[...], grads * clip, p_first_ref[...], p_second_ref[...], rate_vector, 0.0)
        for ref, value in zip(outs[4:7], new):
            ref[...] = value
        for b in range(w_ref.shape[0]):
            new, first, second = adam_step(
                w_ref[b], g_ref[b] * clip, first_ref[b], second_ref[b], rate_matrix, weight_decay
            )
            outs[0][b] = new
            outs[1][b] = new.astype(bf16)
            outs[2][b] = first
            outs[3][b] = second

    dims = weights[0].shape
    outs = [shape(dims, f32), shape(dims, bf16), shape(dims, f32), shape(dims, f32)]
    outs = outs + [shape((4, D), f32)] * 3 + [shape((8, 128), f32)]
    return call(body, "update", [VM] * 8, outs, (sums, *weights, *norms), us=4)


def sync(*values):
    return lax.optimization_barrier(values)


def add_low(a, b):
    return (a.astype(f32) + b.astype(f32)).astype(bf16)


def step_small(
    patches,
    cotangent,
    input_views,
    token_live,
    master,
    moment_one,
    moment_two,
    norm_params,
    norm_moment_one,
    norm_moment_two,
):
    tokens = patches.shape[0]
    rows, blocks, cols = master.shape
    dp = lax.axis_index("dp")
    seq = lax.axis_index("seq")
    quarter, x_place = seq // 2, seq % 2
    y_place, core = dp // 2, dp % 2
    place = gray(quarter)
    at = jnp.stack([x_place, y_place, core, place]).astype(jnp.int32)

    def to_core(value):
        return swap(value, "dp", 1)

    def to_y(value):
        return swap(value, "dp", 2)

    def to_x(value):
        return swap(value, "seq", 1)

    def by_core(first, second):
        return jnp.where(core == 0, first, second), jnp.where(core == 0, second, first)

    def by_y(first, second):
        return jnp.where(y_place == 0, first, second), jnp.where(y_place == 0, second, first)

    def own_y(value):
        return lax.dynamic_slice_in_dim(value, y_place * 384, 384, value.ndim - 1)

    def other_y(value):
        return lax.dynamic_slice_in_dim(value, (1 - y_place) * 384, 384, value.ndim - 1)

    master_t = jnp.transpose(master, (1, 0, 2))
    low_t = jnp.transpose(master_t.astype(bf16), (0, 2, 1))
    flags = jnp.pad(token_live.astype(bf16)[None, :], ((0, 7), (0, D - tokens)))
    out_block = jnp.pad(low_t[3], ((0, 0), (0, 256 - rows))).reshape(3, 32, 256)
    out_block = jnp.transpose(out_block, (1, 0, 2)).reshape(32, D)
    ring0 = jnp.concatenate([patches, flags, out_block], axis=0)
    near_halves = [low_t[0:3, h * HALF : (h + 1) * HALF].reshape(3 * HALF, rows) for h in range(2)]
    far_halves = [
        jnp.concatenate(
            [low_t[4 + 2 * h : 6 + 2 * h].reshape(2 * cols, rows), low_t[8 + 2 * h : 10 + 2 * h].reshape(2 * cols, rows)],
            axis=0,
        )
        for h in range(2)
    ]

    ring1, beside0 = hop_quarter(ring0, 1), to_x(ring0)
    own, other = by_core(*near_halves)
    near = jnp.concatenate(by_core(own, to_core(other)), axis=1)
    near = jnp.stack([near, to_x(near)])
    own, other = by_y(*far_halves)
    far0 = jnp.concatenate(by_y(own, to_y(other)), axis=1)
    ring1, beside0, near, far0 = sync(ring1, beside0, near, far0)

    ring2, beside1 = hop_quarter(ring1, 1), to_x(ring1)
    near = jnp.stack([near, to_y(near)])
    near_there = to_core(near)
    ring2, beside1, near, near_there = sync(ring2, beside1, near, near_there)

    ring3, beside2, cot_there = hop_quarter(ring2, 1), to_x(ring2), to_y(cotangent)
    w_qkv = place_qkv(at, near, near_there)
    got0 = list(project(ring0, beside0, w_qkv, norm_params))
    ring3, beside2, cot_there, first = sync(ring3, beside2, cot_there, got0[0])
    got0[0] = first

    beside3, far1, far3 = to_x(ring3), hop_quarter(after(far0, ring3), 1), hop_quarter(after(far0, ring3), 3)
    got1 = list(project(ring1, after(beside1, first), w_qkv, norm_params))
    got2 = list(project(ring2, beside2, w_qkv, norm_params))
    beside3, far1, far3, got1[0], got2[0] = sync(beside3, far1, far3, got1[0], got2[0])

    far2 = hop_quarter(far1, 1)
    far013 = jnp.stack([far0, far1, far3])
    far013 = jnp.stack([far013, to_x(far013)], axis=1).reshape(6, 384, 384)
    got3 = project(ring3, beside3, w_qkv, norm_params)
    acts, normals, qs, ks, vs, out_own = zip(got0, got1, got2, got3)
    out_own = jnp.concatenate(out_own)
    out_own = jnp.stack([out_own, to_y(out_own)])
    mixed, full, q_back = attend(at, qs, ks, vs)
    mixed = list(mixed)
    *mixed, full, far2, far013, out_own = sync(*mixed, full, far2, far013, out_own)

    mixed = [mixed[0]] + [hop_quarter(mixed[4 - k], k) for k in (3, 2, 1)]
    far2 = jnp.stack([far2, to_x(far2)])
    w_out = place_out(at, out_own, to_core(out_own))
    *mixed, far2, w_out = sync(*mixed, far2, w_out)

    far013_there, far2_there = to_core(far013), to_core(far2)
    two, resid, normal_two, inverse_two, act_three = out_norm(at, patches, mixed, w_out, norm_params)
    w_mlp = (far013, far2, far013_there, far2_there)
    act_three, *w_mlp = sync(act_three, *w_mlp)

    act_there = to_y(act_three)
    hidden, wide, out_mine, three_mine = mlp(at, act_three, cotangent, w_mlp, f32)
    act_there, out_mine = sync(act_there, out_mine)
    hidden_there, wide_there, out_send, three_send = mlp(at, act_there, cot_there, w_mlp, bf16)
    three_send, hidden_there = sync(three_send, hidden_there)
    three_there = to_y(three_send)
    operands = (at, (act_three, act_there), (cotangent, cot_there), (hidden, hidden_there), (wide, wide_there))
    low_keep, low_send = mlp_weights(*operands, (1, 2))
    high_keep, high_send = mlp_weights(*operands, (3, 0))
    three_there, low_send, high_send = sync(three_there, low_send, high_send)

    low_there, high_there = to_core(low_send), to_core(high_send)
    grad_resid, sums_two, parts, grad_low = norm_out_back(
        at, three_mine, three_there, cotangent, normal_two, inverse_two, w_out, norm_params
    )
    *parts, grad_low = sync(*parts, grad_low)

    grads = [parts[0]] + [hop_quarter(parts[k], k) for k in (1, 2, 3)]
    low_sum = add_low(low_keep, low_there)
    high_sum = add_low(high_keep, high_there)
    low_x = to_x(low_sum[1])
    w_out_keep, w_out_send = out_weights(at, grad_low, two)
    out_sum = add_low(w_out_keep, to_core(w_out_send))
    out_sum = add_low(own_y(out_sum), to_y(other_y(out_sum))).reshape(4, 2, HALF, 384)
    *grads, low_x, high_sum, out_sum, out_send = sync(*grads, low_x, high_sum, out_sum, out_send)

    low_half = add_low(low_sum[0], low_x)
    far_got = [hop_quarter(low_half[0], -1), hop_quarter(low_half[1], -2)]
    high_half = add_low(high_sum[0], to_x(high_sum[1]))
    out_sum = add_low(out_sum[:, 0], to_x(out_sum[:, 1]))
    dqs, dks, dvs = attend_back(at, q_back, ks, vs, full, grads)
    dqs = list(dqs)
    dqs[1], high_half, out_sum = sync(dqs[1], high_half, out_sum)
    out_there = to_y(after(out_send, dqs[1]))
    block_out = (resid + out_mine + out_there.astype(f32)).astype(bf16)

    last = hop_quarter(jnp.concatenate([high_half[0], out_sum[3]], axis=0), 1)
    far_got.append(last[:384])
    out_got = [last[384:], hop_quarter(out_sum[1], -1), hop_quarter(out_sum[2], -2)]
    one, sums_one = {}, []
    for ks_here in ((1, 2), (3, 0)):
        keep, send, sums = input_back(*([m[k] for k in ks_here] for m in (normals, dqs, dks, dvs)), w_qkv)
        dqs[0], dqs[3] = after(dqs[0], keep[0]), after(dqs[3], keep[0])
        sums_one.append(sums)
        for k, a, b in zip(ks_here, keep, send):
            one[k] = (a, b)
    near_keep, near_send = projections_back(at, acts, dqs, dks, dvs)
    one1 = to_x(one[1][1])
    one1, near_send, *far_got, block_out = sync(one1, near_send, *far_got, block_out)

    one_ring = hop_quarter(add_low(one[1][0], one1), 1)
    one2 = to_x(after(one[2][1], one1))
    near_sum = add_low(near_keep, to_core(near_send))
    near_sum = add_low(own_y(near_sum), to_y(other_y(near_sum)))
    one_ring, one2, near_sum = sync(one_ring, one2, near_sum)

    near_x = to_x(near_sum[3:6])
    one_ring = hop_quarter(add_low(one_ring, add_low(one[2][0], one2)), 1)
    one3 = to_x(after(one[3][1], one2))
    far_sum = high_half[1].astype(f32)
    for part in far_got:
        far_sum = far_sum + part.astype(f32)
    out_sum = out_sum[0].astype(f32)
    for part in out_got:
        out_sum = out_sum + part.astype(f32)
    near_sum = near_sum[0:3].astype(f32) + near_x.astype(f32)
    near_sum = jnp.concatenate([near_sum.reshape(3 * HALF, 2 * rows), out_sum], axis=0)
    far_own, far_other = by_y(far_sum[:, :rows], far_sum[:, rows:])
    near_own, near_other = by_core(near_sum[:, :rows], near_sum[:, rows:])
    weight_grad = turn(at, far_own, to_y(far_other.astype(bf16)), near_own, to_core(near_other.astype(bf16)))
    squares = jnp.full((4, D), jnp.sum(far_sum * far_sum) + jnp.sum(near_sum * near_sum), f32)
    sums = jnp.concatenate([sums_one[0][0:2] + sums_one[1][0:2], sums_two[0:2], squares], axis=0)
    for by in (1, 2):
        sums = sums + hop_quarter(sums, by)
    sums, one_ring, one3 = sync(sums, one_ring, one3)

    one_ring = hop_quarter(add_low(one_ring, add_low(one[3][0], one3)), 1)
    one0 = to_x(one[0][1])
    sums = sums + swap(sums, "seq", 1)
    sums = after(sums + swap(sums, "dp", 2), weight_grad)
    sums = sums + swap(sums, "dp", 1)
    updated = update(
        sums,
        (master_t, weight_grad, jnp.transpose(moment_one, (1, 0, 2)), jnp.transpose(moment_two, (1, 0, 2))),
        (norm_params, norm_moment_one, norm_moment_two),
    )
    new_master, new_copy, new_moment_one, new_moment_two = (jnp.transpose(m, (1, 0, 2)) for m in updated[0:4])
    new_norm_params, new_norm_moment_one, new_norm_moment_two, grad_norm = updated[4:]
    grad_norm = grad_norm[0, 0]

    grad_one = one_ring.astype(f32) + one[0][0].astype(f32) + one0.astype(f32)
    normal_one, inverse_one = layer_stats(patches.astype(f32))
    patches_grad = grad_resid + layer_back(grad_one, normal_one, inverse_one, norm_params[0])
    return (
        block_out,
        patches_grad,
        new_master,
        new_copy,
        new_moment_one,
        new_moment_two,
        new_norm_params,
        new_norm_moment_one,
        new_norm_moment_two,
        grad_norm,
    )


def solution(mesh):
    tokens = P(("dp", "seq"), None)
    weights = P("dp", None, "seq")
    small = mesh.shape["dp"] == 4 and mesh.shape["seq"] == 8
    return jax.shard_map(
        step_small if small else step_general,
        mesh=mesh,
        in_specs=(tokens, tokens, P("dp"), P(("dp", "seq")), weights, weights, weights, P(), P(), P()),
        out_specs=(tokens, tokens, weights, weights, weights, weights, P(), P(), P(), P()),
        check_vma=False,
    )
```

```python
import math
from functools import partial

import jax
import jax.numpy as jnp
from jax import lax
from jax.experimental import pallas as pl
from jax.experimental.pallas import tpu as pltpu
from jax.sharding import PartitionSpec as P

D = 768
HEADS = 12
HEAD_DIM = 64
FF = 3072
VIEW = 1024
STEP = 10
GROUPS = 4
GROUP_HEADS = HEADS // GROUPS
GROUP_WIDTH = GROUP_HEADS * HEAD_DIM
WIDE = FF // D
RING = (0, 1, 3, 2)

layer_eps = 1e-05
beta_first = 0.9
beta_second = 0.95
adam_eps = 1e-08
rate_matrix = 0.08
rate_vector = 0.8
weight_decay = 0.1
masked_score = -1e30
bf16 = jnp.bfloat16
f32 = jnp.float32


def gray(v):
    return v ^ (v >> 1)


def hop_quarter(value, by):
    split = lax.axis_size("seq") // GROUPS
    pairs = [
        (RING[p] * split + x, RING[(p + by) % GROUPS] * split + x) for p in range(GROUPS) for x in range(split)
    ]
    return lax.ppermute(value, "seq", pairs)


def hop_within(value, by):
    split = lax.axis_size("seq") // GROUPS
    pairs = [(q * split + x, q * split + (x + by) % split) for q in range(GROUPS) for x in range(split)]
    return lax.ppermute(value, "seq", pairs)


def swap(value, axis, bit):
    return lax.ppermute(value, axis, [(i, i ^ bit) for i in range(lax.axis_size(axis))])


def bits_of(axis):
    return [1 << b for b in range(lax.axis_size(axis).bit_length() - 1)]


def total(value):
    for axis in ("dp", "seq"):
        for bit in bits_of(axis):
            value = value + swap(value, axis, bit)
    return value


def pick(stack, index):
    return lax.dynamic_index_in_dim(stack, index, 0, keepdims=False)


def layer_stats(values):
    centre = jnp.mean(values, axis=-1, keepdims=True)
    shifted = values - centre
    spread = jnp.mean(shifted * shifted, axis=-1, keepdims=True)
    inverse = lax.rsqrt(spread + layer_eps)
    return (shifted * inverse, inverse)


def layer_back(grad_normed, normalized, inverse, gain):
    scaled = grad_normed * gain
    centred = jnp.mean(scaled, axis=-1, keepdims=True)
    along = jnp.mean(scaled * normalized, axis=-1, keepdims=True)
    return inverse * (scaled - centred - normalized * along)


def mm(a, b):
    return jnp.dot(a, b, preferred_element_type=f32)


def mm_nt(a, b):
    return lax.dot_general(a, b, (((1,), (1,)), ((), ())), preferred_element_type=f32)


def mm_tn(a, b):
    return lax.dot_general(a, b, (((0,), (0,)), ((), ())), preferred_element_type=f32)


def gather_rows(piece):
    for bit in reversed(bits_of("dp")):
        piece = jnp.concatenate([piece, swap(piece, "dp", bit)], axis=1)
    return piece


def row_order():
    order = [0]
    for bit in reversed(bits_of("dp")):
        order = order + [o ^ bit for o in order]
    return order


def reduce_rows(piece):
    for bit in bits_of("dp"):
        half = piece.shape[1] // 2
        there = swap(piece[:, half:], "dp", bit)
        piece = (piece[:, :half].astype(f32) + there.astype(f32)).astype(bf16)
    return piece


def reduce_within(piece):
    own = piece[0].astype(f32)
    for j in range(1, piece.shape[0]):
        own = own + hop_within(piece[j], -j).astype(f32)
    return own.astype(bf16)


def reduce_ring(slots):
    moving = slots[1]
    for k in (2, 3):
        moving = (hop_quarter(moving, 1).astype(f32) + slots[k].astype(f32)).astype(bf16)
    return hop_quarter(moving, 1).astype(f32) + slots[0].astype(f32)


def adam_step(params, grads, first, second, rate, decay):
    first_new = beta_first * first + (1.0 - beta_first) * grads
    second_new = beta_second * second + (1.0 - beta_second) * grads * grads
    first_hat = first_new / (1.0 - beta_first**STEP)
    second_hat = second_new / (1.0 - beta_second**STEP)
    params_new = params - rate * (first_hat / (jnp.sqrt(second_hat) + adam_eps) + decay * params)
    return (params_new, first_new, second_new)


def relative(dp, absolute, order):
    index = jnp.int32(0)
    for at, offset in enumerate(order):
        index = jnp.where((dp ^ absolute) == offset, at, index)
    return index


def step_general(
    patches,
    cotangent,
    input_views,
    token_live,
    master,
    moment_one,
    moment_two,
    norm_params,
    norm_moment_one,
    norm_moment_two,
):
    tokens = patches.shape[0]
    rows, blocks, cols = master.shape
    n_dp = lax.axis_size("dp")
    split = lax.axis_size("seq") // GROUPS
    dp = lax.axis_index("dp")
    seq = lax.axis_index("seq")
    quarter, within = seq // split, seq % split
    place = gray(quarter)
    inputs_seen = input_views[0]
    gain_one, shift_one, gain_two, shift_two = (norm_params[i] for i in range(4))
    order = row_order()
    dp_place = [order.index(a) for a in range(n_dp)]

    def quarter_behind(k):
        return gray((place - k) & 3)

    flags = jnp.pad(token_live.astype(bf16)[None, :], ((0, 7), (0, D - tokens)))
    ring = [jnp.concatenate([patches, flags], axis=0)]
    for _ in range(3):
        ring.append(hop_quarter(ring[-1], 1))
    pieces = [[ring[k]] + [hop_within(ring[k], j) for j in range(1, split)] for k in range(4)]
    scene = jnp.stack([jnp.stack([p[:tokens] for p in pieces[k]]) for k in range(4)])
    live = jnp.stack([jnp.concatenate([p[tokens, :tokens] for p in pieces[k]]) for k in range(4)])

    copy_low = master.astype(bf16)
    mine = copy_low[:, 0:3, :].reshape(rows, 3 * cols)
    near = jnp.stack([mine] + [hop_within(mine, j) for j in range(1, split)])
    near = gather_rows(near).reshape(split, n_dp, rows, 3, cols)
    near = jnp.stack([pick(near, (within - a) % split) for a in range(split)])
    near = jnp.moveaxis(near, 1, 0)
    near = jnp.stack([pick(near, order_at) for order_at in [relative(dp, a, order) for a in range(n_dp)]])
    w_qkv = jnp.transpose(near, (0, 2, 3, 1, 4)).reshape(D, 3, GROUP_WIDTH)

    up = copy_low[:, 4 : 4 + WIDE].reshape(rows, WIDE * cols)
    down = copy_low[:, 4 + WIDE :].reshape(rows, WIDE * cols)
    far = [jnp.concatenate([up, down, copy_low[:, 3]], axis=1)]
    for _ in range(3):
        far.append(hop_quarter(far[-1], 1))
    weights = [gather_rows(jnp.stack([f] + [hop_within(f, j) for j in range(1, split)])) for f in far]
    width = WIDE * cols
    w_up = [w[:, :, :width] for w in weights]
    w_down = [w[:, :, width : 2 * width] for w in weights]
    w_out = jnp.stack([w[:, :, 2 * width :] for w in weights]).reshape(4 * split, n_dp, rows, cols)

    def slot_of(quarter_abs, within_abs):
        return ((place - gray(quarter_abs)) & 3) * split + (within - within_abs) % split

    w_out = jnp.stack([pick(w_out, slot_of(a // split, a % split)) for a in range(4 * split)])
    w_out = jnp.moveaxis(w_out, 1, 0)
    w_out = jnp.stack([pick(w_out, relative(dp, a, order)) for a in range(n_dp)])
    w_out = jnp.transpose(w_out, (0, 2, 1, 3)).reshape(D, D)

    normal_one, inverse_one = layer_stats(scene.astype(f32))
    act_one = (normal_one * gain_one + shift_one).astype(bf16)
    act_all = act_one.reshape(4 * split * tokens, D)
    act_own = act_one[:, 0].reshape(4 * tokens, D)
    q = mm(act_own, w_qkv[:, 0]).astype(bf16)
    k = mm(act_all, w_qkv[:, 1]).astype(bf16)
    v = mm(act_all, w_qkv[:, 2]).astype(bf16)

    def heads(m):
        return jnp.transpose(m.reshape(m.shape[0], GROUP_HEADS, HEAD_DIM), (1, 0, 2))

    def unheads(m):
        return jnp.transpose(m, (1, 0, 2)).reshape(m.shape[1], GROUP_WIDTH)

    views = jnp.stack([(quarter_behind(i) * split * tokens) // VIEW for i in range(4)])
    open_block = (views[None, :] < inputs_seen) | (views[None, :] == views[:, None])
    visible = open_block[:, None, :, None] & (live > 0)[None, None]
    visible = jnp.broadcast_to(visible, (4, tokens, 4, split * tokens)).reshape(4 * tokens, -1)
    scaling = 1.0 / math.sqrt(HEAD_DIM)
    qh, kh, vh = heads(q), heads(k), heads(v)
    scores = jnp.einsum("hqd,hkd->hqk", qh, kh, preferred_element_type=f32) * scaling
    scores = jnp.where(visible[None], scores, masked_score)
    top = jnp.max(scores, axis=-1, keepdims=True)
    probs = jnp.where(visible[None], jnp.exp(scores - top), 0.0)
    probs = probs / jnp.sum(probs, axis=-1, keepdims=True)
    probs_low = probs.astype(bf16)
    attended = jnp.einsum("hqk,hkd->hqd", probs_low, vh, preferred_element_type=f32)
    flat = unheads(attended).astype(bf16).reshape(4, tokens, GROUP_WIDTH)
    back = jnp.stack([flat[0]] + [hop_quarter(flat[i], -i) for i in range(1, 4)])
    act_two = jnp.concatenate([pick(back, (gray(a) - place) & 3) for a in range(4)], axis=1)

    patch_float = patches.astype(f32)
    resid = patch_float + mm(act_two, w_out)
    normal_two, inverse_two = layer_stats(resid)
    act_three = (normal_two * gain_two + shift_two).astype(bf16)

    def to_relative(m):
        parts = m.reshape(tokens, n_dp, rows)
        return jnp.concatenate([lax.dynamic_index_in_dim(parts, dp ^ o, 1, keepdims=False) for o in order], axis=1)

    def from_relative(m):
        parts = m.reshape(tokens, n_dp, rows)
        return jnp.concatenate(
            [lax.dynamic_index_in_dim(parts, relative(dp, a, order), 1, keepdims=False) for a in range(n_dp)], axis=1
        )

    act_rel = to_relative(act_three)
    cot_rel = to_relative(cotangent)
    branch_rel = jnp.zeros((tokens, D), f32)
    three_rel = jnp.zeros((tokens, D), f32)
    far_grads = []
    for i in range(4):
        group = []
        for j in range(split):
            widened = mm(act_rel, w_up[i][j])
            activated, gelu_pull = jax.vjp(partial(jax.nn.gelu, approximate=False), widened)
            hidden = activated.astype(bf16)
            branch_rel = branch_rel + mm_nt(hidden, w_down[i][j])
            grad_wide = gelu_pull(mm(cot_rel, w_down[i][j]))[0].astype(bf16)
            three_rel = three_rel + mm_nt(grad_wide, w_up[i][j])
            grad_up = mm_tn(act_rel, grad_wide).astype(bf16)
            grad_down = mm_tn(cot_rel, hidden).astype(bf16)
            group.append((grad_up, grad_down))
        far_grads.append(group)
    block_out = (resid + from_relative(branch_rel)).astype(bf16)
    grad_three = from_relative(three_rel)
    gain_two_grad = jnp.sum(grad_three * normal_two, axis=0)
    shift_two_grad = jnp.sum(grad_three, axis=0)
    grad_resid = cotangent.astype(f32) + layer_back(grad_three, normal_two, inverse_two, gain_two)
    grad_branch = grad_resid.astype(bf16)
    grad_attended = mm_nt(grad_branch, w_out).astype(bf16)
    grad_w_out = mm_tn(act_two, grad_branch).astype(bf16)

    parts = jnp.transpose(grad_attended.reshape(tokens, 4, GROUP_WIDTH), (1, 0, 2))
    parts = [pick(parts, gray((place + i) & 3)) for i in range(4)]
    grad_here = jnp.concatenate([parts[0]] + [hop_quarter(parts[i], i) for i in range(1, 4)], axis=0)
    gh = heads(grad_here)
    dprobs = jnp.einsum("hqd,hkd->hqk", gh, vh, preferred_element_type=f32)
    delta = jnp.sum(gh.astype(f32) * attended, axis=-1, keepdims=True)
    grad_scores = (probs * (dprobs - delta)).astype(bf16)
    dq = unheads(jnp.einsum("hqk,hkd->hqd", grad_scores, kh, preferred_element_type=f32) * scaling).astype(bf16)
    dk = unheads(jnp.einsum("hqk,hqd->hkd", grad_scores, qh, preferred_element_type=f32) * scaling).astype(bf16)
    dv = unheads(jnp.einsum("hqk,hqd->hkd", probs_low, gh, preferred_element_type=f32)).astype(bf16)

    grad_near = jnp.stack([mm_tn(act_own, dq), mm_tn(act_all, dk), mm_tn(act_all, dv)], axis=1).astype(bf16)
    grad_near = grad_near.reshape(n_dp, rows, 3, split, cols)
    grad_near = jnp.stack([pick(grad_near, dp ^ o) for o in order])
    grad_near = jnp.transpose(grad_near, (3, 0, 1, 2, 4)).reshape(split, D, 3 * cols)
    grad_near = jnp.stack([pick(grad_near, (within - j) % split) for j in range(split)])
    grad_near = reduce_within(reduce_rows(grad_near)).astype(f32).reshape(rows, 3, cols)

    one_q = mm_nt(dq, w_qkv[:, 0]).reshape(4, 1, tokens, D)
    one_kv = (mm_nt(dk, w_qkv[:, 1]) + mm_nt(dv, w_qkv[:, 2])).reshape(4, split, tokens, D)
    one = jnp.concatenate([one_kv[:, :1] + one_q, one_kv[:, 1:]], axis=1)
    gain_one_grad = jnp.sum(one * normal_one, axis=(0, 1, 2))
    shift_one_grad = jnp.sum(one, axis=(0, 1, 2))
    one_low = one.astype(bf16)
    grad_one = reduce_ring([reduce_within(one_low[i]) for i in range(4)])
    patches_grad = grad_resid + layer_back(grad_one, normal_one[0, 0], inverse_one[0, 0], gain_one)

    out_parts = grad_w_out.reshape(n_dp, rows, 4 * split, cols)
    out_parts = jnp.stack([pick(out_parts, dp ^ o) for o in order])
    out_parts = jnp.transpose(out_parts, (2, 0, 1, 3)).reshape(4 * split, D, cols)
    slots = []
    for i in range(4):
        stack = []
        for j in range(split):
            own_out = pick(out_parts, quarter_behind(i) * split + (within - j) % split)
            stack.append(jnp.concatenate([*far_grads[i][j], own_out], axis=1))
        slots.append(reduce_within(reduce_rows(jnp.stack(stack))))
    far_sum = reduce_ring(slots)
    grad_up = far_sum[:, :width].reshape(rows, WIDE, cols)
    grad_down = far_sum[:, width : 2 * width].reshape(rows, WIDE, cols)
    grad_out = far_sum[:, 2 * width :].reshape(rows, 1, cols)

    weight_grad = jnp.concatenate([grad_near, grad_out, grad_up, grad_down], axis=1)
    param_grad = total(jnp.stack([gain_one_grad, shift_one_grad, gain_two_grad, shift_two_grad]))
    squares = total(jnp.full((8, 128), jnp.sum(weight_grad * weight_grad), f32))[0, 0] + jnp.sum(param_grad * param_grad)
    grad_norm = jnp.sqrt(squares)
    clip = 1.0 / jnp.maximum(grad_norm, 1.0)
    new_master, new_moment_one, new_moment_two = adam_step(
        master, weight_grad * clip, moment_one, moment_two, rate_matrix, weight_decay
    )
    new_norm_params, new_norm_moment_one, new_norm_moment_two = adam_step(
        norm_params, param_grad * clip, norm_moment_one, norm_moment_two, rate_vector, 0.0
    )
    return (
        block_out,
        patches_grad,
        new_master,
        new_master.astype(bf16),
        new_moment_one,
        new_moment_two,
        new_norm_params,
        new_norm_moment_one,
        new_norm_moment_two,
        grad_norm,
    )


HALF = 48
ANY = pl.BlockSpec(memory_space=pl.ANY)
SMEM = pl.BlockSpec(memory_space=pltpu.SMEM)
VMEM_LIMIT = 34
SCALE = 0.1


def call(body, name, ins, outs, operands, scratch=(), us=4, out_specs=None, aliases=None, mem=None):
    return pl.pallas_call(
        body,
        name=name,
        out_shape=outs,
        in_specs=ins,
        out_specs=out_specs or jax.tree.map(lambda _: pl.BlockSpec(memory_space=pltpu.VMEM), outs),
        scratch_shapes=list(scratch),
        input_output_aliases=aliases or {},
        cost_estimate=pl.CostEstimate(flops=int(us * SCALE * 1e9), bytes_accessed=int(us * SCALE * 3.6e6), transcendentals=0),
        compiler_params=pltpu.CompilerParams(vmem_limit_bytes=(mem or VMEM_LIMIT) << 20),
    )(*operands)


VM = pl.BlockSpec(memory_space=pltpu.VMEM)


def shape(dims, dtype):
    return jax.ShapeDtypeStruct(dims, dtype)


def run_copies(copies):
    for c in copies:
        c.start()
    for c in copies:
        c.wait()


def place_qkv(at, own_half, other_half):
    def body(at_ref, own_ref, other_ref, out_ref, sems):
        x, y, c = at_ref[0], at_ref[1], at_ref[2]
        copies = []
        for block in range(3):
            for j in range(2):
                for r in range(2):
                    for h, ref in ((0, own_ref), (1, other_ref)):
                        row = block * GROUP_WIDTH + (x ^ j) * 96 + (c ^ h) * HALF
                        copies.append(
                            pltpu.make_async_copy(
                                ref.at[r, j, pl.ds(block * HALF, HALF), :],
                                out_ref.at[
                                    pl.ds(pl.multiple_of(row, 16), HALF),
                                    pl.ds(pl.multiple_of((y ^ r) * 384, 128), 384),
                                ],
                                sems.at[len(copies)],
                            )
                        )
        run_copies(copies)

    return call(
        body,
        "place_qkv",
        [SMEM, ANY, ANY],
        shape((3 * GROUP_WIDTH, D), bf16),
        (at, own_half, other_half),
        [pltpu.SemaphoreType.DMA((24,))],
    )


def place_out(at, own_half, other_half):
    def body(at_ref, own_ref, other_ref, out_ref, sems):
        x, y, c, place = at_ref[0], at_ref[1], at_ref[2], at_ref[3]
        copies = []
        for k in range(4):
            quarter = gray((place - k) & 3)
            for j in range(2):
                for r in range(2):
                    for h, ref in ((0, own_ref), (1, other_ref)):
                        row = (quarter * 2 + (x ^ j)) * 96
                        copies.append(
                            pltpu.make_async_copy(
                                ref.at[r, k * 2 + j],
                                out_ref.at[(y ^ r) * 2 + (c ^ h), pl.ds(pl.multiple_of(row, 16), 96), :],
                                sems.at[len(copies)],
                            )
                        )
        run_copies(copies)

    return call(
        body,
        "place_out",
        [SMEM, ANY, ANY],
        shape((4, D, 256), bf16),
        (at, own_half, other_half),
        [pltpu.SemaphoreType.DMA((32,))],
        us=3,
    )


def normalize(values):
    centre = jnp.mean(values, axis=-1, keepdims=True)
    shifted = values - centre
    inverse = lax.rsqrt(jnp.mean(shifted * shifted, axis=-1, keepdims=True) + layer_eps)
    return shifted * inverse, inverse


def lane_index(dims):
    return lax.broadcasted_iota(jnp.int32, dims, len(dims) - 1)


def project(first, second, w_t, norms):
    def body(a_ref, b_ref, w_ref, norm_ref, act_ref, normal_ref, q_ref, k_ref, v_ref, out_ref, wide_ref):
        wide_ref[...] = jnp.zeros_like(wide_ref)
        for h in range(9):
            wide_ref[h * 128 : h * 128 + 64, :] = w_ref[h * 64 : h * 64 + 64, :]
        gain, shift = norm_ref[0:1, :], norm_ref[1:2, :]
        for piece, ref in enumerate((a_ref, b_ref)):
            at = slice(piece * 256, piece * 256 + 256)
            normal, _ = normalize(ref[0:256, :].astype(f32))
            act = (normal * gain + shift).astype(bf16)
            normal_ref[at, :] = normal.astype(bf16)
            act_ref[at, :] = act
            for n in range(3):
                out_ref[piece, n * 32 : n * 32 + 32, :] = ref[264:296, n * 256 : n * 256 + 256]
            flags = ref[256:257, 0:256].astype(f32)
            mask = jnp.where(flags > 0, 0.0, masked_score)
            mask = jnp.transpose(jnp.broadcast_to(mask, (128, 256)))
            lanes = lane_index((256, 128))
            def head(h, _):
                def rows(block):
                    return wide_ref[pl.ds(pl.multiple_of((3 * block + h) * 128, 128), 128), :]

                if piece == 0:
                    q = mm_nt(act, rows(0)).astype(bf16).astype(f32)
                    q = jnp.where(lanes == 64, 1.0, q * (1.0 / math.sqrt(HEAD_DIM)))
                    q_ref[h] = q.astype(bf16)
                k = jnp.where(lanes == 64, mask, mm_nt(act, rows(1)))
                k_ref[h, at, :] = jnp.where((lanes > 64) & (lanes < 68), 1.0, k).astype(bf16)
                v = mm_nt(act, rows(2))
                v_ref[h, at, :] = jnp.where((lanes > 63) & (lanes < 67), 1.0, v).astype(bf16)
                return 0

            lax.fori_loop(0, 3, head, 0)

    outs = [
        shape((512, D), bf16),
        shape((512, D), bf16),
        shape((3, 256, 128), bf16),
        shape((3, 512, 128), bf16),
        shape((3, 512, 128), bf16),
        shape((2, 96, 256), bf16),
    ]
    return call(body, "norm_project", [VM] * 4, outs, (first, second, w_t, norms), [pltpu.VMEM((1152, D), bf16)], us=4)


def in_three(value):
    high = value.astype(bf16).astype(f32)
    rest = value - high
    mid = rest.astype(bf16).astype(f32)
    return high, mid, rest - mid


def with_parts(base, lanes, first, value):
    for i, part in enumerate(in_three(value)):
        base = jnp.where(lanes == first + i, part, base)
    return base


def join_heads(parts):
    return jnp.concatenate([p[:, :HEAD_DIM] for p in parts], axis=1)


def stack_slots(place, slots, stacked, sems, base=0):
    return [
        pltpu.make_async_copy(ref, stacked.at[gray((place - k) & 3)], sems.at[base + k]) for k, ref in enumerate(slots)
    ]


def attend(at, qs, ks, vs):
    def body(at_ref, *refs):
        low_refs, full_ref, back_ref = refs[12:16], refs[16], refs[17]
        q_ref, k_ref, v_ref, sems = refs[18:22]
        place = at_ref[3]
        lanes = lane_index((256, 128))
        run_copies(
            stack_slots(place, refs[0:4], q_ref, sems)
            + stack_slots(place, refs[4:8], k_ref, sems, 4)
            + stack_slots(place, refs[8:12], v_ref, sems, 8)
        )

        def head(h, _):
            for i in range(4):
                chunks = (0, 1) if i < 2 else (0, 1, 2, 3)
                q = q_ref[i, h]
                scores = [mm_nt(q, k_ref[c, h]) for c in chunks]
                top = None
                for s in scores:
                    for b in range(0, s.shape[1], 128):
                        part = s[:, b : b + 128]
                        top = part if top is None else jnp.maximum(top, part)
                top = jnp.max(top, axis=1, keepdims=True)
                mixed = None
                for s, c in zip(scores, chunks):
                    part = mm(jnp.exp(s - top).astype(bf16), v_ref[c, h])
                    mixed = part if mixed is None else mixed + part
                norm = mixed[:, HEAD_DIM : HEAD_DIM + 1]
                full_ref[i, h] = mixed / norm
                logsum = top + jnp.log(norm)
                back_ref[i, h] = with_parts(q.astype(f32), lanes, 65, -logsum).astype(bf16)
            return 0

        lax.fori_loop(0, 3, head, 0)
        for k in range(4):
            i = gray((place - k) & 3)
            low_refs[k][...] = join_heads([full_ref[i, h] for h in range(3)]).astype(bf16)

    outs = (
        [shape((256, GROUP_WIDTH), bf16)] * 4 + [shape((4, 3, 256, 128), f32)] + [shape((4, 3, 256, 128), bf16)]
    )
    got = call(
        body,
        "attend",
        [SMEM] + [ANY] * 12,
        outs,
        (at, *qs, *ks, *vs),
        [
            pltpu.VMEM((4, 3, 256, 128), bf16),
            pltpu.VMEM((4, 3, 512, 128), bf16),
            pltpu.VMEM((4, 3, 512, 128), bf16),
            pltpu.SemaphoreType.DMA((12,)),
        ],
        us=12,
    )
    return got[0:4], got[4], got[5]


def attend_back(at, q_back, ks, vs, full, grads):
    def body(at_ref, q_ref, *refs):
        full_ref, g_refs = refs[8], refs[9:13]
        dq_refs, dk_refs, dv_refs = refs[13:17], refs[17:21], refs[21:25]
        k_ref, v_ref, g_ref, dq_ref, dk_ref, dv_ref, sems = refs[25:32]
        place = at_ref[3]
        copies = stack_slots(place, refs[0:4], k_ref, sems) + stack_slots(place, refs[4:8], v_ref, sems, 4)
        for c in copies:
            c.start()
        lanes = lane_index((256, 128))
        for k in range(4):
            i = gray((place - k) & 3)
            for h in range(3):
                g = g_refs[k][:, h * 64 : h * 64 + 64].astype(f32)
                delta = jnp.sum(g * full_ref[i, h][:, :64], axis=-1, keepdims=True)
                g = jnp.concatenate([g, jnp.zeros((256, 64), f32)], axis=1)
                g_ref[h, pl.ds(pl.multiple_of(i * 256, 256), 256), :] = with_parts(g, lanes, 64, -delta).astype(bf16)
        for c in copies:
            c.wait()

        def head(h, _):
            q_all = jnp.concatenate([q_ref[i, h] for i in range(4)], axis=0)
            for c in range(4):
                first = 0 if c < 2 else 512
                k, v = k_ref[c, h], v_ref[c, h]
                q, g = q_all[first:], g_ref[h, first:, :]
                p = jnp.exp(mm_nt(k, q))
                ds = (p * mm_nt(v, g)).astype(bf16)
                dv_ref[c, h] = mm(p.astype(bf16), g)
                dk_ref[c, h] = mm(ds, q)
                dq = mm(jnp.transpose(k), ds)
                if c == 0:
                    dq_ref[h] = dq
                else:
                    dq_ref[h, :, first:] += dq
            return 0

        lax.fori_loop(0, 3, head, 0)
        for k in range(4):
            i = gray((place - k) & 3)
            cols = pl.ds(pl.multiple_of(i * 256, 256), 256)
            parts = [jnp.transpose(dq_ref[h, :, cols]) for h in range(3)]
            dq_refs[k][...] = (join_heads(parts) * (1.0 / math.sqrt(HEAD_DIM))).astype(bf16)
            dk_refs[k][...] = join_heads([dk_ref[i, h] for h in range(3)]).astype(bf16)
            dv_refs[k][...] = join_heads([dv_ref[i, h] for h in range(3)]).astype(bf16)

    outs = [shape((256, GROUP_WIDTH), bf16)] * 4 + [shape((512, GROUP_WIDTH), bf16)] * 8
    got = call(
        body,
        "attend_back",
        [SMEM, VM] + [ANY] * 8 + [VM] * 5,
        outs,
        (at, q_back, *ks, *vs, full, *grads),
        [
            pltpu.VMEM((4, 3, 512, 128), bf16),
            pltpu.VMEM((4, 3, 512, 128), bf16),
            pltpu.VMEM((3, 1024, 128), bf16),
            pltpu.VMEM((3, 128, 1024), f32),
            pltpu.VMEM((4, 3, 512, 128), f32),
            pltpu.VMEM((4, 3, 512, 128), f32),
            pltpu.SemaphoreType.DMA((8,)),
        ],
        us=16,
        mem=34,
    )
    return got[0:4], got[4:8], got[8:12]


def input_back(normals, dqs, dks, dvs, w_t):
    count = len(normals)

    def body(*refs):
        normal_refs, dq_refs, dk_refs, dv_refs = (refs[n * count : (n + 1) * count] for n in range(4))
        w_ref, *outs = refs[4 * count :]
        keep_refs, send_refs, norm_ref = outs[0:count], outs[count : 2 * count], outs[2 * count]
        gains, shifts = jnp.zeros((1, D), f32), jnp.zeros((1, D), f32)
        for i in range(count):
            for j, out_ref in enumerate((keep_refs[i], send_refs[i])):
                r = slice(j * 256, j * 256 + 256)
                one = mm(dk_refs[i][r, :], w_ref[192:384, :]) + mm(dv_refs[i][r, :], w_ref[384:576, :])
                if j == 0:
                    one = one + mm(dq_refs[i][...], w_ref[0:192, :])
                gains = gains + jnp.sum(one * normal_refs[i][r, :].astype(f32), axis=0, keepdims=True)
                shifts = shifts + jnp.sum(one, axis=0, keepdims=True)
                out_ref[...] = one.astype(bf16)
        norm_ref[...] = jnp.concatenate([gains, shifts, jnp.zeros((6, D), f32)], axis=0)

    outs = [shape((256, D), bf16)] * (2 * count) + [shape((8, D), f32)]
    got = call(body, "input_back", [VM] * (4 * count + 1), outs, (*normals, *dqs, *dks, *dvs, w_t), us=count + 1)
    return got[0:count], got[count : 2 * count], got[2 * count]


def projections_back(at, acts, dqs, dks, dvs):
    def body(at_ref, *refs):
        act_refs, dq_refs, dk_refs, dv_refs = (refs[4 * n : 4 * n + 4] for n in range(4))
        w_keep_ref, w_send_ref, dw_ref = refs[16:19]
        for i in range(4):
            act = act_refs[i][...]
            for b, (ref, rows) in enumerate(((dq_refs[i], 256), (dk_refs[i], 512), (dv_refs[i], 512))):
                part = mm_tn(ref[...], act[:rows])
                at_rows = slice(b * GROUP_WIDTH, (b + 1) * GROUP_WIDTH)
                dw_ref[at_rows, :] = part if i == 0 else dw_ref[at_rows, :] + part
        x, c = at_ref[0], at_ref[2]
        for b in range(3):
            for xa in range(2):
                for half in range(2):
                    row = b * GROUP_WIDTH + (xa * 2 + half) * HALF
                    block = dw_ref[row : row + HALF, :].astype(bf16)

                    @pl.when(c == half)
                    def _():
                        w_keep_ref[(x ^ xa) * 3 + b] = block

                    @pl.when(c != half)
                    def _():
                        w_send_ref[(x ^ xa) * 3 + b] = block

    return call(
        body,
        "projections_back",
        [SMEM] + [VM] * 16,
        [shape((6, HALF, D), bf16)] * 2,
        (at, *acts, *dqs, *dks, *dvs),
        [pltpu.VMEM((3 * GROUP_WIDTH, D), f32)],
        us=6,
    )


def out_norm(at, patches, mixed, w_out, norms):
    def body(at_ref, x_ref, m0, m1, m2, m3, w_ref, norm_ref, two_ref, resid_ref, normal_ref, inverse_ref, three_ref):
        place = at_ref[3]
        parts = [m[...].astype(f32) for m in (m0, m1, m2, m3)]
        groups = []
        for a in range(4):
            steps = (gray(a) - place) & 3
            part = parts[0]
            for k in (1, 2, 3):
                part = jnp.where(steps == k, parts[k], part)
            groups.append(part)
        resid = x_ref[...].astype(f32)
        for a in range(4):
            resid = resid + mm_nt(groups[a].astype(bf16), w_ref[a][:, :GROUP_WIDTH])
        two_ref[...] = jnp.concatenate(groups, axis=1).astype(bf16)
        resid_ref[...] = resid
        normal, inverse = normalize(resid)
        normal_ref[...] = normal
        inverse_ref[...] = jnp.broadcast_to(inverse, (256, 128))
        three_ref[...] = (normal * norm_ref[2:3, :] + norm_ref[3:4, :]).astype(bf16)

    outs = [
        shape((256, D), bf16),
        shape((256, D), f32),
        shape((256, D), f32),
        shape((256, 128), f32),
        shape((256, D), bf16),
    ]
    return call(body, "out_norm", [SMEM] + [VM] * 7, outs, (at, patches, *mixed, w_out, norms))


def by_core_rows(values):
    return jnp.concatenate([values[:, n * 192 : n * 192 + 192] for n in (0, 2, 1, 3)], axis=1)


def mlp(at, act, cot, weights, out_dtype):
    def body(at_ref, a_ref, c_ref, *refs):
        w_refs = refs[0:4]
        hidden_ref, wide_ref, out_ref, three_ref, act_ref, cot_ref, w_ref, out_acc, three_acc, sems = refs[4:14]
        core = at_ref[2]
        own_lanes = pl.ds(pl.multiple_of(core * 384, 128), 384)
        other_lanes = pl.ds(pl.multiple_of((1 - core) * 384, 128), 384)
        copies = []
        for k in range(4):
            group = []
            for r, lanes in enumerate((own_lanes, other_lanes)):
                for j in range(2):
                    for u in range(2):
                        group.append(
                            pltpu.make_async_copy(
                                w_refs[2 * r + (k == 2)].at[2 * (0, 1, 0, 2)[k] + j, pl.ds(u * 192, 192), :],
                                w_ref.at[k, u, pl.ds(j * 192, 192), lanes],
                                sems.at[k, len(group)],
                            )
                        )
            copies.append(group)
            for c in group:
                c.start()
        act_ref[...] = by_core_rows(a_ref[...])
        cot_ref[...] = by_core_rows(c_ref[...])
        for k in range(4):
            for c in copies[k]:
                c.wait()
            up, down = w_ref[k, 0], w_ref[k, 1]
            widened = mm_nt(act_ref[...], up)
            inner = 0.5 * (1.0 + lax.erf(widened * (1.0 / math.sqrt(2.0))))
            slope = inner + widened * jnp.exp(-0.5 * widened * widened) * (1.0 / math.sqrt(2.0 * math.pi))
            hidden = (widened * inner).astype(bf16)
            wide = (mm_nt(cot_ref[...], down) * slope).astype(bf16)
            hidden_ref[:, k * 384 : k * 384 + 384] = hidden
            wide_ref[:, k * 384 : k * 384 + 384] = wide
            out, three = mm(hidden, down), mm(wide, up)
            out_acc[...] = out if k == 0 else out_acc[...] + out
            three_acc[...] = three if k == 0 else three_acc[...] + three
        out_ref[...] = by_core_rows(out_acc[...]).astype(out_dtype)
        three_ref[...] = by_core_rows(three_acc[...]).astype(out_dtype)

    return call(
        body,
        "mlp",
        [SMEM] + [VM] * 2 + [ANY] * 4,
        [shape((256, 1536), bf16)] * 2 + [shape((256, D), out_dtype)] * 2,
        (at, act, cot, *weights),
        [
            pltpu.VMEM((256, D), bf16),
            pltpu.VMEM((256, D), bf16),
            pltpu.VMEM((4, 2, 384, D), bf16),
            pltpu.VMEM((256, D), f32),
            pltpu.VMEM((256, D), f32),
            pltpu.SemaphoreType.DMA((4, 8)),
        ],
        us=8,
    )


def mlp_weights(at, acts, cots, hiddens, wides, slots):
    count = len(slots)

    def body(at_ref, *refs):
        a_refs, c_refs, h_refs, w_refs = (refs[2 * n : 2 * n + 2] for n in range(4))
        keep_ref, send_ref, act_ref, cot_ref, in_ref, stage_ref, in_sems, out_sems = refs[8:16]
        arriving = []
        for n, k in enumerate(slots):
            group = []
            for which, sources in enumerate((w_refs, h_refs)):
                for i in range(2):
                    group.append(
                        pltpu.make_async_copy(
                            sources[i].at[:, pl.ds(k * 384, 384)],
                            in_ref.at[n, which, pl.ds(i * 256, 256), :],
                            in_sems.at[n, len(group)],
                        )
                    )
                    group[-1].start()
            arriving.append(group)
        for i in range(2):
            act_ref[i * 256 : i * 256 + 256, :] = by_core_rows(a_refs[i][...])
            cot_ref[i * 256 : i * 256 + 256, :] = by_core_rows(c_refs[i][...])
        core = at_ref[2]
        own_lanes = pl.ds(pl.multiple_of(core * 384, 128), 384)
        other_lanes = pl.ds(pl.multiple_of((1 - core) * 384, 128), 384)
        leaving = []
        for n in range(count):
            for c in arriving[n]:
                c.wait()
            up = mm_tn(in_ref[n, 0], act_ref[...]).astype(bf16)
            down = mm_tn(in_ref[n, 1], cot_ref[...]).astype(bf16)
            for j in range(2):
                stage_ref[n, j, 0:192, :] = up[j * 192 : j * 192 + 192]
                stage_ref[n, j, 192:384, :] = down[j * 192 : j * 192 + 192]
            for i, (lanes, ref) in enumerate(((own_lanes, keep_ref), (other_lanes, send_ref))):
                leaving.append(pltpu.make_async_copy(stage_ref.at[n, :, :, lanes], ref.at[:, n], out_sems.at[n, i]))
                leaving[-1].start()
        for c in leaving:
            c.wait()

    return call(
        body,
        "mlp_weights",
        [SMEM] + [VM] * 4 + [ANY] * 4,
        [shape((2, count, 384, 384), bf16)] * 2,
        (at, *acts, *cots, *hiddens, *wides),
        [
            pltpu.VMEM((512, D), bf16),
            pltpu.VMEM((512, D), bf16),
            pltpu.VMEM((count, 2, 512, 384), bf16),
            pltpu.VMEM((count, 2, 384, D), bf16),
            pltpu.SemaphoreType.DMA((count, 4)),
            pltpu.SemaphoreType.DMA((count, 2)),
        ],
        us=4,
        out_specs=[ANY] * 2,
    )


def norm_out_back(at, three, three_there, cotangent, normal, inverse, w_out, norms):
    def body(at_ref, t_ref, s_ref, c_ref, n_ref, i_ref, w_ref, norm_ref, *outs):
        resid_ref, sums_ref = outs[0:2]
        g_refs, low_ref = outs[2:6], outs[6]
        place = at_ref[3]
        grad = t_ref[...] + s_ref[...].astype(f32)
        normal = n_ref[...]
        sums_ref[...] = jnp.concatenate(
            [jnp.sum(grad * normal, axis=0, keepdims=True), jnp.sum(grad, axis=0, keepdims=True), jnp.zeros((6, D), f32)],
            axis=0,
        )
        resid = c_ref[...].astype(f32) + layer_back(grad, normal, i_ref[:, 0:1], norm_ref[2:3, :])
        resid_ref[...] = resid
        low = resid.astype(bf16)
        groups = [mm(low, w_ref[a][:, :GROUP_WIDTH]) for a in range(4)]
        for k in range(4):
            ahead = gray((place + k) & 3)
            part = groups[0]
            for a in (1, 2, 3):
                part = jnp.where(ahead == a, groups[a], part)
            g_refs[k][...] = part.astype(bf16)
        low_ref[...] = low

    outs = (
        [shape((256, D), f32), shape((8, D), f32)] + [shape((256, GROUP_WIDTH), bf16)] * 4 + [shape((256, D), bf16)]
    )
    got = call(
        body,
        "norm_out_back",
        [SMEM] + [VM] * 7,
        outs,
        (at, three, three_there, cotangent, normal, inverse, w_out, norms),
        us=4,
    )
    return got[0], got[1], got[2:6], got[6]


def out_weights(at, low, two):
    def body(at_ref, low_ref, two_ref, keep_ref, send_ref, dw_ref):
        x, c, place = at_ref[0], at_ref[2], at_ref[3]
        dw_ref[...] = mm_tn(low_ref[...], two_ref[...])
        for q in range(4):
            for xa in range(2):
                slot = ((place - gray(q)) & 3) * 2 + (x ^ xa)
                for half in range(2):
                    row = (q * 2 + xa) * 96 + half * HALF
                    block = dw_ref[row : row + HALF, :].astype(bf16)

                    @pl.when(c == half)
                    def _():
                        keep_ref[slot] = block

                    @pl.when(c != half)
                    def _():
                        send_ref[slot] = block

    return call(
        body,
        "out_weights",
        [SMEM, VM, VM],
        [shape((8, HALF, D), bf16)] * 2,
        (at, low, two),
        [pltpu.VMEM((D, D), f32)],
        us=3,
    )


def after(value, *others):
    return lax.optimization_barrier((value, *others))[0]


def turn(at, far_own, far_there, near_own, near_there):
    def body(at_ref, far_own_ref, far_there_ref, near_own_ref, near_there_ref, out_ref):
        def write_far(refs):
            for half, ref in enumerate(refs):
                for u in range(2):
                    for j in range(2):
                        row = u * 192 + j * 96
                        out_ref[4 + 4 * u + 2 * half + j] = jnp.transpose(ref[row : row + 96, :].astype(f32))

        def write_near(refs):
            for b in range(4):
                rows = slice(b * HALF, (b + 1) * HALF)
                block = jnp.concatenate([ref[rows, :].astype(f32) for ref in refs], axis=0)
                out_ref[b] = jnp.transpose(block)

        for value in range(2):

            @pl.when(at_ref[1] == value)
            def _():
                write_far((far_own_ref, far_there_ref)[:: 1 if value == 0 else -1])

            @pl.when(at_ref[2] == value)
            def _():
                write_near((near_own_ref, near_there_ref)[:: 1 if value == 0 else -1])

    return call(
        body,
        "turn",
        [SMEM] + [VM] * 4,
        shape((12, 192, 96), f32),
        (at, far_own, far_there, near_own, near_there),
        us=4,
    )


def update(sums, weights, norms):
    def body(sums_ref, w_ref, g_ref, first_ref, second_ref, p_ref, p_first_ref, p_second_ref, *outs):
        grads = sums_ref[0:4, :]
        total_squares = sums_ref[4:5, 0:1] + jnp.sum(jnp.sum(grads * grads, axis=1, keepdims=True), axis=0, keepdims=True)
        norm = jnp.sqrt(total_squares)
        outs[7][...] = jnp.broadcast_to(norm, (8, 128))
        clip = 1.0 / jnp.maximum(norm, 1.0)
        new = adam_step(p_ref[...], grads * clip, p_first_ref[...], p_second_ref[...], rate_vector, 0.0)
        for ref, value in zip(outs[4:7], new):
            ref[...] = value
        for b in range(w_ref.shape[0]):
            new, first, second = adam_step(
                w_ref[b], g_ref[b] * clip, first_ref[b], second_ref[b], rate_matrix, weight_decay
            )
            outs[0][b] = new
            outs[1][b] = new.astype(bf16)
            outs[2][b] = first
            outs[3][b] = second

    dims = weights[0].shape
    outs = [shape(dims, f32), shape(dims, bf16), shape(dims, f32), shape(dims, f32)]
    outs = outs + [shape((4, D), f32)] * 3 + [shape((8, 128), f32)]
    return call(body, "update", [VM] * 8, outs, (sums, *weights, *norms), us=4)


def sync(*values):
    return lax.optimization_barrier(values)


def add_low(a, b):
    return (a.astype(f32) + b.astype(f32)).astype(bf16)


def step_small(
    patches,
    cotangent,
    input_views,
    token_live,
    master,
    moment_one,
    moment_two,
    norm_params,
    norm_moment_one,
    norm_moment_two,
):
    tokens = patches.shape[0]
    rows, blocks, cols = master.shape
    dp = lax.axis_index("dp")
    seq = lax.axis_index("seq")
    quarter, x_place = seq // 2, seq % 2
    y_place, core = dp // 2, dp % 2
    place = gray(quarter)
    at = jnp.stack([x_place, y_place, core, place]).astype(jnp.int32)

    def to_core(value):
        return swap(value, "dp", 1)

    def to_y(value):
        return swap(value, "dp", 2)

    def to_x(value):
        return swap(value, "seq", 1)

    def by_core(first, second):
        return jnp.where(core == 0, first, second), jnp.where(core == 0, second, first)

    def by_y(first, second):
        return jnp.where(y_place == 0, first, second), jnp.where(y_place == 0, second, first)

    def own_y(value):
        return lax.dynamic_slice_in_dim(value, y_place * 384, 384, value.ndim - 1)

    def other_y(value):
        return lax.dynamic_slice_in_dim(value, (1 - y_place) * 384, 384, value.ndim - 1)

    master_t = jnp.transpose(master, (1, 0, 2))
    low_t = jnp.transpose(master_t.astype(bf16), (0, 2, 1))
    flags = jnp.pad(token_live.astype(bf16)[None, :], ((0, 7), (0, D - tokens)))
    out_block = jnp.pad(low_t[3], ((0, 0), (0, 256 - rows))).reshape(3, 32, 256)
    out_block = jnp.transpose(out_block, (1, 0, 2)).reshape(32, D)
    ring0 = jnp.concatenate([patches, flags, out_block], axis=0)
    near_halves = [low_t[0:3, h * HALF : (h + 1) * HALF].reshape(3 * HALF, rows) for h in range(2)]
    far_halves = [
        jnp.concatenate(
            [low_t[4 + 2 * h : 6 + 2 * h].reshape(2 * cols, rows), low_t[8 + 2 * h : 10 + 2 * h].reshape(2 * cols, rows)],
            axis=0,
        )
        for h in range(2)
    ]

    ring1, beside0 = hop_quarter(ring0, 1), to_x(ring0)
    own, other = by_core(*near_halves)
    near = jnp.concatenate(by_core(own, to_core(other)), axis=1)
    near = jnp.stack([near, to_x(near)])
    own, other = by_y(*far_halves)
    far0 = jnp.concatenate(by_y(own, to_y(other)), axis=1)
    ring1, beside0, near, far0 = sync(ring1, beside0, near, far0)

    ring2, beside1 = hop_quarter(ring1, 1), to_x(ring1)
    near = jnp.stack([near, to_y(near)])
    near_there = to_core(near)
    ring2, beside1, near, near_there = sync(ring2, beside1, near, near_there)

    ring3, beside2, cot_there = hop_quarter(ring2, 1), to_x(ring2), to_y(cotangent)
    w_qkv = place_qkv(at, near, near_there)
    got0 = list(project(ring0, beside0, w_qkv, norm_params))
    ring3, beside2, cot_there, first = sync(ring3, beside2, cot_there, got0[0])
    got0[0] = first

    beside3, far1, far3 = to_x(ring3), hop_quarter(after(far0, ring3), 1), hop_quarter(after(far0, ring3), 3)
    got1 = list(project(ring1, after(beside1, first), w_qkv, norm_params))
    got2 = list(project(ring2, beside2, w_qkv, norm_params))
    beside3, far1, far3, got1[0], got2[0] = sync(beside3, far1, far3, got1[0], got2[0])

    far2 = hop_quarter(far1, 1)
    far013 = jnp.stack([far0, far1, far3])
    far013 = jnp.stack([far013, to_x(far013)], axis=1).reshape(6, 384, 384)
    got3 = project(ring3, beside3, w_qkv, norm_params)
    acts, normals, qs, ks, vs, out_own = zip(got0, got1, got2, got3)
    out_own = jnp.concatenate(out_own)
    out_own = jnp.stack([out_own, to_y(out_own)])
    mixed, full, q_back = attend(at, qs, ks, vs)
    mixed = list(mixed)
    *mixed, full, far2, far013, out_own = sync(*mixed, full, far2, far013, out_own)

    mixed = [mixed[0]] + [hop_quarter(mixed[4 - k], k) for k in (3, 2, 1)]
    far2 = jnp.stack([far2, to_x(far2)])
    w_out = place_out(at, out_own, to_core(out_own))
    *mixed, far2, w_out = sync(*mixed, far2, w_out)

    far013_there, far2_there = to_core(far013), to_core(far2)
    two, resid, normal_two, inverse_two, act_three = out_norm(at, patches, mixed, w_out, norm_params)
    w_mlp = (far013, far2, far013_there, far2_there)
    act_three, *w_mlp = sync(act_three, *w_mlp)

    act_there = to_y(act_three)
    hidden, wide, out_mine, three_mine = mlp(at, act_three, cotangent, w_mlp, f32)
    act_there, out_mine = sync(act_there, out_mine)
    hidden_there, wide_there, out_send, three_send = mlp(at, act_there, cot_there, w_mlp, bf16)
    three_send, hidden_there = sync(three_send, hidden_there)
    three_there = to_y(three_send)
    operands = (at, (act_three, act_there), (cotangent, cot_there), (hidden, hidden_there), (wide, wide_there))
    low_keep, low_send = mlp_weights(*operands, (1, 2))
    high_keep, high_send = mlp_weights(*operands, (3, 0))
    three_there, low_send, high_send = sync(three_there, low_send, high_send)

    low_there, high_there = to_core(low_send), to_core(high_send)
    grad_resid, sums_two, parts, grad_low = norm_out_back(
        at, three_mine, three_there, cotangent, normal_two, inverse_two, w_out, norm_params
    )
    *parts, grad_low = sync(*parts, grad_low)

    grads = [parts[0]] + [hop_quarter(parts[k], k) for k in (1, 2, 3)]
    low_sum = add_low(low_keep, low_there)
    high_sum = add_low(high_keep, high_there)
    low_x = to_x(low_sum[1])
    w_out_keep, w_out_send = out_weights(at, grad_low, two)
    out_sum = add_low(w_out_keep, to_core(w_out_send))
    out_sum = add_low(own_y(out_sum), to_y(other_y(out_sum))).reshape(4, 2, HALF, 384)
    *grads, low_x, high_sum, out_sum, out_send = sync(*grads, low_x, high_sum, out_sum, out_send)

    low_half = add_low(low_sum[0], low_x)
    far_got = [hop_quarter(low_half[0], -1), hop_quarter(low_half[1], -2)]
    high_half = add_low(high_sum[0], to_x(high_sum[1]))
    out_sum = add_low(out_sum[:, 0], to_x(out_sum[:, 1]))
    dqs, dks, dvs = attend_back(at, q_back, ks, vs, full, grads)
    dqs = list(dqs)
    dqs[1], high_half, out_sum = sync(dqs[1], high_half, out_sum)
    out_there = to_y(after(out_send, dqs[1]))
    block_out = (resid + out_mine + out_there.astype(f32)).astype(bf16)

    last = hop_quarter(jnp.concatenate([high_half[0], out_sum[3]], axis=0), 1)
    far_got.append(last[:384])
    out_got = [last[384:], hop_quarter(out_sum[1], -1), hop_quarter(out_sum[2], -2)]
    one, sums_one = {}, []
    for ks_here in ((1, 2), (3, 0)):
        keep, send, sums = input_back(*([m[k] for k in ks_here] for m in (normals, dqs, dks, dvs)), w_qkv)
        dqs[0], dqs[3] = after(dqs[0], keep[0]), after(dqs[3], keep[0])
        sums_one.append(sums)
        for k, a, b in zip(ks_here, keep, send):
            one[k] = (a, b)
    near_keep, near_send = projections_back(at, acts, dqs, dks, dvs)
    one1 = to_x(one[1][1])
    one1, near_send, *far_got, block_out = sync(one1, near_send, *far_got, block_out)

    one_ring = hop_quarter(add_low(one[1][0], one1), 1)
    one2 = to_x(after(one[2][1], one1))
    near_sum = add_low(near_keep, to_core(near_send))
    near_sum = add_low(own_y(near_sum), to_y(other_y(near_sum)))
    one_ring, one2, near_sum = sync(one_ring, one2, near_sum)

    near_x = to_x(near_sum[3:6])
    one_ring = hop_quarter(add_low(one_ring, add_low(one[2][0], one2)), 1)
    one3 = to_x(after(one[3][1], one2))
    far_sum = high_half[1].astype(f32)
    for part in far_got:
        far_sum = far_sum + part.astype(f32)
    out_sum = out_sum[0].astype(f32)
    for part in out_got:
        out_sum = out_sum + part.astype(f32)
    near_sum = near_sum[0:3].astype(f32) + near_x.astype(f32)
    near_sum = jnp.concatenate([near_sum.reshape(3 * HALF, 2 * rows), out_sum], axis=0)
    far_own, far_other = by_y(far_sum[:, :rows], far_sum[:, rows:])
    near_own, near_other = by_core(near_sum[:, :rows], near_sum[:, rows:])
    weight_grad = turn(at, far_own, to_y(far_other.astype(bf16)), near_own, to_core(near_other.astype(bf16)))
    squares = jnp.full((4, D), jnp.sum(far_sum * far_sum) + jnp.sum(near_sum * near_sum), f32)
    sums = jnp.concatenate([sums_one[0][0:2] + sums_one[1][0:2], sums_two[0:2], squares], axis=0)
    for by in (1, 2):
        sums = sums + hop_quarter(sums, by)
    sums, one_ring, one3 = sync(sums, one_ring, one3)

    one_ring = hop_quarter(add_low(one_ring, add_low(one[3][0], one3)), 1)
    one0 = to_x(one[0][1])
    sums = sums + swap(sums, "seq", 1)
    sums = after(sums + swap(sums, "dp", 2), weight_grad)
    sums = sums + swap(sums, "dp", 1)
    updated = update(
        sums,
        (master_t, weight_grad, jnp.transpose(moment_one, (1, 0, 2)), jnp.transpose(moment_two, (1, 0, 2))),
        (norm_params, norm_moment_one, norm_moment_two),
    )
    new_master, new_copy, new_moment_one, new_moment_two = (jnp.transpose(m, (1, 0, 2)) for m in updated[0:4])
    new_norm_params, new_norm_moment_one, new_norm_moment_two, grad_norm = updated[4:]
    grad_norm = grad_norm[0, 0]

    grad_one = one_ring.astype(f32) + one[0][0].astype(f32) + one0.astype(f32)
    normal_one, inverse_one = layer_stats(patches.astype(f32))
    patches_grad = grad_resid + layer_back(grad_one, normal_one, inverse_one, norm_params[0])
    return (
        block_out,
        patches_grad,
        new_master,
        new_copy,
        new_moment_one,
        new_moment_two,
        new_norm_params,
        new_norm_moment_one,
        new_norm_moment_two,
        grad_norm,
    )


def solution(mesh):
    tokens = P(("dp", "seq"), None)
    weights = P("dp", None, "seq")
    small = mesh.shape["dp"] == 4 and mesh.shape["seq"] == 8
    return jax.shard_map(
        step_small if small else step_general,
        mesh=mesh,
        in_specs=(tokens, tokens, P("dp"), P(("dp", "seq")), weights, weights, weights, P(), P(), P()),
        out_specs=(tokens, tokens, weights, weights, weights, weights, P(), P(), P(), P()),
        check_vma=False,
    )
```
